32 devices in a mesh: parts: 2 (over x), tm: 16 (over z, y, core).
Axes of the slice: x: 2, y: 2, z: 4, core: 2. Of those that a mesh axis runs over, the one named last changes fastest.
Arguments:
- currents: bfloat16 [49152, 1024], P('tm', 'parts'), parts along dimension 1, may hold values from -5 to 5
- seed_on_tension: bfloat16 [49152, 1024], P('tm', 'parts'), parts along dimension 1, may hold values from -6 to 6
- mode_diffusivity_factor: float32 [32, 98304], P(None, ('parts', 'tm')), parts along dimension 1, may hold values from 0.25 to 34410
- decay_rates: float32 [32], replicated, may hold values from 6.1035156e-06 to 0.34
- fit_weights: float32 [32], replicated, may hold values from 0.06 to 0.3
- counts: int32 [1024], P('parts'), parts along dimension 0, may hold values from 1 to 16
Outputs:
- tension_at_end: bfloat16 [49152, 1024], P('tm', 'parts'), parts along dimension 1
- gradient_wrt_draw: bfloat16 [49152, 1024], P('tm', 'parts'), parts along dimension 1
- softened_peak_tension: float32 [1024], P('parts'), parts along dimension 0
The draws below stay inside these ranges and needn't reach their ends.
There are 2 independent parts, one for each index of `parts`. The reference program is written for one: setup_inputs(seed, part) draws one part's arguments, and reference() takes and returns one part's arrays. A program takes and returns all parts, laid end to end along the dimension named above; an argument that names none is the same for every part. Nothing has to cross between parts.
All inputs are finite; a program needn't handle non-finite values.
Results may differ from the reference program's by a relative error of at most 0.0053.
Values sent between devices are 32-bit elements; how exact they have to be, the bound alone decides.
No kernel may reach another device: no remote copies, remote signals or barrier semaphores. Data moves between devices by JAX's collectives and lax.ppermute only.
A program may use at most 192 MiB of HBM per device.

```python
import math
import jax
import jax.numpy as jnp
from jax import lax

EXPONENTIAL_MODES = 32
SLAB_WIRES = 512
DEVICE_LENGTH = 3072
KERNEL_SPAN = 768
TRACE_LENGTH = 49152


def draw_currents(key, part):
    initial_rng_entry = jax.random.fold_in(key, 0)
    entry_array = jnp.clip(jax.random.normal(initial_rng_entry, (TRACE_LENGTH, SLAB_WIRES), jnp.float32), -5.0, 5.0)
    return entry_array.astype(jnp.bfloat16)


def draw_mode_diffusivity_factor(key, part):
    initial_rng_entry, middle_rng_entry, closing_random_entry = jax.random.split(key, 3)
    device_pieces = TRACE_LENGTH // DEVICE_LENGTH
    tier_list = jnp.exp(jax.random.uniform(initial_rng_entry, (device_pieces,), jnp.float32, math.log(0.5), math.log(2.0)))
    jaggedness = jnp.exp(jax.random.uniform(middle_rng_entry, (EXPONENTIAL_MODES, TRACE_LENGTH), jnp.float32, math.log(0.5), math.log(2.0)))
    mode_diffusivity_factor = jnp.repeat(tier_list, DEVICE_LENGTH)[None, :] * jaggedness
    pulse_positions = jax.random.randint(closing_random_entry, (EXPONENTIAL_MODES, 2), 0, TRACE_LENGTH)
    segment_starts = jnp.arange(TRACE_LENGTH)
    pulse_flags = jnp.any(segment_starts[None, None, :] == pulse_positions[:, :, None], axis=1)
    pulse_level = float(7 * TRACE_LENGTH // 10)
    return mode_diffusivity_factor + jnp.where(pulse_flags, pulse_level, 0.0).astype(jnp.float32)


def draw_decay_rates(key, part):
    initial_rng_entry, middle_rng_entry, closing_random_entry = jax.random.split(key, 3)
    share = 0.5
    gentle_decay_speeds = jnp.exp(jax.random.uniform(initial_rng_entry, (EXPONENTIAL_MODES,), jnp.float32, math.log(0.3), math.log(0.9))) / TRACE_LENGTH
    fast_rates = jnp.exp(jax.random.uniform(middle_rng_entry, (EXPONENTIAL_MODES,), jnp.float32, math.log(1.0 / 300.0), math.log(1.0 / 3.0)))
    picks = jax.random.uniform(closing_random_entry, (EXPONENTIAL_MODES,), jnp.float32) < share
    return jnp.where(picks, gentle_decay_speeds, fast_rates)


def touch_ends(entries, own_key, low, top_value):
    spot = [jax.random.randint(jax.random.fold_in(own_key, axis), (), 0, length) for axis, length in enumerate(entries.shape)]
    main_axis = entries.shape.index(max(entries.shape))
    beside = spot[:main_axis] + [(spot[main_axis] + 1) % entries.shape[main_axis]] + spot[main_axis + 1:]
    return entries.at[tuple(spot)].set(low).at[tuple(beside)].set(top_value)


def block_scale(key, extent, cuts, least, top_value):
    gain, own = 1.0, jax.random.fold_in(key, 6)
    for axis_at, shards_of in cuts:
        heights = jnp.exp(jax.random.uniform(jax.random.fold_in(own, axis_at), (shards_of,), jnp.float32, least / len(cuts), top_value / len(cuts)))
        gain = gain * jnp.repeat(heights, extent[axis_at] // shards_of).reshape([-1 if axis == axis_at else 1 for axis in range(len(extent))])
    return gain


def gaussian(rng, dims, width, bound, cuts=(), dtype=jnp.bfloat16):
    array = jax.random.normal(rng, dims, jnp.float32) * width
    if len(cuts) > 0:
        array = block_scale(rng, dims, cuts, -0.22, 0.18) * array
    return jnp.clip(array, min=-bound, max=bound).astype(dtype)


def setup_inputs(seed: int = 0, part: int = 0) -> dict:
    key_list = jax.random.split(jax.random.key(seed), 7)
    own_keys = jax.random.split(jax.random.fold_in(key_list[6], part), 7)
    currents = draw_currents(jax.random.fold_in(jax.random.fold_in(key_list[6], part), 71), part)
    seed_on_tension = gaussian(own_keys[1], (TRACE_LENGTH, SLAB_WIRES), 1.0, 6.0, ((0, 16),))
    mode_diffusivity_factor = draw_mode_diffusivity_factor(jax.random.fold_in(jax.random.fold_in(key_list[6], part), 71), part)
    decay_rates = draw_decay_rates(jax.random.fold_in(key_list[6], 71), part)
    fit_weights = jnp.clip(jnp.exp(jax.random.uniform(key_list[4], (EXPONENTIAL_MODES,), jnp.float32, math.log(0.06), math.log(0.3))), 0.06, 0.3)
    counts = touch_ends(jax.random.randint(own_keys[5], (SLAB_WIRES,), 1, 17), jax.random.fold_in(own_keys[5], 1), 1, 16).astype(jnp.int32)
    return dict(currents=currents, seed_on_tension=seed_on_tension, mode_diffusivity_factor=mode_diffusivity_factor, decay_rates=decay_rates, fit_weights=fit_weights, counts=counts)


SHARPNESS = 4.0
FAR_AWAY = 1e+30

def block_tables(heat_block, decay_rates, mode_gains):
    prefix = jnp.cumsum(heat_block, axis=1)
    spread = prefix[:, :, None] - prefix[:, None, :]
    row_ids = lax.broadcasted_iota(jnp.int32, (KERNEL_SPAN, KERNEL_SPAN), 0)
    col_ids = lax.broadcasted_iota(jnp.int32, (KERNEL_SPAN, KERNEL_SPAN), 1)
    spread = jnp.where((row_ids >= col_ids)[None], spread, FAR_AWAY)
    kernel = lax.optimization_barrier(jnp.sum(mode_gains[:, None, None] * jnp.exp(-decay_rates[:, None, None] * spread), axis=0))
    closing_instant = prefix[:, -1]
    prefix_rows = prefix.T
    back_table = jnp.exp(-decay_rates[None, :] * (closing_instant[None, :] - prefix_rows))
    start_table = mode_gains[None, :] * jnp.exp(-decay_rates[None, :] * prefix_rows)
    decays = jnp.exp(-decay_rates * closing_instant)
    return (kernel.astype(jnp.bfloat16), back_table, start_table, decays)

def reference(currents, seed_on_tension, mode_diffusivity_factor, decay_rates, fit_weights, counts):
    mode_gains = fit_weights * jnp.sqrt(decay_rates)
    length_scale = counts.astype(jnp.float32) / 4.0
    kernel_spans = TRACE_LENGTH // KERNEL_SPAN
    conductor_total = currents.shape[1]
    mode_count = decay_rates.shape[0]
    cur_blocks = currents.reshape(kernel_spans, KERNEL_SPAN, conductor_total)
    cot_blocks = seed_on_tension.reshape(kernel_spans, KERNEL_SPAN, conductor_total)
    heat_blocks = mode_diffusivity_factor.reshape(mode_count, kernel_spans, KERNEL_SPAN).transpose(1, 0, 2)
    contract = (((0,), (0,)), ((), ()))

    def forward_sweep(carried, inputs):
        mode_state, highest, amount = carried
        current_block, heat_block = inputs
        kernel, back_table, start_table, decays = block_tables(heat_block, decay_rates, mode_gains)
        in_block = jnp.dot(kernel, current_block, preferred_element_type=jnp.float32)
        carried_in = jnp.dot(start_table, mode_state, precision=lax.Precision.HIGHEST, preferred_element_type=jnp.float32)
        stress_full = length_scale[None, :] * (in_block + carried_in)
        fresh_state = lax.dot_general(back_table.astype(jnp.bfloat16), current_block, contract, preferred_element_type=jnp.float32)
        mode_state = decays[:, None] * mode_state + fresh_state
        scores = SHARPNESS * stress_full
        new_high = jnp.maximum(highest, lax.optimization_barrier(jnp.max(scores, axis=0)))
        amount = amount * jnp.exp(highest - new_high) + lax.optimization_barrier(jnp.sum(jnp.exp(scores - new_high[None, :]), axis=0))
        return ((mode_state, new_high, amount), stress_full.astype(jnp.bfloat16))
    initial = (jnp.zeros((mode_count, conductor_total), jnp.float32), jnp.full((conductor_total,), -FAR_AWAY, jnp.float32), jnp.zeros((conductor_total,), jnp.float32))
    (mode_state, highest, amount), tension_at_end = lax.scan(forward_sweep, initial, (cur_blocks, heat_blocks))
    softened_peak_tension = (highest + jnp.log(amount)) / SHARPNESS

    def adjoint(adjoint_state, inputs):
        cot_block, heat_block = inputs
        kernel, back_table, start_table, decays = block_tables(heat_block, decay_rates, mode_gains)
        in_block = lax.dot_general(kernel, cot_block, contract, preferred_element_type=jnp.float32)
        carried_in = jnp.dot(back_table, adjoint_state, precision=lax.Precision.HIGHEST, preferred_element_type=jnp.float32)
        result_block = (length_scale[None, :] * (in_block + carried_in)).astype(jnp.bfloat16)
        fresh_state = lax.dot_general(start_table.astype(jnp.bfloat16), cot_block, contract, preferred_element_type=jnp.float32)
        adjoint_state = decays[:, None] * adjoint_state + fresh_state
        return (adjoint_state, result_block)
    final_state, gradient_wrt_draw = lax.scan(adjoint, jnp.zeros((mode_count, conductor_total), jnp.float32), (cot_blocks, heat_blocks), reverse=True)
    return (tension_at_end.reshape(TRACE_LENGTH, conductor_total), gradient_wrt_draw.reshape(TRACE_LENGTH, conductor_total), softened_peak_tension)
```

```python
import functools
import math

import jax
import jax.numpy as jnp
from jax import lax
from jax.experimental import pallas as pl
from jax.experimental.pallas import tpu as pltpu
from jax.sharding import PartitionSpec as P

CHUNK = 128
LEVELS = 7
SHARPNESS = 4.0
LOG2E = math.log2(math.e)
LN2 = math.log(2.0)
F32 = jnp.float32
BF16 = jnp.bfloat16


def as_column(row):
    m = row.shape[1]
    r = lax.broadcasted_iota(jnp.int32, (m, m), 0)
    c = lax.broadcasted_iota(jnp.int32, (m, m), 1)
    return jnp.sum(jnp.where(r == c, jnp.broadcast_to(row, (m, m)), 0.0), axis=1, keepdims=True)


def rates_and_gains(rates_ref, fit_ref):
    rates = as_column(rates_ref[...])
    gains = as_column(fit_ref[...]) * jnp.sqrt(rates)
    return rates * LOG2E, gains


def doubling(heat, with_levels):
    lane = lax.broadcasted_iota(jnp.int32, heat.shape, 1)
    pre, suf = heat, jnp.zeros_like(heat)
    tables = []
    for level in range(LEVELS):
        half = 1 << level
        second = (lane & half) != 0
        if with_levels:
            tables.append(jnp.exp2(-jnp.where(second, pre, suf)))
        total = pre + suf
        sibling = jnp.where(
            second, pltpu.roll(total, half, 1), pltpu.roll(total, CHUNK - half, 1)
        )
        pre = jnp.where(second, pre + sibling, pre)
        suf = jnp.where(second, suf, suf + sibling)
    return pre, suf, tables


def wide(a, times):
    return jnp.concatenate([a] * times, axis=1)


def totals_kernel(
    heat_ref, rates_ref, fit_ref, cur_ref, cot_ref,
    fresh_f_ref, fresh_a_ref, decay_ref, msg_ref, tf, ta, dc,
):
    step = pl.program_id(0)
    modes = heat_ref.shape[0]
    wires = cur_ref.shape[1]
    reps = wires // CHUNK

    @pl.when(step == 0)
    def _():
        tf[...] = jnp.zeros_like(tf)
        ta[...] = jnp.zeros_like(ta)
        dc[...] = jnp.ones_like(dc)

    speed, gains = rates_and_gains(rates_ref, fit_ref)
    for c in range(heat_ref.shape[1] // CHUNK):
        span = slice(c * CHUNK, (c + 1) * CHUNK)
        rows = slice(c * modes, (c + 1) * modes)
        pre, suf, _ = doubling(heat_ref[:, span] * speed, False)
        start = (gains * jnp.exp2(-pre)).astype(BF16)
        back = jnp.exp2(-suf).astype(BF16)
        decay = jnp.exp2(-(pre + suf))
        fresh_f = jnp.dot(back, cur_ref[span, :], preferred_element_type=F32)
        fresh_a = jnp.dot(start, cot_ref[span, :], preferred_element_type=F32)
        fresh_f_ref[rows, :] = fresh_f
        fresh_a_ref[rows, :] = fresh_a
        decay_ref[rows, :] = decay
        tf[...] = wide(decay, reps) * tf[...] + fresh_f
        ta[...] = ta[...] + wide(dc[...], reps) * fresh_a
        dc[...] = dc[...] * decay

    @pl.when(step == pl.num_programs(0) - 1)
    def _():
        for k in range(reps):
            lanes = slice(k * CHUNK, (k + 1) * CHUNK)
            msg_ref[k] = tf[:, lanes]
            msg_ref[reps + k] = ta[:, lanes]
        msg_ref[2 * reps] = dc[...]


def kernels_kernel(heat_ref, rates_ref, fit_ref, kf_ref, ka_ref, aux_ref):
    modes = heat_ref.shape[0]
    speed, gains = rates_and_gains(rates_ref, fit_ref)
    gain_sum = jnp.sum(gains, axis=0, keepdims=True)
    t = lax.broadcasted_iota(jnp.int32, (CHUNK, CHUNK), 0)
    s = lax.broadcasted_iota(jnp.int32, (CHUNK, CHUNK), 1)
    apart = jnp.where(t >= s, t ^ s, -1)
    base = jnp.where(apart == 0, jnp.broadcast_to(gain_sum, (CHUNK, CHUNK)), 0.0)
    zero = jnp.zeros((modes, CHUNK), BF16)
    for c in range(heat_ref.shape[1] // CHUNK):
        span = slice(c * CHUNK, (c + 1) * CHUNK)
        pre, suf, tables = doubling(heat_ref[:, span] * speed, True)
        left = [gains * e for e in tables]
        right = [e.astype(BF16) for e in tables]
        kernel = base
        for lv in range(0, LEVELS - 1, 2):
            lhs = jnp.concatenate([left[lv], left[lv + 1]], axis=0).T.astype(BF16)
            rhs = jnp.concatenate(
                [
                    jnp.concatenate([right[lv], zero], axis=1),
                    jnp.concatenate([zero, right[lv + 1]], axis=1),
                ],
                axis=0,
            )
            both = jnp.dot(lhs, rhs, preferred_element_type=F32)
            kernel = jnp.where(apart >= (1 << lv), both[:, :CHUNK], kernel)
            kernel = jnp.where(apart >= (2 << lv), both[:, CHUNK:], kernel)
        back = jnp.exp2(-suf)
        aux = jnp.concatenate(
            [left[LEVELS - 1], gains * jnp.exp2(-pre), back, back], axis=0
        ).T.astype(BF16)
        rhs = jnp.concatenate([right[LEVELS - 1], zero, zero, zero], axis=0)
        last = jnp.dot(aux, rhs, preferred_element_type=F32)
        kernel = jnp.where(apart >= (1 << (LEVELS - 1)), last, kernel)
        kf_ref[span, :] = kernel.astype(BF16)
        ka_ref[span, :] = kernel.T.astype(BF16)
        aux_ref[span, :] = aux


def stress_kernel(
    cur_ref, kf_ref, aux_ref, fresh_ref, decay_ref, in_ref, counts_ref,
    out_ref, lse_ref, state, high, amount,
):
    step = pl.program_id(0)
    wires = cur_ref.shape[1]
    reps = wires // CHUNK
    modes = in_ref.shape[1]

    @pl.when(step == 0)
    def _():
        for k in range(reps):
            state[:, k * CHUNK : (k + 1) * CHUNK] = in_ref[k]
        high[...] = jnp.full_like(high, -1e30)
        amount[...] = jnp.zeros_like(amount)

    scale = counts_ref[...].astype(F32) * 0.25
    scale2 = scale * (SHARPNESS * LOG2E)
    zero1 = jnp.zeros((modes, wires), BF16)
    zero2 = jnp.zeros((CHUNK - 2 * modes, wires), BF16)
    for c in range(cur_ref.shape[0] // CHUNK):
        span = slice(c * CHUNK, (c + 1) * CHUNK)
        rows = slice(c * modes, (c + 1) * modes)
        now = state[...]
        lhs = jnp.concatenate([kf_ref[span, :], aux_ref[span, :]], axis=1)
        rhs = jnp.concatenate([cur_ref[span, :], zero1, now.astype(BF16), zero2], axis=0)
        acc = jnp.dot(lhs, rhs, preferred_element_type=F32)
        out_ref[span, :] = (acc * scale).astype(BF16)
        z = (acc * scale2).reshape(CHUNK // 8, 8, wires)
        old = high[...]
        new = jnp.maximum(old, jnp.max(z, axis=0))
        amount[...] = amount[...] * jnp.exp2(old - new) + jnp.sum(jnp.exp2(z - new[None]), axis=0)
        high[...] = new
        state[...] = wide(decay_ref[rows, :], reps) * now + fresh_ref[rows, :]

    @pl.when(step == pl.num_programs(0) - 1)
    def _():
        top = jnp.max(high[...], axis=0, keepdims=True)
        total = jnp.sum(amount[...] * jnp.exp2(high[...] - top), axis=0, keepdims=True)
        value = top + jnp.log(total) * LOG2E
        lse_ref[...] = jnp.broadcast_to(value[None], lse_ref.shape)


def adjoint_kernel(
    cot_ref, ka_ref, aux_ref, fresh_ref, decay_ref, in_ref, counts_ref, out_ref, state
):
    step = pl.program_id(0)
    wires = cot_ref.shape[1]
    reps = wires // CHUNK
    modes = in_ref.shape[1]

    @pl.when(step == 0)
    def _():
        for k in range(reps):
            state[:, k * CHUNK : (k + 1) * CHUNK] = in_ref[k]

    scale = counts_ref[...].astype(F32) * 0.25
    zero2 = jnp.zeros((2 * modes, wires), BF16)
    zero1 = jnp.zeros((CHUNK - 3 * modes, wires), BF16)
    for c in reversed(range(cot_ref.shape[0] // CHUNK)):
        span = slice(c * CHUNK, (c + 1) * CHUNK)
        rows = slice(c * modes, (c + 1) * modes)
        now = state[...]
        lhs = jnp.concatenate([ka_ref[span, :], aux_ref[span, :]], axis=1)
        rhs = jnp.concatenate([cot_ref[span, :], zero2, now.astype(BF16), zero1], axis=0)
        acc = jnp.dot(lhs, rhs, preferred_element_type=F32)
        out_ref[span, :] = (acc * scale).astype(BF16)
        state[...] = wide(decay_ref[rows, :], reps) * now + fresh_ref[rows, :]


def steps_for(chunks):
    for steps in (4, 3, 2):
        if chunks % steps == 0:
            return steps
    return 1


def scan_devices(msg, reps):
    n = lax.axis_size("tm")
    me = lax.axis_index("tm")
    before = jnp.zeros_like(msg[:reps])
    after = jnp.zeros_like(msg[:reps])
    d_before = jnp.ones_like(msg[2 * reps :])
    d_after = jnp.ones_like(msg[2 * reps :])
    hop = 1
    while hop < n:
        pairs = [(i, i ^ hop) for i in range(n)]
        upper = (me & hop) != 0
        mine_f, mine_a, mine_d = msg[:reps], msg[reps : 2 * reps], msg[2 * reps :]
        if 2 * hop < n:
            got = lax.ppermute(msg, "tm", pairs)
            got_f, got_a, got_d = got[:reps], got[reps : 2 * reps], got[2 * reps :]
            next_f = jnp.where(upper, mine_d * got_f + mine_f, got_d * mine_f + got_f)
            next_a = jnp.where(upper, got_d * mine_a + got_a, mine_d * got_a + mine_a)
            msg = jnp.concatenate([next_f, next_a, mine_d * got_d], axis=0)
            before = jnp.where(upper, d_before * got_f + before, before)
            after = jnp.where(upper, after, d_after * got_a + after)
            d_before = jnp.where(upper, d_before * got_d, d_before)
            d_after = jnp.where(upper, d_after, d_after * got_d)
        else:
            got = lax.ppermute(jnp.where(upper, mine_a, mine_f), "tm", pairs)
            before = jnp.where(upper, d_before * got + before, before)
            after = jnp.where(upper, after, d_after * got + after)
        hop *= 2
    return before, after


def body(currents, seed_on_tension, mode_diffusivity_factor, decay_rates, fit_weights, counts):
    samples, wires = currents.shape
    modes = decay_rates.shape[0]
    devices = lax.axis_size("tm")
    chunks = samples // CHUNK
    steps = steps_for(chunks)
    block = samples // steps
    mblock = chunks * modes // steps
    reps = wires // CHUNK
    rates = decay_rates.reshape(1, modes)
    fits = fit_weights.reshape(1, modes)
    counts = counts.reshape(1, wires)
    params = pltpu.CompilerParams(vmem_limit_bytes=48 << 20)
    small = pl.BlockSpec((1, modes), lambda i: (0, 0))
    flops = 2 * samples * wires

    fresh_f, fresh_a, decay, msg = pl.pallas_call(
        totals_kernel,
        name="totals",
        grid=(steps,),
        in_specs=[
            pl.BlockSpec((modes, block), lambda i: (0, i)),
            small,
            small,
            pl.BlockSpec((block, wires), lambda i: (i, 0)),
            pl.BlockSpec((block, wires), lambda i: (i, 0)),
        ],
        out_specs=[
            pl.BlockSpec((mblock, wires), lambda i: (i, 0)),
            pl.BlockSpec((mblock, wires), lambda i: (i, 0)),
            pl.BlockSpec((mblock, CHUNK), lambda i: (i, 0)),
            pl.BlockSpec((2 * reps + 1, modes, CHUNK), lambda i: (0, 0, 0)),
        ],
        out_shape=[
            jax.ShapeDtypeStruct((chunks * modes, wires), F32),
            jax.ShapeDtypeStruct((chunks * modes, wires), F32),
            jax.ShapeDtypeStruct((chunks * modes, CHUNK), F32),
            jax.ShapeDtypeStruct((2 * reps + 1, modes, CHUNK), F32),
        ],
        scratch_shapes=[
            pltpu.VMEM((modes, wires), F32),
            pltpu.VMEM((modes, wires), F32),
            pltpu.VMEM((modes, CHUNK), F32),
        ],
        compiler_params=params,
        cost_estimate=pl.CostEstimate(
            flops=2 * modes * flops, bytes_accessed=14 << 20, transcendentals=0
        ),
    )(mode_diffusivity_factor, rates, fits, currents, seed_on_tension)

    kf, ka, aux = pl.pallas_call(
        kernels_kernel,
        name="kernels",
        grid=(steps,),
        in_specs=[pl.BlockSpec((modes, block), lambda i: (0, i)), small, small],
        out_specs=[pl.BlockSpec((block, CHUNK), lambda i: (i, 0))] * 3,
        out_shape=[jax.ShapeDtypeStruct((samples, CHUNK), BF16)] * 3,
        compiler_params=params,
        cost_estimate=pl.CostEstimate(
            flops=CHUNK * flops, bytes_accessed=16 << 20, transcendentals=0
        ),
    )(mode_diffusivity_factor, rates, fits)

    before, after = scan_devices(msg, reps)

    def common(reverse):
        def at(i):
            return (steps - 1 - i if reverse else i, 0)

        return [
            pl.BlockSpec((block, wires), at),
            pl.BlockSpec((block, CHUNK), at),
            pl.BlockSpec((block, CHUNK), at),
            pl.BlockSpec((mblock, wires), at),
            pl.BlockSpec((mblock, CHUNK), at),
            pl.BlockSpec((reps, modes, CHUNK), lambda i: (0, 0, 0)),
            pl.BlockSpec((1, wires), lambda i: (0, 0)),
        ], pl.BlockSpec((block, wires), at)

    specs, out_spec = common(False)
    tension, lse = pl.pallas_call(
        stress_kernel,
        name="stress",
        grid=(steps,),
        in_specs=specs,
        out_specs=[out_spec, pl.BlockSpec((devices, 1, wires), lambda i: (0, 0, 0))],
        out_shape=[
            jax.ShapeDtypeStruct((samples, wires), BF16),
            jax.ShapeDtypeStruct((devices, 1, wires), F32),
        ],
        scratch_shapes=[
            pltpu.VMEM((modes, wires), F32),
            pltpu.VMEM((8, wires), F32),
            pltpu.VMEM((8, wires), F32),
        ],
        compiler_params=params,
        cost_estimate=pl.CostEstimate(
            flops=2 * CHUNK * flops, bytes_accessed=10 << 20, transcendentals=0
        ),
    )(currents, kf, aux, fresh_f, decay, before, counts)

    all_lse = lax.all_to_all(lse, "tm", 0, 0, tiled=True)

    specs, out_spec = common(True)
    gradient = pl.pallas_call(
        adjoint_kernel,
        name="adjoint",
        grid=(steps,),
        in_specs=specs,
        out_specs=out_spec,
        out_shape=jax.ShapeDtypeStruct((samples, wires), BF16),
        scratch_shapes=[pltpu.VMEM((modes, wires), F32)],
        compiler_params=params,
        cost_estimate=pl.CostEstimate(
            flops=2 * CHUNK * flops, bytes_accessed=10 << 20, transcendentals=0
        ),
    )(seed_on_tension, ka, aux, fresh_a, decay, after, counts)

    top = jnp.max(all_lse, axis=0)
    total = jnp.sum(jnp.exp2(all_lse - top[None]), axis=0)
    softened = ((top * LN2 + jnp.log(total)) / SHARPNESS).reshape(wires)
    return (tension, gradient, softened)


def solution(mesh):
    placed = (P("tm", "parts"), P("tm", "parts"), P(None, ("parts", "tm")), P(), P(), P("parts"))
    return jax.shard_map(
        body,
        mesh=mesh,
        in_specs=placed,
        out_specs=(P("tm", "parts"), P("tm", "parts"), P("parts")),
        check_vma=False,
    )
```

```python
import functools
import math

import jax
import jax.numpy as jnp
from jax import lax
from jax.experimental import pallas as pl
from jax.experimental.pallas import tpu as pltpu
from jax.sharding import PartitionSpec as P

CHUNK = 128
LEVELS = 7
SHARPNESS = 4.0
LOG2E = math.log2(math.e)
LN2 = math.log(2.0)
F32 = jnp.float32
BF16 = jnp.bfloat16


def as_column(row):
    m = row.shape[1]
    r = lax.broadcasted_iota(jnp.int32, (m, m), 0)
    c = lax.broadcasted_iota(jnp.int32, (m, m), 1)
    return jnp.sum(jnp.where(r == c, jnp.broadcast_to(row, (m, m)), 0.0), axis=1, keepdims=True)


def rates_and_gains(rates_ref, fit_ref):
    rates = as_column(rates_ref[...])
    gains = as_column(fit_ref[...]) * jnp.sqrt(rates)
    return rates * LOG2E, gains


def doubling(heat, with_levels):
    lane = lax.broadcasted_iota(jnp.int32, heat.shape, 1)
    pre, suf = heat, jnp.zeros_like(heat)
    tables = []
    for level in range(LEVELS):
        half = 1 << level
        second = (lane & half) != 0
        if with_levels:
            tables.append(jnp.exp2(-jnp.where(second, pre, suf)))
        total = pre + suf
        sibling = jnp.where(
            second, pltpu.roll(total, half, 1), pltpu.roll(total, CHUNK - half, 1)
        )
        pre = jnp.where(second, pre + sibling, pre)
        suf = jnp.where(second, suf, suf + sibling)
    return pre, suf, tables


def wide(a, times):
    return jnp.concatenate([a] * times, axis=1)


def stacked(heat_ref, speed, first, count):
    return jnp.concatenate(
        [
            heat_ref[:, c * CHUNK : (c + 1) * CHUNK] * speed
            for c in range(first, first + count)
        ],
        axis=0,
    )


def group_of(chunks, most):
    return max(g for g in range(1, most + 1) if chunks % g == 0)


def totals_kernel(
    heat_ref, rates_ref, fit_ref, cur_ref, cot_ref,
    fresh_f_ref, fresh_a_ref, decay_ref, msg_ref, tf_ref, ta_ref, dc_ref,
):
    step = pl.program_id(0)
    modes = heat_ref.shape[0]
    wires = cur_ref.shape[1]
    reps = wires // CHUNK
    chunks = heat_ref.shape[1] // CHUNK
    group = group_of(chunks, 3)

    @pl.when(step == 0)
    def _():
        tf_ref[...] = jnp.zeros_like(tf_ref)
        ta_ref[...] = jnp.zeros_like(ta_ref)
        dc_ref[...] = jnp.ones_like(dc_ref)

    speed, gains = rates_and_gains(rates_ref, fit_ref)
    gain_stack = jnp.concatenate([gains] * group, axis=0)
    tf, ta, dc = tf_ref[...], ta_ref[...], dc_ref[...]
    for first in range(0, chunks, group):
        pre, suf, _ = doubling(stacked(heat_ref, speed, first, group), False)
        starts = (gain_stack * jnp.exp2(-pre)).astype(BF16)
        backs = jnp.exp2(-suf).astype(BF16)
        decays = jnp.exp2(-(pre + suf))
        for c in range(group):
            part = slice(c * modes, (c + 1) * modes)
            span = slice((first + c) * CHUNK, (first + c + 1) * CHUNK)
            rows = slice((first + c) * modes, (first + c + 1) * modes)
            decay = decays[part]
            fresh_f = jnp.dot(backs[part], cur_ref[span, :], preferred_element_type=F32)
            fresh_a = jnp.dot(starts[part], cot_ref[span, :], preferred_element_type=F32)
            fresh_f_ref[rows, :] = fresh_f
            fresh_a_ref[rows, :] = fresh_a
            decay_ref[rows, :] = decay
            tf = wide(decay, reps) * tf + fresh_f
            ta = ta + wide(dc, reps) * fresh_a
            dc = dc * decay
    tf_ref[...], ta_ref[...], dc_ref[...] = tf, ta, dc

    @pl.when(step == pl.num_programs(0) - 1)
    def _():
        for k in range(reps):
            lanes = slice(k * CHUNK, (k + 1) * CHUNK)
            msg_ref[k] = tf[:, lanes]
            msg_ref[reps + k] = ta[:, lanes]
        msg_ref[2 * reps] = dc


def kernels_kernel(heat_ref, rates_ref, fit_ref, *refs):
    kf_ref, ka_ref, aux_ref = refs[-3:]
    modes = heat_ref.shape[0]
    chunks = heat_ref.shape[1] // CHUNK
    group = group_of(chunks, 2)
    speed, gains = rates_and_gains(rates_ref, fit_ref)
    gain_sum = jnp.sum(gains, axis=0, keepdims=True)
    t = lax.broadcasted_iota(jnp.int32, (CHUNK, CHUNK), 0)
    s = lax.broadcasted_iota(jnp.int32, (CHUNK, CHUNK), 1)
    apart = jnp.where(t >= s, t ^ s, -1)
    base = jnp.where(apart == 0, jnp.broadcast_to(gain_sum, (CHUNK, CHUNK)), 0.0)
    zero = jnp.zeros((modes, CHUNK), BF16)
    for first in range(0, chunks, group):
        pres, sufs, stacks = doubling(stacked(heat_ref, speed, first, group), True)
        for c in range(group):
            part = slice(c * modes, (c + 1) * modes)
            span = slice((first + c) * CHUNK, (first + c + 1) * CHUNK)
            pre, suf = pres[part], sufs[part]
            tables = [e[part] for e in stacks]
            left = [gains * e for e in tables]
            right = [e.astype(BF16) for e in tables]
            kernel = base
            for lv in range(0, LEVELS - 1, 2):
                lhs = jnp.concatenate([left[lv], left[lv + 1]], axis=0).T.astype(BF16)
                rhs = jnp.concatenate(
                    [
                        jnp.concatenate([right[lv], zero], axis=1),
                        jnp.concatenate([zero, right[lv + 1]], axis=1),
                    ],
                    axis=0,
                )
                both = jnp.dot(lhs, rhs, preferred_element_type=F32)
                kernel = jnp.where(apart >= (1 << lv), both[:, :CHUNK], kernel)
                kernel = jnp.where(apart >= (2 << lv), both[:, CHUNK:], kernel)
            back = jnp.exp2(-suf)
            aux = jnp.concatenate(
                [left[LEVELS - 1], gains * jnp.exp2(-pre), back, back], axis=0
            ).T.astype(BF16)
            rhs = jnp.concatenate([right[LEVELS - 1], zero, zero, zero], axis=0)
            last = jnp.dot(aux, rhs, preferred_element_type=F32)
            kernel = jnp.where(apart >= (1 << (LEVELS - 1)), last, kernel)
            kf_ref[span, :] = kernel.astype(BF16)
            ka_ref[span, :] = kernel.T.astype(BF16)
            aux_ref[span, :] = aux


def stress_kernel(
    cur_ref, kf_ref, aux_ref, fresh_ref, decay_ref, in_ref, counts_ref,
    out_ref, lse_ref, state_ref, high_ref, amount_ref,
):
    step = pl.program_id(0)
    wires = cur_ref.shape[1]
    reps = wires // CHUNK
    modes = in_ref.shape[1]

    @pl.when(step == 0)
    def _():
        for k in range(reps):
            state_ref[:, k * CHUNK : (k + 1) * CHUNK] = in_ref[k]
        high_ref[...] = jnp.full_like(high_ref, -1e30)
        amount_ref[...] = jnp.zeros_like(amount_ref)

    scale = counts_ref[...].astype(F32) * 0.25
    scale2 = scale * (SHARPNESS * LOG2E)
    zero1 = jnp.zeros((modes, wires), BF16)
    zero2 = jnp.zeros((CHUNK - 2 * modes, wires), BF16)
    state, high, amount = state_ref[...], high_ref[...], amount_ref[...]
    for c in range(cur_ref.shape[0] // CHUNK):
        span = slice(c * CHUNK, (c + 1) * CHUNK)
        rows = slice(c * modes, (c + 1) * modes)
        lhs = jnp.concatenate([kf_ref[span, :], aux_ref[span, :]], axis=1)
        rhs = jnp.concatenate([cur_ref[span, :], zero1, state.astype(BF16), zero2], axis=0)
        acc = jnp.dot(lhs, rhs, preferred_element_type=F32)
        out_ref[span, :] = (acc * scale).astype(BF16)
        z = (acc * scale2).reshape(CHUNK // 8, 8, wires)
        new = jnp.maximum(high, jnp.max(z, axis=0))
        amount = amount * jnp.exp2(high - new) + jnp.sum(jnp.exp2(z - new[None]), axis=0)
        high = new
        state = wide(decay_ref[rows, :], reps) * state + fresh_ref[rows, :]
    state_ref[...], high_ref[...], amount_ref[...] = state, high, amount

    @pl.when(step == pl.num_programs(0) - 1)
    def _():
        top = jnp.max(high, axis=0, keepdims=True)
        total = jnp.sum(amount * jnp.exp2(high - top), axis=0, keepdims=True)
        value = top + jnp.log(total) * LOG2E
        lse_ref[...] = jnp.broadcast_to(value[None], lse_ref.shape)


def adjoint_kernel(
    cot_ref, ka_ref, aux_ref, fresh_ref, decay_ref, in_ref, counts_ref, out_ref, state_ref
):
    step = pl.program_id(0)
    wires = cot_ref.shape[1]
    reps = wires // CHUNK
    modes = in_ref.shape[1]

    @pl.when(step == 0)
    def _():
        for k in range(reps):
            state_ref[:, k * CHUNK : (k + 1) * CHUNK] = in_ref[k]

    scale = counts_ref[...].astype(F32) * 0.25
    zero2 = jnp.zeros((2 * modes, wires), BF16)
    zero1 = jnp.zeros((CHUNK - 3 * modes, wires), BF16)
    state = state_ref[...]
    for c in reversed(range(cot_ref.shape[0] // CHUNK)):
        span = slice(c * CHUNK, (c + 1) * CHUNK)
        rows = slice(c * modes, (c + 1) * modes)
        lhs = jnp.concatenate([ka_ref[span, :], aux_ref[span, :]], axis=1)
        rhs = jnp.concatenate([cot_ref[span, :], zero2, state.astype(BF16), zero1], axis=0)
        acc = jnp.dot(lhs, rhs, preferred_element_type=F32)
        out_ref[span, :] = (acc * scale).astype(BF16)
        state = wide(decay_ref[rows, :], reps) * state + fresh_ref[rows, :]
    state_ref[...] = state


def on_hbm(a):
    return pltpu.with_memory_space_constraint(a, pltpu.HBM)


def steps_for(chunks):
    for steps in (4, 3, 2):
        if chunks % steps == 0:
            return steps
    return 1


def scan_devices(msg, reps, run_part, parts):
    n = lax.axis_size("tm")
    me = lax.axis_index("tm")
    before = jnp.zeros_like(msg[:reps])
    after = jnp.zeros_like(msg[:reps])
    d_before = jnp.ones_like(msg[2 * reps :])
    d_after = jnp.ones_like(msg[2 * reps :])
    hops = [1 << k for k in range(n.bit_length() - 1)]
    for index, hop in enumerate(hops):
        pairs = [(i, i ^ hop) for i in range(n)]
        upper = (me & hop) != 0
        mine_f, mine_a, mine_d = msg[:reps], msg[reps : 2 * reps], msg[2 * reps :]
        part = index - len(hops) + parts
        final = index == len(hops) - 1
        sent = jnp.where(upper, mine_a, mine_f) if final else msg
        sent = run_part.gate(part, sent)
        got = lax.ppermute(sent, "tm", pairs)
        got = run_part(part, got)
        if final:
            before = jnp.where(upper, d_before * got + before, before)
            after = jnp.where(upper, after, d_after * got + after)
        else:
            got_f, got_a, got_d = got[:reps], got[reps : 2 * reps], got[2 * reps :]
            next_f = jnp.where(upper, mine_d * got_f + mine_f, got_d * mine_f + got_f)
            next_a = jnp.where(upper, got_d * mine_a + got_a, mine_d * got_a + mine_a)
            msg = jnp.concatenate([next_f, next_a, mine_d * got_d], axis=0)
            before = jnp.where(upper, d_before * got_f + before, before)
            after = jnp.where(upper, after, d_after * got_a + after)
            d_before = jnp.where(upper, d_before * got_d, d_before)
            d_after = jnp.where(upper, d_after, d_after * got_d)
            msg, before, after, d_before, d_after = lax.optimization_barrier(
                (msg, before, after, d_before, d_after)
            )
    return before, after


class KernelParts:
    def __init__(self, heat, rates, fits, parts, params):
        self.heat, self.rates, self.fits, self.parts = heat, rates, fits, parts
        self.params, self.arrays = params, ()

    def gate(self, part, sent):
        if part >= 0:
            sent, self.rates = lax.optimization_barrier((sent, self.rates))
        return sent

    def __call__(self, part, got):
        if part < 0:
            return got
        modes, samples = self.heat.shape
        length = samples // self.parts
        inner = 2 if (length // CHUNK) % 2 == 0 else 1
        block = length // inner
        small = pl.BlockSpec((1, modes), lambda i: (0, 0))
        rest = len(self.arrays)
        self.arrays = tuple(
            pl.pallas_call(
                kernels_kernel,
                name="kernels",
                grid=(inner,),
                in_specs=[
                    pl.BlockSpec((modes, block), lambda i: (0, part * inner + i)),
                    small,
                    small,
                ]
                + [pl.BlockSpec(memory_space=pl.ANY)] * rest,
                out_specs=[pl.BlockSpec((block, CHUNK), lambda i: (part * inner + i, 0))] * 3,
                out_shape=[jax.ShapeDtypeStruct((samples, CHUNK), BF16)] * 3,
                input_output_aliases={3 + k: k for k in range(rest)},
                compiler_params=self.params,
                cost_estimate=pl.CostEstimate(
                    flops=20 * length * CHUNK * CHUNK, bytes_accessed=8 << 20, transcendentals=0
                ),
            )(on_hbm(self.heat), on_hbm(self.rates), on_hbm(self.fits), *self.arrays)
        )
        got, arrays = lax.optimization_barrier((got, self.arrays))
        self.arrays = arrays
        return got


def body(currents, seed_on_tension, mode_diffusivity_factor, decay_rates, fit_weights, counts):
    samples, wires = currents.shape
    modes = decay_rates.shape[0]
    devices = lax.axis_size("tm")
    chunks = samples // CHUNK
    steps = steps_for(chunks)
    block = samples // steps
    mblock = chunks * modes // steps
    reps = wires // CHUNK
    rates = decay_rates.reshape(1, modes)
    fits = fit_weights.reshape(1, modes)
    counts = counts.reshape(1, wires)
    params = pltpu.CompilerParams(vmem_limit_bytes=24 << 20)
    small = pl.BlockSpec((1, modes), lambda i: (0, 0))
    flops = 2 * samples * wires

    fresh_f, fresh_a, decay, msg = pl.pallas_call(
        totals_kernel,
        name="totals",
        grid=(steps,),
        in_specs=[
            pl.BlockSpec((modes, block), lambda i: (0, i)),
            small,
            small,
            pl.BlockSpec((block, wires), lambda i: (i, 0)),
            pl.BlockSpec((block, wires), lambda i: (i, 0)),
        ],
        out_specs=[
            pl.BlockSpec((mblock, wires), lambda i: (i, 0)),
            pl.BlockSpec((mblock, wires), lambda i: (i, 0)),
            pl.BlockSpec((mblock, CHUNK), lambda i: (i, 0)),
            pl.BlockSpec((2 * reps + 1, modes, CHUNK), lambda i: (0, 0, 0)),
        ],
        out_shape=[
            pltpu.HBM((chunks * modes, wires), F32),
            pltpu.HBM((chunks * modes, wires), F32),
            pltpu.HBM((chunks * modes, CHUNK), F32),
            jax.ShapeDtypeStruct((2 * reps + 1, modes, CHUNK), F32),
        ],
        scratch_shapes=[
            pltpu.VMEM((modes, wires), F32),
            pltpu.VMEM((modes, wires), F32),
            pltpu.VMEM((modes, CHUNK), F32),
        ],
        compiler_params=params,
        cost_estimate=pl.CostEstimate(
            flops=2 * modes * flops, bytes_accessed=14 << 20, transcendentals=0
        ),
    )(
        on_hbm(mode_diffusivity_factor),
        on_hbm(rates),
        on_hbm(fits),
        on_hbm(currents),
        on_hbm(seed_on_tension),
    )

    parts = 3 if chunks % 3 == 0 else 1
    covered = KernelParts(mode_diffusivity_factor, rates, fits, parts, params)
    before, after = scan_devices(msg, reps, covered, parts)
    kf, ka, aux = covered.arrays

    def common(reverse):
        def at(i):
            return (steps - 1 - i if reverse else i, 0)

        return [
            pl.BlockSpec((block, wires), at),
            pl.BlockSpec((block, CHUNK), at),
            pl.BlockSpec((block, CHUNK), at),
            pl.BlockSpec((mblock, wires), at),
            pl.BlockSpec((mblock, CHUNK), at),
            pl.BlockSpec((reps, modes, CHUNK), lambda i: (0, 0, 0)),
            pl.BlockSpec((1, wires), lambda i: (0, 0)),
        ], pl.BlockSpec((block, wires), at)

    specs, out_spec = common(False)
    tension, lse = pl.pallas_call(
        stress_kernel,
        name="stress",
        grid=(steps,),
        in_specs=specs,
        out_specs=[out_spec, pl.BlockSpec((devices, 1, wires), lambda i: (0, 0, 0))],
        out_shape=[
            jax.ShapeDtypeStruct((samples, wires), BF16),
            pltpu.HBM((devices, 1, wires), F32),
        ],
        scratch_shapes=[
            pltpu.VMEM((modes, wires), F32),
            pltpu.VMEM((8, wires), F32),
            pltpu.VMEM((8, wires), F32),
        ],
        compiler_params=params,
        cost_estimate=pl.CostEstimate(
            flops=2 * CHUNK * flops, bytes_accessed=10 << 20, transcendentals=0
        ),
    )(on_hbm(currents), kf, aux, on_hbm(fresh_f), on_hbm(decay), before, on_hbm(counts))

    all_lse = lax.all_to_all(lse, "tm", 0, 0, tiled=True)

    specs, out_spec = common(True)
    gradient = pl.pallas_call(
        adjoint_kernel,
        name="adjoint",
        grid=(steps,),
        in_specs=specs,
        out_specs=out_spec,
        out_shape=jax.ShapeDtypeStruct((samples, wires), BF16),
        scratch_shapes=[pltpu.VMEM((modes, wires), F32)],
        compiler_params=params,
        cost_estimate=pl.CostEstimate(
            flops=2 * CHUNK * flops, bytes_accessed=10 << 20, transcendentals=0
        ),
    )(on_hbm(seed_on_tension), ka, aux, on_hbm(fresh_a), on_hbm(decay), after, on_hbm(counts))

    top = jnp.max(all_lse, axis=0)
    total = jnp.sum(jnp.exp2(all_lse - top[None]), axis=0)
    softened = ((top * LN2 + jnp.log(total)) / SHARPNESS).reshape(wires)
    return (tension, gradient, softened)


def solution(mesh):
    placed = (P("tm", "parts"), P("tm", "parts"), P(None, ("parts", "tm")), P(), P(), P("parts"))
    return jax.shard_map(
        body,
        mesh=mesh,
        in_specs=placed,
        out_specs=(P("tm", "parts"), P("tm", "parts"), P("parts")),
        check_vma=False,
    )
```

```python
import functools
import math

import jax
import jax.numpy as jnp
from jax import lax
from jax.experimental import pallas as pl
from jax.experimental.pallas import tpu as pltpu
from jax.sharding import PartitionSpec as P

CHUNK = 128
LEVELS = 7
SHARPNESS = 4.0
LOG2E = math.log2(math.e)
LN2 = math.log(2.0)
F32 = jnp.float32
BF16 = jnp.bfloat16


def as_column(row):
    m = row.shape[1]
    r = lax.broadcasted_iota(jnp.int32, (m, m), 0)
    c = lax.broadcasted_iota(jnp.int32, (m, m), 1)
    return jnp.sum(jnp.where(r == c, jnp.broadcast_to(row, (m, m)), 0.0), axis=1, keepdims=True)


def rates_and_gains(rates_ref, fit_ref):
    rates = as_column(rates_ref[...])
    gains = as_column(fit_ref[...]) * jnp.sqrt(rates)
    return rates * LOG2E, gains


def doubling(heat, with_levels):
    lane = lax.broadcasted_iota(jnp.int32, heat.shape, 1)
    pre, suf = heat, jnp.zeros_like(heat)
    tables = []
    for level in range(LEVELS):
        half = 1 << level
        second = (lane & half) != 0
        if with_levels:
            tables.append(jnp.exp2(-jnp.where(second, pre, suf)))
        total = pre + suf
        sibling = jnp.where(
            second, pltpu.roll(total, half, 1), pltpu.roll(total, CHUNK - half, 1)
        )
        pre = jnp.where(second, pre + sibling, pre)
        suf = jnp.where(second, suf, suf + sibling)
    return pre, suf, tables


def wide(a, times):
    return jnp.concatenate([a] * times, axis=1)


def stacked(heat_ref, speed, first, count):
    return jnp.concatenate(
        [
            heat_ref[:, c * CHUNK : (c + 1) * CHUNK] * speed
            for c in range(first, first + count)
        ],
        axis=0,
    )


def group_of(chunks, most):
    return max(g for g in range(1, most + 1) if chunks % g == 0)


def pieces_of(chunks):
    if chunks % 8:
        return [1] * chunks
    unit = chunks // 8
    return [3 * unit, 2 * unit, 2 * unit, unit]


def prefixes(heat):
    high = heat.astype(BF16)
    rest = heat - high.astype(F32)
    middle = rest.astype(BF16)
    low = (rest - middle.astype(F32)).astype(BF16)
    v = lax.broadcasted_iota(jnp.int32, (CHUNK, CHUNK), 0)
    u = lax.broadcasted_iota(jnp.int32, (CHUNK, CHUNK), 1)
    ones = jnp.concatenate(
        [jnp.where(v <= u, 1.0, 0.0).astype(BF16), jnp.where(v > u, 1.0, 0.0).astype(BF16)],
        axis=1,
    )
    both = jnp.dot(
        jnp.concatenate([high, middle, low], axis=1),
        jnp.concatenate([ones] * 3, axis=0),
        preferred_element_type=F32,
    )
    return both[:, :CHUNK], both[:, CHUNK:]


def totals_kernel(
    heat_hbm, rates_hbm, fits_hbm, cur_hbm, cot_hbm,
    cur_ref, fresh_f_ref, fresh_a_ref, decay_ref, msg_ref,
    cot_ref, heat_ref, rates_ref, fits_ref, start_ref, back_ref, small_sem, cur_sem, cot_sem,
):
    modes = heat_ref.shape[0]
    samples, wires = cur_ref.shape
    reps = wires // CHUNK
    chunks = samples // CHUNK
    group = group_of(chunks, 3)

    small = [
        pltpu.make_async_copy(heat_hbm, heat_ref, small_sem.at[0]),
        pltpu.make_async_copy(rates_hbm, rates_ref, small_sem.at[1]),
        pltpu.make_async_copy(fits_hbm, fits_ref, small_sem.at[2]),
    ]
    for copy in small:
        copy.start()
    loads = []
    at = 0
    for k, piece in enumerate(pieces_of(chunks)):
        rows = pl.ds(at * CHUNK, piece * CHUNK)
        pair = (
            pltpu.make_async_copy(cur_hbm.at[rows], cur_ref.at[rows], cur_sem.at[k]),
            pltpu.make_async_copy(cot_hbm.at[rows], cot_ref.at[rows], cot_sem.at[k]),
        )
        for copy in pair:
            copy.start()
        loads.append((at, piece, pair))
        at += piece
    for copy in small:
        copy.wait()

    speed, gains = rates_and_gains(rates_ref, fits_ref)
    gain_stack = jnp.concatenate([gains] * group, axis=0)
    for first in range(0, chunks, group):
        rows = slice(first * modes, (first + group) * modes)
        pre, suf = prefixes(stacked(heat_ref, speed, first, group))
        start_ref[rows, :] = (gain_stack * jnp.exp2(-pre)).astype(BF16)
        back_ref[rows, :] = jnp.exp2(-suf).astype(BF16)
        decay_ref[rows, :] = jnp.exp2(-(pre + suf))

    tf = jnp.zeros((modes, wires), F32)
    ta = jnp.zeros((modes, wires), F32)
    dc = jnp.ones((modes, CHUNK), F32)
    for first, piece, pair in loads:
        for copy in pair:
            copy.wait()
        for c in range(first, first + piece):
            span = slice(c * CHUNK, (c + 1) * CHUNK)
            rows = slice(c * modes, (c + 1) * modes)
            decay = decay_ref[rows, :]
            fresh_f = jnp.dot(back_ref[rows, :], cur_ref[span, :], preferred_element_type=F32)
            fresh_a = jnp.dot(start_ref[rows, :], cot_ref[span, :], preferred_element_type=F32)
            fresh_f_ref[rows, :] = fresh_f
            fresh_a_ref[rows, :] = fresh_a.astype(BF16)
            tf = wide(decay, reps) * tf + fresh_f
            ta = ta + wide(dc, reps) * fresh_a
            dc = dc * decay
    for k in range(reps):
        lanes = slice(k * CHUNK, (k + 1) * CHUNK)
        msg_ref[k] = tf[:, lanes]
        msg_ref[reps + k] = ta[:, lanes]
    msg_ref[2 * reps] = dc


def kernels_kernel(heat_ref, rates_ref, fit_ref, *refs):
    kf_ref, ka_ref, aux_ref = refs[-3:]
    modes = heat_ref.shape[0]
    chunks = heat_ref.shape[1] // CHUNK
    group = group_of(chunks, 2)
    speed, gains = rates_and_gains(rates_ref, fit_ref)
    gain_sum = jnp.sum(gains, axis=0, keepdims=True)
    t = lax.broadcasted_iota(jnp.int32, (CHUNK, CHUNK), 0)
    s = lax.broadcasted_iota(jnp.int32, (CHUNK, CHUNK), 1)
    apart = jnp.where(t >= s, t ^ s, -1)
    base = jnp.where(apart == 0, jnp.broadcast_to(gain_sum, (CHUNK, CHUNK)), 0.0)
    zero = jnp.zeros((modes, CHUNK), BF16)
    for first in range(0, chunks, group):
        pres, sufs, stacks = doubling(stacked(heat_ref, speed, first, group), True)
        for c in range(group):
            part = slice(c * modes, (c + 1) * modes)
            span = slice((first + c) * CHUNK, (first + c + 1) * CHUNK)
            pre, suf = pres[part], sufs[part]
            tables = [e[part] for e in stacks]
            left = [gains * e for e in tables]
            right = [e.astype(BF16) for e in tables]
            kernel = base
            for lv in range(0, LEVELS - 1, 2):
                lhs = jnp.concatenate([left[lv], left[lv + 1]], axis=0).T.astype(BF16)
                rhs = jnp.concatenate(
                    [
                        jnp.concatenate([right[lv], zero], axis=1),
                        jnp.concatenate([zero, right[lv + 1]], axis=1),
                    ],
                    axis=0,
                )
                both = jnp.dot(lhs, rhs, preferred_element_type=F32)
                kernel = jnp.where(apart >= (1 << lv), both[:, :CHUNK], kernel)
                kernel = jnp.where(apart >= (2 << lv), both[:, CHUNK:], kernel)
            back = jnp.exp2(-suf)
            aux = jnp.concatenate(
                [gains * jnp.exp2(-pre), back, left[LEVELS - 1], back], axis=0
            ).T.astype(BF16)
            rhs = jnp.concatenate([zero, zero, right[LEVELS - 1], zero], axis=0)
            last = jnp.dot(aux, rhs, preferred_element_type=F32)
            kernel = jnp.where(apart >= (1 << (LEVELS - 1)), last, kernel)
            kf_ref[span, :] = kernel.astype(BF16)
            ka_ref[span, :] = kernel.T.astype(BF16)
            aux_ref[span, :] = aux


def stress_kernel(
    cur_ref, kf_ref, aux_ref, fresh_ref, decay_ref, in_ref, counts_ref,
    out_hbm, lse_ref, out_ref, sem,
):
    samples, wires = cur_ref.shape
    reps = wires // CHUNK
    modes = in_ref.shape[1]
    scale = counts_ref[...].astype(F32) * 0.25
    scale2 = scale * (SHARPNESS * LOG2E)
    state = jnp.concatenate([in_ref[k] for k in range(reps)], axis=1)
    high = jnp.full((8, wires), -1e30, F32)
    amount = jnp.zeros((8, wires), F32)
    stores = []
    first = 0
    for k, piece in enumerate(pieces_of(samples // CHUNK)):
        for c in range(first, first + piece):
            span = slice(c * CHUNK, (c + 1) * CHUNK)
            rows = slice(c * modes, (c + 1) * modes)
            acc = jnp.dot(kf_ref[span, :], cur_ref[span, :], preferred_element_type=F32) + jnp.dot(
                aux_ref[span, :modes], state.astype(BF16), preferred_element_type=F32
            )
            out_ref[span, :] = (acc * scale).astype(BF16)
            z = (acc * scale2).reshape(CHUNK // 8, 8, wires)
            new = jnp.maximum(high, jnp.max(z, axis=0))
            amount = amount * jnp.exp2(high - new) + jnp.sum(jnp.exp2(z - new[None]), axis=0)
            high = new
            state = wide(decay_ref[rows, :], reps) * state + fresh_ref[rows, :]
        done = pl.ds(first * CHUNK, piece * CHUNK)
        copy = pltpu.make_async_copy(out_ref.at[done], out_hbm.at[done], sem.at[k])
        copy.start()
        stores.append(copy)
        first += piece
    top = jnp.max(high, axis=0, keepdims=True)
    total = jnp.sum(amount * jnp.exp2(high - top), axis=0, keepdims=True)
    value = top + jnp.log(total) * LOG2E
    lse_ref[...] = jnp.broadcast_to(value[None], lse_ref.shape)
    for copy in stores:
        copy.wait()


def adjoint_kernel(
    cot_hbm, ka_ref, aux_ref, fresh_ref, decay_ref, in_ref, counts_ref,
    out_hbm, cot_ref, out_ref, load_sem, sem,
):
    samples, wires = cot_ref.shape
    reps = wires // CHUNK
    chunks = samples // CHUNK
    modes = in_ref.shape[1]
    scale = counts_ref[...].astype(F32) * 0.25
    zero = jnp.zeros((modes, wires), BF16)
    state = jnp.concatenate([in_ref[k] for k in range(reps)], axis=1)
    loads = []
    end = chunks
    for k, piece in enumerate(pieces_of(chunks)):
        rows = pl.ds((end - piece) * CHUNK, piece * CHUNK)
        copy = pltpu.make_async_copy(cot_hbm.at[rows], cot_ref.at[rows], load_sem.at[k])
        copy.start()
        loads.append(copy)
        end -= piece
    stores = []
    end = chunks
    for k, piece in enumerate(pieces_of(chunks)):
        loads[k].wait()
        for c in reversed(range(end - piece, end)):
            span = slice(c * CHUNK, (c + 1) * CHUNK)
            rows = slice(c * modes, (c + 1) * modes)
            carried = jnp.concatenate([zero, state.astype(BF16)], axis=0)
            acc = jnp.dot(ka_ref[span, :], cot_ref[span, :], preferred_element_type=F32) + jnp.dot(
                aux_ref[span, : 2 * modes], carried, preferred_element_type=F32
            )
            out_ref[span, :] = (acc * scale).astype(BF16)
            state = wide(decay_ref[rows, :], reps) * state + fresh_ref[rows, :].astype(F32)
        done = pl.ds((end - piece) * CHUNK, piece * CHUNK)
        copy = pltpu.make_async_copy(out_ref.at[done], out_hbm.at[done], sem.at[k])
        copy.start()
        stores.append(copy)
        end -= piece
    for copy in stores:
        copy.wait()


def on_vmem(a):
    return pltpu.with_memory_space_constraint(a, pltpu.VMEM)


def on_hbm(a):
    return pltpu.with_memory_space_constraint(a, pltpu.HBM)


def hops_of(n):
    return [1 << k for k in range(n.bit_length() - 1)]


def scan_devices(msg, uppers, reps, run_part, parts):
    n = lax.axis_size("tm")
    before = jnp.zeros_like(msg[:reps])
    after = jnp.zeros_like(msg[:reps])
    d_before = jnp.ones_like(msg[2 * reps :])
    d_after = jnp.ones_like(msg[2 * reps :])
    hops = hops_of(n)
    for index, hop in enumerate(hops):
        pairs = [(i, i ^ hop) for i in range(n)]
        upper = uppers[index]
        mine_f, mine_a, mine_d = msg[:reps], msg[reps : 2 * reps], msg[2 * reps :]
        part = index - len(hops) + parts
        final = index == len(hops) - 1
        sent = jnp.where(upper, mine_a, mine_f) if final else msg
        sent = run_part.gate(part, sent)
        got = lax.ppermute(sent, "tm", pairs)
        got = run_part(part, got)
        if final:
            before = jnp.where(upper, d_before * got + before, before)
            after = jnp.where(upper, after, d_after * got + after)
        else:
            got_f, got_a, got_d = got[:reps], got[reps : 2 * reps], got[2 * reps :]
            next_f = jnp.where(upper, mine_d * got_f + mine_f, got_d * mine_f + got_f)
            next_a = jnp.where(upper, got_d * mine_a + got_a, mine_d * got_a + mine_a)
            msg = jnp.concatenate([next_f, next_a, mine_d * got_d], axis=0)
            before = jnp.where(upper, d_before * got_f + before, before)
            after = jnp.where(upper, after, d_after * got_a + after)
            d_before = jnp.where(upper, d_before * got_d, d_before)
            d_after = jnp.where(upper, d_after, d_after * got_d)
            msg, before, after, d_before, d_after = lax.optimization_barrier(
                (msg, before, after, d_before, d_after)
            )
    return before, after


class KernelParts:
    def __init__(self, heat, rates, fits, parts, params):
        self.heat, self.rates, self.fits, self.parts = heat, rates, fits, parts
        self.params, self.arrays = params, ()

    def gate(self, part, sent):
        if part >= 0:
            sent, self.rates = lax.optimization_barrier((sent, self.rates))
        return sent

    def __call__(self, part, got):
        if part < 0:
            return got
        modes, samples = self.heat.shape
        length = samples // self.parts
        inner = 2 if (length // CHUNK) % 2 == 0 else 1
        block = length // inner
        small = pl.BlockSpec((1, modes), lambda i: (0, 0))
        rest = len(self.arrays)
        self.arrays = tuple(
            pl.pallas_call(
                kernels_kernel,
                name="kernels",
                grid=(inner,),
                in_specs=[
                    pl.BlockSpec((modes, block), lambda i: (0, part * inner + i)),
                    small,
                    small,
                ]
                + [pl.BlockSpec(memory_space=pl.ANY)] * rest,
                out_specs=[pl.BlockSpec((block, CHUNK), lambda i: (part * inner + i, 0))] * 3,
                out_shape=[jax.ShapeDtypeStruct((samples, CHUNK), BF16)] * 3,
                input_output_aliases={3 + k: k for k in range(rest)},
                compiler_params=self.params,
                cost_estimate=pl.CostEstimate(
                    flops=20 * length * CHUNK * CHUNK, bytes_accessed=8 << 20, transcendentals=0
                ),
            )(on_hbm(self.heat), on_hbm(self.rates), on_hbm(self.fits), *self.arrays)
        )
        got, arrays = lax.optimization_barrier((got, self.arrays))
        self.arrays = arrays
        return got


def body(currents, seed_on_tension, mode_diffusivity_factor, decay_rates, fit_weights, counts):
    samples, wires = currents.shape
    modes = decay_rates.shape[0]
    devices = lax.axis_size("tm")
    chunks = samples // CHUNK
    reps = wires // CHUNK
    me = lax.axis_index("tm")
    uppers = tuple((me & hop) != 0 for hop in hops_of(devices))
    rates, uppers = lax.optimization_barrier((decay_rates.reshape(1, modes), uppers))
    fits = fit_weights.reshape(1, modes)
    counts = counts.reshape(1, wires)
    params = pltpu.CompilerParams(vmem_limit_bytes=16 << 20)
    apart = pl.BlockSpec(memory_space=pl.ANY)
    whole = pl.BlockSpec(memory_space=pltpu.VMEM)
    flops = 2 * samples * wires
    copies = len(pieces_of(chunks))

    cur, fresh_f, fresh_a, decay, msg = pl.pallas_call(
        totals_kernel,
        name="totals",
        in_specs=[apart] * 5,
        out_specs=[whole] * 5,
        out_shape=[
            pltpu.VMEM((samples, wires), BF16),
            pltpu.VMEM((chunks * modes, wires), F32),
            pltpu.VMEM((chunks * modes, wires), BF16),
            pltpu.VMEM((chunks * modes, CHUNK), F32),
            pltpu.VMEM((2 * reps + 1, modes, CHUNK), F32),
        ],
        scratch_shapes=[
            pltpu.VMEM((samples, wires), BF16),
            pltpu.VMEM((modes, samples), F32),
            pltpu.VMEM((1, modes), F32),
            pltpu.VMEM((1, modes), F32),
            pltpu.VMEM((chunks * modes, CHUNK), BF16),
            pltpu.VMEM((chunks * modes, CHUNK), BF16),
            pltpu.SemaphoreType.DMA((3,)),
            pltpu.SemaphoreType.DMA((copies,)),
            pltpu.SemaphoreType.DMA((copies,)),
        ],
        compiler_params=params,
        cost_estimate=pl.CostEstimate(
            flops=2 * modes * flops, bytes_accessed=14 << 20, transcendentals=0
        ),
    )(
        on_hbm(mode_diffusivity_factor),
        on_hbm(rates),
        on_hbm(fits),
        on_hbm(currents),
        on_hbm(seed_on_tension),
    )

    parts = 3 if chunks % 3 == 0 else 1
    covered = KernelParts(mode_diffusivity_factor, rates, fits, parts, params)
    before, after = scan_devices(msg, uppers, reps, covered, parts)
    kf, ka, aux = covered.arrays

    tension, lse = pl.pallas_call(
        stress_kernel,
        name="stress",
        in_specs=[whole] * 7,
        out_specs=[apart, whole],
        out_shape=[
            pltpu.HBM((samples, wires), BF16),
            pltpu.HBM((devices, 1, wires), F32),
        ],
        scratch_shapes=[pltpu.VMEM((samples, wires), BF16), pltpu.SemaphoreType.DMA((copies,))],
        compiler_params=params,
        cost_estimate=pl.CostEstimate(
            flops=2 * CHUNK * flops, bytes_accessed=10 << 20, transcendentals=0
        ),
    )(*map(on_vmem, (cur, kf, aux, fresh_f, decay, before, counts)))

    all_lse = lax.all_to_all(lse, "tm", 0, 0, tiled=True)

    gradient = pl.pallas_call(
        adjoint_kernel,
        name="adjoint",
        in_specs=[apart] + [whole] * 6,
        out_specs=apart,
        out_shape=pltpu.HBM((samples, wires), BF16),
        scratch_shapes=[
            pltpu.VMEM((samples, wires), BF16),
            pltpu.VMEM((samples, wires), BF16),
            pltpu.SemaphoreType.DMA((copies,)),
            pltpu.SemaphoreType.DMA((copies,)),
        ],
        compiler_params=params,
        cost_estimate=pl.CostEstimate(
            flops=2 * CHUNK * flops, bytes_accessed=10 << 20, transcendentals=0
        ),
    )(
        on_hbm(seed_on_tension),
        *map(on_vmem, (ka, aux, fresh_a, decay, after, counts)),
    )

    top = jnp.max(all_lse, axis=0)
    total = jnp.sum(jnp.exp2(all_lse - top[None]), axis=0)
    softened = ((top * LN2 + jnp.log(total)) / SHARPNESS).reshape(wires)
    return (tension, gradient, softened)


def solution(mesh):
    placed = (P("tm", "parts"), P("tm", "parts"), P(None, ("parts", "tm")), P(), P(), P("parts"))
    return jax.shard_map(
        body,
        mesh=mesh,
        in_specs=placed,
        out_specs=(P("tm", "parts"), P("tm", "parts"), P("parts")),
        check_vma=False,
    )
```

```python
import functools
import math

import jax
import jax.numpy as jnp
from jax import lax
from jax.experimental import pallas as pl
from jax.experimental.pallas import tpu as pltpu
from jax.sharding import PartitionSpec as P

CHUNK = 128
LEVELS = 7
SHARPNESS = 4.0
LOG2E = math.log2(math.e)
LN2 = math.log(2.0)
F32 = jnp.float32
BF16 = jnp.bfloat16


def as_column(row):
    m = row.shape[1]
    r = lax.broadcasted_iota(jnp.int32, (m, m), 0)
    c = lax.broadcasted_iota(jnp.int32, (m, m), 1)
    return jnp.sum(jnp.where(r == c, jnp.broadcast_to(row, (m, m)), 0.0), axis=1, keepdims=True)


def rates_and_gains(rates_ref, fit_ref):
    rates = as_column(rates_ref[...])
    gains = as_column(fit_ref[...]) * jnp.sqrt(rates)
    return rates * LOG2E, gains


def level_sums():
    v = lax.broadcasted_iota(jnp.int32, (CHUNK, CHUNK), 0)
    u = lax.broadcasted_iota(jnp.int32, (CHUNK, CHUNK), 1)
    apart = v ^ u
    tables = []
    for level in range(LEVELS):
        half = 1 << level
        near = apart < half
        inside = jnp.where((u & half) != 0, jnp.where(v <= u, -1.0, 0.0), jnp.where(v > u, -1.0, 0.0))
        tables.append(jnp.where(near, inside, 0.0).astype(BF16))
    return jnp.concatenate(tables, axis=1)


def wide(a, times):
    return jnp.concatenate([a] * times, axis=1)


def stacked(heat_ref, speed, first, count):
    return jnp.concatenate(
        [
            heat_ref[:, c * CHUNK : (c + 1) * CHUNK] * speed
            for c in range(first, first + count)
        ],
        axis=0,
    )


def group_of(chunks, most):
    return max(g for g in range(1, most + 1) if chunks % g == 0)


def pieces_of(chunks):
    if chunks % 8:
        return [1] * chunks
    unit = chunks // 8
    return [3 * unit, 2 * unit, 2 * unit, unit]


def prefixes(heat):
    high = heat.astype(BF16)
    rest = heat - high.astype(F32)
    middle = rest.astype(BF16)
    low = (rest - middle.astype(F32)).astype(BF16)
    v = lax.broadcasted_iota(jnp.int32, (CHUNK, CHUNK), 0)
    u = lax.broadcasted_iota(jnp.int32, (CHUNK, CHUNK), 1)
    ones = jnp.concatenate(
        [jnp.where(v <= u, 1.0, 0.0).astype(BF16), jnp.where(v > u, 1.0, 0.0).astype(BF16)],
        axis=1,
    )
    both = jnp.dot(
        jnp.concatenate([high, middle, low], axis=1),
        jnp.concatenate([ones] * 3, axis=0),
        preferred_element_type=F32,
    )
    return both[:, :CHUNK], both[:, CHUNK:], jnp.concatenate([high, middle], axis=1)


def totals_kernel(
    heat_hbm, rates_hbm, fits_hbm, cur_hbm, cot_hbm,
    cur_ref, fresh_f_ref, fresh_a_ref, decay_ref, msg_ref,
    split_ref, start_ref, back_ref, gains_ref, sums_ref,
    cot_ref, heat_ref, rates_ref, fits_ref, small_sem, cur_sem, cot_sem,
):
    modes = heat_ref.shape[0]
    samples, wires = cur_ref.shape
    reps = wires // CHUNK
    chunks = samples // CHUNK
    group = group_of(chunks, 3)

    small = [
        pltpu.make_async_copy(heat_hbm, heat_ref, small_sem.at[0]),
        pltpu.make_async_copy(rates_hbm, rates_ref, small_sem.at[1]),
        pltpu.make_async_copy(fits_hbm, fits_ref, small_sem.at[2]),
    ]
    for copy in small:
        copy.start()
    loads = []
    at = 0
    for k, piece in enumerate(pieces_of(chunks)):
        rows = pl.ds(at * CHUNK, piece * CHUNK)
        pair = (
            pltpu.make_async_copy(cur_hbm.at[rows], cur_ref.at[rows], cur_sem.at[k]),
            pltpu.make_async_copy(cot_hbm.at[rows], cot_ref.at[rows], cot_sem.at[k]),
        )
        for copy in pair:
            copy.start()
        loads.append((at, piece, pair))
        at += piece
    sums_ref[...] = level_sums()
    for copy in small:
        copy.wait()

    speed, gains = rates_and_gains(rates_ref, fits_ref)
    gain_stack = jnp.concatenate([gains] * group, axis=0)
    gains_ref[...] = jnp.broadcast_to(
        jnp.concatenate([gains] * (CHUNK // modes), axis=0), gains_ref.shape
    )
    for first in range(0, chunks, group):
        rows = slice(first * modes, (first + group) * modes)
        pre, suf, split = prefixes(stacked(heat_ref, speed, first, group))
        split_ref[rows, :] = split
        start_ref[rows, :] = (gain_stack * jnp.exp2(-pre)).astype(BF16)
        back_ref[rows, :] = jnp.exp2(-suf).astype(BF16)
        decay_ref[rows, :] = jnp.exp2(-(pre + suf))

    tf = jnp.zeros((modes, wires), F32)
    ta = jnp.zeros((modes, wires), F32)
    dc = jnp.ones((modes, CHUNK), F32)
    for first, piece, pair in loads:
        for copy in pair:
            copy.wait()
        for c in range(first, first + piece):
            span = slice(c * CHUNK, (c + 1) * CHUNK)
            rows = slice(c * modes, (c + 1) * modes)
            decay = decay_ref[rows, :]
            fresh_f = jnp.dot(back_ref[rows, :], cur_ref[span, :], preferred_element_type=F32)
            fresh_a = jnp.dot(start_ref[rows, :], cot_ref[span, :], preferred_element_type=F32)
            fresh_f_ref[rows, :] = fresh_f
            fresh_a_ref[rows, :] = fresh_a.astype(BF16)
            tf = wide(decay, reps) * tf + fresh_f
            ta = ta + wide(dc, reps) * fresh_a
            dc = dc * decay
    for k in range(reps):
        lanes = slice(k * CHUNK, (k + 1) * CHUNK)
        msg_ref[k] = tf[:, lanes]
        msg_ref[reps + k] = ta[:, lanes]
    msg_ref[2 * reps] = dc


def kernels_kernel(modes, first, split_ref, gains_ref, sums_ref, kf_ref, ka_ref):
    group = CHUNK // modes
    t = lax.broadcasted_iota(jnp.int32, (CHUNK, CHUNK), 0)
    s = lax.broadcasted_iota(jnp.int32, (CHUNK, CHUNK), 1)
    apart = jnp.where(t >= s, t ^ s, -1)
    gains = gains_ref[...]
    gain_sum = jnp.sum(gains[:modes], axis=0, keepdims=True)
    base = jnp.where(apart == 0, jnp.broadcast_to(gain_sum, (CHUNK, CHUNK)), 0.0)
    for g in range(kf_ref.shape[0] // (CHUNK * group)):
        rows = slice((first + g) * CHUNK, (first + g + 1) * CHUNK)
        sums = jnp.dot(
            split_ref[rows, :],
            jnp.concatenate([sums_ref[...]] * 2, axis=0),
            preferred_element_type=F32,
        )
        kernels = [base] * group
        for level in range(LEVELS):
            table = jnp.exp2(sums[:, level * CHUNK : (level + 1) * CHUNK])
            left = (gains * table).astype(BF16).T
            right = table.astype(BF16)
            columns = []
            for c in range(group):
                parts = []
                if c > 0:
                    parts.append(jnp.zeros((c * modes, CHUNK), BF16))
                parts.append(right[c * modes : (c + 1) * modes])
                if c + 1 < group:
                    parts.append(jnp.zeros(((group - 1 - c) * modes, CHUNK), BF16))
                columns.append(jnp.concatenate(parts, axis=0))
            both = jnp.dot(left, jnp.concatenate(columns, axis=1), preferred_element_type=F32)
            keep = apart >= (1 << level)
            kernels = [
                jnp.where(keep, both[:, c * CHUNK : (c + 1) * CHUNK], kernels[c])
                for c in range(group)
            ]
        for c in range(group):
            span = slice((g * group + c) * CHUNK, (g * group + c + 1) * CHUNK)
            kernel = kernels[c].astype(BF16)
            kf_ref[span, :] = kernel
            ka_ref[span, :] = kernel.T


def carry(table, state):
    return lax.dot_general(
        table, state, (((0,), (0,)), ((), ())), preferred_element_type=F32
    )


def part_of(refs, c):
    for ref in refs:
        chunks = ref.shape[0] // CHUNK
        if c < chunks:
            return ref[c * CHUNK : (c + 1) * CHUNK, :]
        c -= chunks


def stress_kernel(
    cur_ref, start_ref, fresh_ref, decay_ref, in_ref, counts_ref, *refs
):
    kf_refs = refs[:-4]
    out_hbm, lse_ref, out_ref, sem = refs[-4:]
    samples, wires = cur_ref.shape
    reps = wires // CHUNK
    modes = in_ref.shape[1]
    scale = counts_ref[...].astype(F32) * 0.25
    scale2 = scale * (SHARPNESS * LOG2E)
    state = jnp.concatenate([in_ref[k] for k in range(reps)], axis=1)
    high = jnp.full((8, wires), -1e30, F32)
    amount = jnp.zeros((8, wires), F32)
    stores = []
    first = 0
    for k, piece in enumerate(pieces_of(samples // CHUNK)):
        for c in range(first, first + piece):
            span = slice(c * CHUNK, (c + 1) * CHUNK)
            rows = slice(c * modes, (c + 1) * modes)
            acc = jnp.dot(part_of(kf_refs, c), cur_ref[span, :], preferred_element_type=F32)
            acc = acc + carry(start_ref[rows, :], state.astype(BF16))
            out_ref[span, :] = (acc * scale).astype(BF16)
            z = (acc * scale2).reshape(CHUNK // 8, 8, wires)
            new = jnp.maximum(high, jnp.max(z, axis=0))
            amount = amount * jnp.exp2(high - new) + jnp.sum(jnp.exp2(z - new[None]), axis=0)
            high = new
            state = wide(decay_ref[rows, :], reps) * state + fresh_ref[rows, :]
        done = pl.ds(first * CHUNK, piece * CHUNK)
        copy = pltpu.make_async_copy(out_ref.at[done], out_hbm.at[done], sem.at[k])
        copy.start()
        stores.append(copy)
        first += piece
    top = jnp.max(high, axis=0, keepdims=True)
    total = jnp.sum(amount * jnp.exp2(high - top), axis=0, keepdims=True)
    value = top + jnp.log(total) * LOG2E
    lse_ref[...] = jnp.broadcast_to(value[None], lse_ref.shape)
    for copy in stores:
        copy.wait()


def adjoint_kernel(
    cot_hbm, back_ref, fresh_ref, decay_ref, in_ref, counts_ref, *refs
):
    ka_refs = refs[:-5]
    out_hbm, cot_ref, out_ref, load_sem, sem = refs[-5:]
    samples, wires = cot_ref.shape
    reps = wires // CHUNK
    chunks = samples // CHUNK
    modes = in_ref.shape[1]
    scale = counts_ref[...].astype(F32) * 0.25
    state = jnp.concatenate([in_ref[k] for k in range(reps)], axis=1)
    loads = []
    end = chunks
    for k, piece in enumerate(pieces_of(chunks)):
        rows = pl.ds((end - piece) * CHUNK, piece * CHUNK)
        copy = pltpu.make_async_copy(cot_hbm.at[rows], cot_ref.at[rows], load_sem.at[k])
        copy.start()
        loads.append(copy)
        end -= piece
    stores = []
    end = chunks
    for k, piece in enumerate(pieces_of(chunks)):
        loads[k].wait()
        for c in reversed(range(end - piece, end)):
            span = slice(c * CHUNK, (c + 1) * CHUNK)
            rows = slice(c * modes, (c + 1) * modes)
            acc = jnp.dot(part_of(ka_refs, c), cot_ref[span, :], preferred_element_type=F32)
            acc = acc + carry(back_ref[rows, :], state.astype(BF16))
            out_ref[span, :] = (acc * scale).astype(BF16)
            state = wide(decay_ref[rows, :], reps) * state + fresh_ref[rows, :].astype(F32)
        done = pl.ds((end - piece) * CHUNK, piece * CHUNK)
        copy = pltpu.make_async_copy(out_ref.at[done], out_hbm.at[done], sem.at[k])
        copy.start()
        stores.append(copy)
        end -= piece
    for copy in stores:
        copy.wait()


def on_vmem(a):
    return pltpu.with_memory_space_constraint(a, pltpu.VMEM)


def on_hbm(a):
    return pltpu.with_memory_space_constraint(a, pltpu.HBM)


def hops_of(n):
    return [1 << k for k in range(n.bit_length() - 1)]


def scan_devices(msg, uppers, reps, run_part, parts):
    n = lax.axis_size("tm")
    half = reps // 2
    hops = hops_of(n)
    late = uppers[0]
    pairs = [(i, i ^ 1) for i in range(n)]

    low_f, high_f = msg[:half], msg[half:reps]
    low_a, high_a = msg[reps : reps + half], msg[reps + half : 2 * reps]
    mine_d = msg[2 * reps :]
    sent = jnp.concatenate(
        [jnp.where(late, low_f, high_f), jnp.where(late, low_a, high_a), mine_d], axis=0
    )
    mine_f, mine_a = jnp.where(late, high_f, low_f), jnp.where(late, high_a, low_a)
    got = lax.ppermute(sent, "tm", pairs)
    got_f, got_a, got_d = got[:half], got[half : 2 * half], got[2 * half :]
    first_f, last_a = jnp.where(late, got_f, mine_f), jnp.where(late, mine_a, got_a)
    first_d, last_d = jnp.where(late, got_d, mine_d), jnp.where(late, mine_d, got_d)
    msg = jnp.concatenate(
        [
            last_d * first_f + jnp.where(late, mine_f, got_f),
            jnp.where(late, got_a, mine_a) + first_d * last_a,
            mine_d * got_d,
        ],
        axis=0,
    )
    before = jnp.zeros_like(mine_f)
    after = jnp.zeros_like(mine_f)
    d_before = jnp.ones_like(mine_d)
    d_after = jnp.ones_like(mine_d)
    msg, first_f, last_a, first_d, last_d = lax.optimization_barrier(
        (msg, first_f, last_a, first_d, last_d)
    )
    for index, hop in enumerate(hops):
        if index == 0:
            continue
        upper = uppers[index]
        mine_f, mine_a, mine_d = msg[:half], msg[half : 2 * half], msg[2 * half :]
        part = index - len(hops) + parts
        final = index == len(hops) - 1
        sent = jnp.where(upper, mine_a, mine_f) if final else msg
        sent = run_part.gate(part, sent)
        got = lax.ppermute(sent, "tm", [(i, i ^ hop) for i in range(n)])
        got = run_part(part, got)
        if final:
            before = jnp.where(upper, d_before * got + before, before)
            after = jnp.where(upper, after, d_after * got + after)
        else:
            got_f, got_a, got_d = got[:half], got[half : 2 * half], got[2 * half :]
            next_f = jnp.where(upper, mine_d * got_f + mine_f, got_d * mine_f + got_f)
            next_a = jnp.where(upper, got_d * mine_a + got_a, mine_d * got_a + mine_a)
            msg = jnp.concatenate([next_f, next_a, mine_d * got_d], axis=0)
            before = jnp.where(upper, d_before * got_f + before, before)
            after = jnp.where(upper, after, d_after * got_a + after)
            d_before = jnp.where(upper, d_before * got_d, d_before)
            d_after = jnp.where(upper, d_after, d_after * got_d)
            msg, before, after, d_before, d_after = lax.optimization_barrier(
                (msg, before, after, d_before, d_after)
            )
    second_f = first_d * before + first_f
    first_a = last_d * after + last_a
    mine_f, mine_a = jnp.where(late, second_f, before), jnp.where(late, after, first_a)
    sent = jnp.concatenate(
        [jnp.where(late, before, second_f), jnp.where(late, first_a, after)], axis=0
    )
    got = lax.ppermute(sent, "tm", pairs)
    got_f, got_a = got[:half], got[half:]
    before = jnp.concatenate(
        [jnp.where(late, got_f, mine_f), jnp.where(late, mine_f, got_f)], axis=0
    )
    after = jnp.concatenate(
        [jnp.where(late, got_a, mine_a), jnp.where(late, mine_a, got_a)], axis=0
    )
    return before, after


class KernelParts:
    def __init__(self, split, gains, sums, modes, counts, params):
        self.split, self.gains, self.sums = split, gains, sums
        self.modes, self.counts, self.params = modes, counts, params
        self.kf, self.ka = [], []

    def gate(self, part, sent):
        if part >= 0:
            sent, self.gains = lax.optimization_barrier((sent, self.gains))
        return sent

    def __call__(self, part, got):
        if part < 0:
            return got
        length = self.counts[part] * CHUNK * (CHUNK // self.modes)
        whole = pl.BlockSpec(memory_space=pltpu.VMEM)
        kf, ka = pl.pallas_call(
            functools.partial(kernels_kernel, self.modes, sum(self.counts[:part])),
            name="kernels",
            in_specs=[whole] * 3,
            out_specs=[whole] * 2,
            out_shape=[pltpu.VMEM((length, CHUNK), BF16)] * 2,
            compiler_params=self.params,
            cost_estimate=pl.CostEstimate(
                flops=20 * length * CHUNK * CHUNK, bytes_accessed=8 << 20, transcendentals=0
            ),
        )(on_vmem(self.split), on_vmem(self.gains), on_vmem(self.sums))
        got, kf, ka = lax.optimization_barrier((got, kf, ka))
        self.kf.append(kf)
        self.ka.append(ka)
        return got


def body(currents, seed_on_tension, mode_diffusivity_factor, decay_rates, fit_weights, counts):
    samples, wires = currents.shape
    modes = decay_rates.shape[0]
    devices = lax.axis_size("tm")
    chunks = samples // CHUNK
    reps = wires // CHUNK
    me = lax.axis_index("tm")
    uppers = tuple((me & hop) != 0 for hop in hops_of(devices))
    rates, uppers = lax.optimization_barrier((decay_rates.reshape(1, modes), uppers))
    fits = fit_weights.reshape(1, modes)
    counts = counts.reshape(1, wires)
    params = pltpu.CompilerParams(vmem_limit_bytes=16 << 20)
    apart = pl.BlockSpec(memory_space=pl.ANY)
    whole = pl.BlockSpec(memory_space=pltpu.VMEM)
    flops = 2 * samples * wires
    copies = len(pieces_of(chunks))

    cur, fresh_f, fresh_a, decay, msg, split, start, back, gains, sums = pl.pallas_call(
        totals_kernel,
        name="totals",
        in_specs=[apart] * 5,
        out_specs=[whole] * 10,
        out_shape=[
            pltpu.VMEM((samples, wires), BF16),
            pltpu.VMEM((chunks * modes, wires), F32),
            pltpu.VMEM((chunks * modes, wires), BF16),
            pltpu.VMEM((chunks * modes, CHUNK), F32),
            pltpu.VMEM((2 * reps + 1, modes, CHUNK), F32),
            pltpu.VMEM((chunks * modes, 2 * CHUNK), BF16),
            pltpu.VMEM((chunks * modes, CHUNK), BF16),
            pltpu.VMEM((chunks * modes, CHUNK), BF16),
            pltpu.VMEM((CHUNK, CHUNK), F32),
            pltpu.VMEM((CHUNK, LEVELS * CHUNK), BF16),
        ],
        scratch_shapes=[
            pltpu.VMEM((samples, wires), BF16),
            pltpu.VMEM((modes, samples), F32),
            pltpu.VMEM((1, modes), F32),
            pltpu.VMEM((1, modes), F32),
            pltpu.SemaphoreType.DMA((3,)),
            pltpu.SemaphoreType.DMA((copies,)),
            pltpu.SemaphoreType.DMA((copies,)),
        ],
        compiler_params=params,
        cost_estimate=pl.CostEstimate(
            flops=2 * modes * flops, bytes_accessed=14 << 20, transcendentals=0
        ),
    )(
        on_hbm(mode_diffusivity_factor),
        on_hbm(rates),
        on_hbm(fits),
        on_hbm(currents),
        on_hbm(seed_on_tension),
    )

    groups = chunks * modes // CHUNK
    parts = 3
    shares = [groups * (k + 1) // parts - groups * k // parts for k in range(parts)]
    covered = KernelParts(split, gains, sums, modes, shares, params)
    before, after = scan_devices(msg, uppers, reps, covered, parts)

    tension, lse = pl.pallas_call(
        stress_kernel,
        name="stress",
        in_specs=[whole] * (6 + parts),
        out_specs=[apart, whole],
        out_shape=[
            pltpu.HBM((samples, wires), BF16),
            pltpu.HBM((devices, 1, wires), F32),
        ],
        scratch_shapes=[pltpu.VMEM((samples, wires), BF16), pltpu.SemaphoreType.DMA((copies,))],
        compiler_params=params,
        cost_estimate=pl.CostEstimate(
            flops=2 * CHUNK * flops, bytes_accessed=10 << 20, transcendentals=0
        ),
    )(*map(on_vmem, (cur, start, fresh_f, decay, before, counts, *covered.kf)))

    all_lse = lax.all_to_all(lse, "tm", 0, 0, tiled=True)

    gradient = pl.pallas_call(
        adjoint_kernel,
        name="adjoint",
        in_specs=[apart] + [whole] * (5 + parts),
        out_specs=apart,
        out_shape=pltpu.HBM((samples, wires), BF16),
        scratch_shapes=[
            pltpu.VMEM((samples, wires), BF16),
            pltpu.VMEM((samples, wires), BF16),
            pltpu.SemaphoreType.DMA((copies,)),
            pltpu.SemaphoreType.DMA((copies,)),
        ],
        compiler_params=params,
        cost_estimate=pl.CostEstimate(
            flops=2 * CHUNK * flops, bytes_accessed=10 << 20, transcendentals=0
        ),
    )(
        on_hbm(seed_on_tension),
        *map(on_vmem, (back, fresh_a, decay, after, counts, *covered.ka)),
    )

    top = jnp.max(all_lse, axis=0)
    total = jnp.sum(jnp.exp2(all_lse - top[None]), axis=0)
    softened = ((top * LN2 + jnp.log(total)) / SHARPNESS).reshape(wires)
    return (tension, gradient, softened)


def solution(mesh):
    placed = (P("tm", "parts"), P("tm", "parts"), P(None, ("parts", "tm")), P(), P(), P("parts"))
    return jax.shard_map(
        body,
        mesh=mesh,
        in_specs=placed,
        out_specs=(P("tm", "parts"), P("tm", "parts"), P("parts")),
        check_vma=False,
    )
```

```python
import functools
import math

import jax
import jax.numpy as jnp
from jax import lax
from jax.experimental import pallas as pl
from jax.experimental.pallas import tpu as pltpu
from jax.sharding import PartitionSpec as P

CHUNK = 128
LEVELS = 7
SHARPNESS = 4.0
LOG2E = math.log2(math.e)
LN2 = math.log(2.0)
F32 = jnp.float32
BF16 = jnp.bfloat16


def as_column(row):
    m = row.shape[1]
    r = lax.broadcasted_iota(jnp.int32, (m, m), 0)
    c = lax.broadcasted_iota(jnp.int32, (m, m), 1)
    return jnp.sum(jnp.where(r == c, jnp.broadcast_to(row, (m, m)), 0.0), axis=1, keepdims=True)


def rates_and_gains(rates_ref, fit_ref):
    rates = as_column(rates_ref[...])
    gains = as_column(fit_ref[...]) * jnp.sqrt(rates)
    return rates * LOG2E, gains


def level_sums():
    v = lax.broadcasted_iota(jnp.int32, (CHUNK, CHUNK), 0)
    u = lax.broadcasted_iota(jnp.int32, (CHUNK, CHUNK), 1)
    apart = v ^ u
    tables = []
    for level in range(LEVELS):
        half = 1 << level
        near = apart < half
        inside = jnp.where((u & half) != 0, jnp.where(v <= u, -1.0, 0.0), jnp.where(v > u, -1.0, 0.0))
        tables.append(jnp.where(near, inside, 0.0).astype(BF16))
    return jnp.concatenate(tables, axis=1)


def wide(a, times):
    return jnp.concatenate([a] * times, axis=1)


def stacked(heat_ref, speed, first, count):
    return jnp.concatenate(
        [
            heat_ref[:, c * CHUNK : (c + 1) * CHUNK] * speed
            for c in range(first, first + count)
        ],
        axis=0,
    )


def group_of(chunks, most):
    return max(g for g in range(1, most + 1) if chunks % g == 0)


def pieces_of(chunks):
    if chunks % 8:
        return [1] * chunks
    unit = chunks // 8
    return [3 * unit, 2 * unit, 2 * unit, unit]


def prefixes(heat):
    high = heat.astype(BF16)
    rest = heat - high.astype(F32)
    middle = rest.astype(BF16)
    low = (rest - middle.astype(F32)).astype(BF16)
    v = lax.broadcasted_iota(jnp.int32, (CHUNK, CHUNK), 0)
    u = lax.broadcasted_iota(jnp.int32, (CHUNK, CHUNK), 1)
    ones = jnp.concatenate(
        [jnp.where(v <= u, 1.0, 0.0).astype(BF16), jnp.where(v > u, 1.0, 0.0).astype(BF16)],
        axis=1,
    )
    both = jnp.dot(
        jnp.concatenate([high, middle, low], axis=1),
        jnp.concatenate([ones] * 3, axis=0),
        preferred_element_type=F32,
    )
    return both[:, :CHUNK], both[:, CHUNK:], jnp.concatenate([high, middle], axis=1)


def totals_kernel(
    heat_hbm, rates_hbm, fits_hbm, cur_hbm, cot_hbm,
    cur_ref, fresh_f_ref, fresh_a_ref, decay_ref, msg_ref,
    split_ref, start_ref, back_ref, gains_ref, sums_ref,
    cot_ref, heat_ref, rates_ref, fits_ref, small_sem, cur_sem, cot_sem,
):
    modes = heat_ref.shape[0]
    samples, wires = cur_ref.shape
    reps = wires // CHUNK
    chunks = samples // CHUNK
    group = group_of(chunks, 3)

    small = [
        pltpu.make_async_copy(heat_hbm, heat_ref, small_sem.at[0]),
        pltpu.make_async_copy(rates_hbm, rates_ref, small_sem.at[1]),
        pltpu.make_async_copy(fits_hbm, fits_ref, small_sem.at[2]),
    ]
    for copy in small:
        copy.start()
    loads = []
    at = 0
    for k, piece in enumerate(pieces_of(chunks)):
        rows = pl.ds(at * CHUNK, piece * CHUNK)
        pair = (
            pltpu.make_async_copy(cur_hbm.at[rows], cur_ref.at[rows], cur_sem.at[k]),
            pltpu.make_async_copy(cot_hbm.at[rows], cot_ref.at[rows], cot_sem.at[k]),
        )
        for copy in pair:
            copy.start()
        loads.append((at, piece, pair))
        at += piece
    sums_ref[...] = level_sums()
    for copy in small:
        copy.wait()

    speed, gains = rates_and_gains(rates_ref, fits_ref)
    gain_stack = jnp.concatenate([gains] * group, axis=0)
    gains_ref[...] = jnp.broadcast_to(
        jnp.concatenate([gains] * (CHUNK // modes), axis=0), gains_ref.shape
    )
    for first in range(0, chunks, group):
        rows = slice(first * modes, (first + group) * modes)
        pre, suf, split = prefixes(stacked(heat_ref, speed, first, group))
        split_ref[rows, :] = split
        start_ref[rows, :] = (gain_stack * jnp.exp2(-pre)).astype(BF16)
        back_ref[rows, :] = jnp.exp2(-suf).astype(BF16)
        decay_ref[rows, :] = jnp.exp2(-(pre + suf))

    tf = jnp.zeros((modes, wires), F32)
    ta = jnp.zeros((modes, wires), F32)
    dc = jnp.ones((modes, CHUNK), F32)
    for first, piece, pair in loads:
        for copy in pair:
            copy.wait()
        for c in range(first, first + piece):
            span = slice(c * CHUNK, (c + 1) * CHUNK)
            rows = slice(c * modes, (c + 1) * modes)
            decay = decay_ref[rows, :]
            fresh_f = jnp.dot(back_ref[rows, :], cur_ref[span, :], preferred_element_type=F32)
            fresh_a = jnp.dot(start_ref[rows, :], cot_ref[span, :], preferred_element_type=F32)
            fresh_f_ref[rows, :] = fresh_f
            fresh_a_ref[rows, :] = fresh_a.astype(BF16)
            tf = wide(decay, reps) * tf + fresh_f
            ta = ta + wide(dc, reps) * fresh_a
            dc = dc * decay
    for k in range(reps):
        lanes = slice(k * CHUNK, (k + 1) * CHUNK)
        msg_ref[k] = tf[:, lanes]
        msg_ref[reps + k] = ta[:, lanes]
    msg_ref[2 * reps] = dc


def kernels_kernel(modes, first, split_ref, gains_ref, sums_ref, kf_ref, ka_ref):
    group = CHUNK // modes
    t = lax.broadcasted_iota(jnp.int32, (CHUNK, CHUNK), 0)
    s = lax.broadcasted_iota(jnp.int32, (CHUNK, CHUNK), 1)
    apart = jnp.where(t >= s, t ^ s, -1)
    gains = gains_ref[...]
    gain_sum = jnp.sum(gains[:modes], axis=0, keepdims=True)
    base = jnp.where(apart == 0, jnp.broadcast_to(gain_sum, (CHUNK, CHUNK)), 0.0)
    for g in range(kf_ref.shape[0] // (CHUNK * group)):
        rows = slice((first + g) * CHUNK, (first + g + 1) * CHUNK)
        sums = jnp.dot(
            split_ref[rows, :],
            jnp.concatenate([sums_ref[...]] * 2, axis=0),
            preferred_element_type=F32,
        )
        kernels = [base] * group
        for level in range(LEVELS):
            table = jnp.exp2(sums[:, level * CHUNK : (level + 1) * CHUNK])
            left = (gains * table).astype(BF16).T
            right = table.astype(BF16)
            columns = []
            for c in range(group):
                parts = []
                if c > 0:
                    parts.append(jnp.zeros((c * modes, CHUNK), BF16))
                parts.append(right[c * modes : (c + 1) * modes])
                if c + 1 < group:
                    parts.append(jnp.zeros(((group - 1 - c) * modes, CHUNK), BF16))
                columns.append(jnp.concatenate(parts, axis=0))
            both = jnp.dot(left, jnp.concatenate(columns, axis=1), preferred_element_type=F32)
            keep = apart >= (1 << level)
            kernels = [
                jnp.where(keep, both[:, c * CHUNK : (c + 1) * CHUNK], kernels[c])
                for c in range(group)
            ]
        for c in range(group):
            span = slice((g * group + c) * CHUNK, (g * group + c + 1) * CHUNK)
            kernel = kernels[c].astype(BF16)
            kf_ref[span, :] = kernel
            ka_ref[span, :] = kernel.T


def carry(table, state):
    return lax.dot_general(
        table, state, (((0,), (0,)), ((), ())), preferred_element_type=F32
    )


def part_of(refs, c):
    for ref in refs:
        chunks = ref.shape[0] // CHUNK
        if c < chunks:
            return ref[c * CHUNK : (c + 1) * CHUNK, :]
        c -= chunks


def stress_pieces(chunks):
    if chunks % 8:
        return [1] * chunks
    unit = chunks // 8
    return [2 * unit, 2 * unit, unit, unit, 2 * unit]


def stress_kernel(
    cur_ref, start_ref, fresh_ref, decay_ref, in_ref, counts_ref, *refs
):
    kf_refs = refs[:-5]
    out_hbm, tail_ref, lse_ref, out_ref, sem = refs[-5:]
    samples, wires = cur_ref.shape
    reps = wires // CHUNK
    modes = in_ref.shape[1]
    scale = counts_ref[...].astype(F32) * 0.25
    scale2 = scale * (SHARPNESS * LOG2E)
    state = jnp.concatenate([in_ref[k] for k in range(reps)], axis=1)
    high = jnp.full((8, wires), -1e30, F32)
    amount = jnp.zeros((8, wires), F32)
    stores = []
    first = 0
    pieces = stress_pieces(samples // CHUNK)
    for k, piece in enumerate(pieces):
        last = k == len(pieces) - 1
        for c in range(first, first + piece):
            span = slice(c * CHUNK, (c + 1) * CHUNK)
            rows = slice(c * modes, (c + 1) * modes)
            acc = jnp.dot(part_of(kf_refs, c), cur_ref[span, :], preferred_element_type=F32)
            acc = acc + carry(start_ref[rows, :], state.astype(BF16))
            stress = (acc * scale).astype(BF16)
            if last:
                tail_ref[(c - first) * CHUNK : (c - first + 1) * CHUNK, :] = stress
            else:
                out_ref[span, :] = stress
            z = (acc * scale2).reshape(CHUNK // 8, 8, wires)
            new = jnp.maximum(high, jnp.max(z, axis=0))
            amount = amount * jnp.exp2(high - new) + jnp.sum(jnp.exp2(z - new[None]), axis=0)
            high = new
            state = wide(decay_ref[rows, :], reps) * state + fresh_ref[rows, :]
        if not last:
            done = pl.ds(first * CHUNK, piece * CHUNK)
            copy = pltpu.make_async_copy(out_ref.at[done], out_hbm.at[done], sem.at[k])
            copy.start()
            stores.append(copy)
        first += piece
    top = jnp.max(high, axis=0, keepdims=True)
    total = jnp.sum(amount * jnp.exp2(high - top), axis=0, keepdims=True)
    value = top + jnp.log(total) * LOG2E
    lse_ref[...] = jnp.broadcast_to(value[None], lse_ref.shape)
    for copy in stores:
        copy.wait()


def adjoint_kernel(
    cot_hbm, early_hbm, tail_ref, back_ref, fresh_ref, decay_ref, in_ref, counts_ref, *refs
):
    ka_refs = refs[:-7]
    out_hbm, stress_hbm, cot_ref, out_ref, load_sem, sem, tail_sem = refs[-7:]
    samples, wires = cot_ref.shape
    reps = wires // CHUNK
    chunks = samples // CHUNK
    modes = in_ref.shape[1]
    scale = counts_ref[...].astype(F32) * 0.25
    state = jnp.concatenate([in_ref[k] for k in range(reps)], axis=1)
    loads = []
    end = chunks
    for k, piece in enumerate(pieces_of(chunks)):
        rows = pl.ds((end - piece) * CHUNK, piece * CHUNK)
        copy = pltpu.make_async_copy(cot_hbm.at[rows], cot_ref.at[rows], load_sem.at[k])
        copy.start()
        loads.append(copy)
        end -= piece
    tail = tail_ref.shape[0]
    copy = pltpu.make_async_copy(tail_ref, stress_hbm.at[pl.ds(samples - tail, tail)], tail_sem)
    copy.start()
    stores = [copy]
    end = chunks
    for k, piece in enumerate(pieces_of(chunks)):
        loads[k].wait()
        for c in reversed(range(end - piece, end)):
            span = slice(c * CHUNK, (c + 1) * CHUNK)
            rows = slice(c * modes, (c + 1) * modes)
            acc = jnp.dot(part_of(ka_refs, c), cot_ref[span, :], preferred_element_type=F32)
            acc = acc + carry(back_ref[rows, :], state.astype(BF16))
            out_ref[span, :] = (acc * scale).astype(BF16)
            state = wide(decay_ref[rows, :], reps) * state + fresh_ref[rows, :].astype(F32)
        done = pl.ds((end - piece) * CHUNK, piece * CHUNK)
        copy = pltpu.make_async_copy(out_ref.at[done], out_hbm.at[done], sem.at[k])
        copy.start()
        stores.append(copy)
        end -= piece
    for copy in stores:
        copy.wait()


def on_vmem(a):
    return pltpu.with_memory_space_constraint(a, pltpu.VMEM)


def on_hbm(a):
    return pltpu.with_memory_space_constraint(a, pltpu.HBM)


def hops_of(n):
    return [1 << k for k in range(n.bit_length() - 1)]


def scan_devices(msg, uppers, reps, run_part, parts):
    n = lax.axis_size("tm")
    half = reps // 2
    hops = hops_of(n)
    late = uppers[0]
    pairs = [(i, i ^ 1) for i in range(n)]

    low_f, high_f = msg[:half], msg[half:reps]
    low_a, high_a = msg[reps : reps + half], msg[reps + half : 2 * reps]
    mine_d = msg[2 * reps :]
    sent = jnp.concatenate(
        [jnp.where(late, low_f, high_f), jnp.where(late, low_a, high_a), mine_d], axis=0
    )
    mine_f, mine_a = jnp.where(late, high_f, low_f), jnp.where(late, high_a, low_a)
    got = lax.ppermute(sent, "tm", pairs)
    got_f, got_a, got_d = got[:half], got[half : 2 * half], got[2 * half :]
    first_f, last_a = jnp.where(late, got_f, mine_f), jnp.where(late, mine_a, got_a)
    first_d, last_d = jnp.where(late, got_d, mine_d), jnp.where(late, mine_d, got_d)
    msg = jnp.concatenate(
        [
            last_d * first_f + jnp.where(late, mine_f, got_f),
            jnp.where(late, got_a, mine_a) + first_d * last_a,
            mine_d * got_d,
        ],
        axis=0,
    )
    before = jnp.zeros_like(mine_f)
    after = jnp.zeros_like(mine_f)
    d_before = jnp.ones_like(mine_d)
    d_after = jnp.ones_like(mine_d)
    msg, first_f, last_a, first_d, last_d = lax.optimization_barrier(
        (msg, first_f, last_a, first_d, last_d)
    )
    for index, hop in list(enumerate(hops))[1:-2]:
        upper = uppers[index]
        mine_f, mine_a, mine_d = msg[:half], msg[half : 2 * half], msg[2 * half :]
        part = index - len(hops) + 2 + parts - 1
        msg = run_part.gate(part, msg)
        got = lax.ppermute(msg, "tm", [(i, i ^ hop) for i in range(n)])
        got = run_part(part, got)
        got_f, got_a, got_d = got[:half], got[half : 2 * half], got[2 * half :]
        next_f = jnp.where(upper, mine_d * got_f + mine_f, got_d * mine_f + got_f)
        next_a = jnp.where(upper, got_d * mine_a + got_a, mine_d * got_a + mine_a)
        msg = jnp.concatenate([next_f, next_a, mine_d * got_d], axis=0)
        before = jnp.where(upper, d_before * got_f + before, before)
        after = jnp.where(upper, after, d_after * got_a + after)
        d_before = jnp.where(upper, d_before * got_d, d_before)
        d_after = jnp.where(upper, d_after, d_after * got_d)
        msg, before, after, d_before, d_after = lax.optimization_barrier(
            (msg, before, after, d_before, d_after)
        )
    near, far = uppers[-2], uppers[-1]
    mine_f, mine_a, mine_d = msg[:half], msg[half : 2 * half], msg[2 * half :]
    to_near = jnp.concatenate([jnp.where(near, mine_a, mine_f), mine_d], axis=0)
    to_far = jnp.concatenate([jnp.where(far, mine_a, mine_f), mine_d], axis=0)
    to_near, to_far = lax.optimization_barrier((to_near, to_far))
    to_near = run_part.gate(parts - 1, to_near)
    quarter = hops[-2]
    got = [
        lax.ppermute(sent, "tm", [(i, i ^ hop) for i in range(n)])
        for sent, hop in ((to_far, 2 * quarter), (to_near, quarter), (to_far, 3 * quarter))
    ]
    got = run_part(parts - 1, tuple(got))
    (x2, d2), (x1, d1), (x3, d3) = [(g[:half], g[half:]) for g in got]
    others_f = jnp.where(
        far,
        jnp.where(near, (x3 * d2 + x2) * d1 + x1, d3 * x2 + x3),
        jnp.where(near, x1, 0.0),
    )
    others_a = jnp.where(
        far,
        jnp.where(near, 0.0, x1),
        jnp.where(near, x3 + d3 * x2, x1 + d1 * (x2 + d2 * x3)),
    )
    before = d_before * others_f + before
    after = d_after * others_a + after
    second_f = first_d * before + first_f
    first_a = last_d * after + last_a
    mine_f, mine_a = jnp.where(late, second_f, before), jnp.where(late, after, first_a)
    sent = jnp.concatenate(
        [jnp.where(late, before, second_f), jnp.where(late, first_a, after)], axis=0
    )
    got = lax.ppermute(sent, "tm", pairs)
    got_f, got_a = got[:half], got[half:]
    before = jnp.concatenate(
        [jnp.where(late, got_f, mine_f), jnp.where(late, mine_f, got_f)], axis=0
    )
    after = jnp.concatenate(
        [jnp.where(late, got_a, mine_a), jnp.where(late, mine_a, got_a)], axis=0
    )
    return before, after


class KernelParts:
    def __init__(self, split, gains, sums, modes, counts, params):
        self.split, self.gains, self.sums = split, gains, sums
        self.modes, self.counts, self.params = modes, counts, params
        self.kf, self.ka = [], []

    def gate(self, part, sent):
        if part >= 0:
            sent, self.gains = lax.optimization_barrier((sent, self.gains))
        return sent

    def __call__(self, part, got):
        if part < 0:
            return got
        length = self.counts[part] * CHUNK * (CHUNK // self.modes)
        whole = pl.BlockSpec(memory_space=pltpu.VMEM)
        kf, ka = pl.pallas_call(
            functools.partial(kernels_kernel, self.modes, sum(self.counts[:part])),
            name="kernels",
            in_specs=[whole] * 3,
            out_specs=[whole] * 2,
            out_shape=[pltpu.VMEM((length, CHUNK), BF16)] * 2,
            compiler_params=self.params,
            cost_estimate=pl.CostEstimate(
                flops=20 * length * CHUNK * CHUNK, bytes_accessed=8 << 20, transcendentals=0
            ),
        )(on_vmem(self.split), on_vmem(self.gains), on_vmem(self.sums))
        got, kf, ka = lax.optimization_barrier((got, kf, ka))
        self.kf.append(kf)
        self.ka.append(ka)
        return got


def body(currents, seed_on_tension, mode_diffusivity_factor, decay_rates, fit_weights, counts):
    samples, wires = currents.shape
    modes = decay_rates.shape[0]
    devices = lax.axis_size("tm")
    chunks = samples // CHUNK
    reps = wires // CHUNK
    me = lax.axis_index("tm")
    uppers = tuple((me & hop) != 0 for hop in hops_of(devices))
    rates, uppers = lax.optimization_barrier((decay_rates.reshape(1, modes), uppers))
    fits = fit_weights.reshape(1, modes)
    counts = counts.reshape(1, wires)
    params = pltpu.CompilerParams(vmem_limit_bytes=16 << 20)
    apart = pl.BlockSpec(memory_space=pl.ANY)
    whole = pl.BlockSpec(memory_space=pltpu.VMEM)
    flops = 2 * samples * wires
    copies = len(pieces_of(chunks))

    cur, fresh_f, fresh_a, decay, msg, split, start, back, gains, sums = pl.pallas_call(
        totals_kernel,
        name="totals",
        in_specs=[apart] * 5,
        out_specs=[whole] * 10,
        out_shape=[
            pltpu.VMEM((samples, wires), BF16),
            pltpu.VMEM((chunks * modes, wires), F32),
            pltpu.VMEM((chunks * modes, wires), BF16),
            pltpu.VMEM((chunks * modes, CHUNK), F32),
            pltpu.VMEM((2 * reps + 1, modes, CHUNK), F32),
            pltpu.VMEM((chunks * modes, 2 * CHUNK), BF16),
            pltpu.VMEM((chunks * modes, CHUNK), BF16),
            pltpu.VMEM((chunks * modes, CHUNK), BF16),
            pltpu.VMEM((CHUNK, CHUNK), F32),
            pltpu.VMEM((CHUNK, LEVELS * CHUNK), BF16),
        ],
        scratch_shapes=[
            pltpu.VMEM((samples, wires), BF16),
            pltpu.VMEM((modes, samples), F32),
            pltpu.VMEM((1, modes), F32),
            pltpu.VMEM((1, modes), F32),
            pltpu.SemaphoreType.DMA((3,)),
            pltpu.SemaphoreType.DMA((copies,)),
            pltpu.SemaphoreType.DMA((copies,)),
        ],
        compiler_params=params,
        cost_estimate=pl.CostEstimate(
            flops=2 * modes * flops, bytes_accessed=14 << 20, transcendentals=0
        ),
    )(
        on_hbm(mode_diffusivity_factor),
        on_hbm(rates),
        on_hbm(fits),
        on_hbm(currents),
        on_hbm(seed_on_tension),
    )

    groups = chunks * modes // CHUNK
    parts = 2
    shares = [groups - groups // 3, groups // 3]
    covered = KernelParts(split, gains, sums, modes, shares, params)
    before, after = scan_devices(msg, uppers, reps, covered, parts)

    pieces = stress_pieces(chunks)
    early, tail, lse = pl.pallas_call(
        stress_kernel,
        name="stress",
        in_specs=[whole] * (6 + parts),
        out_specs=[apart, whole, whole],
        out_shape=[
            pltpu.HBM((samples, wires), BF16),
            pltpu.VMEM((pieces[-1] * CHUNK, wires), BF16),
            pltpu.HBM((devices, 1, wires), F32),
        ],
        scratch_shapes=[pltpu.VMEM((samples, wires), BF16), pltpu.SemaphoreType.DMA((len(pieces),))],
        compiler_params=params,
        cost_estimate=pl.CostEstimate(
            flops=2 * CHUNK * flops, bytes_accessed=10 << 20, transcendentals=0
        ),
    )(*map(on_vmem, (cur, start, fresh_f, decay, before, counts, *covered.kf)))

    all_lse = lax.all_to_all(lse, "tm", 0, 0, tiled=True)

    gradient, tension = pl.pallas_call(
        adjoint_kernel,
        name="adjoint",
        in_specs=[apart] * 2 + [whole] * (6 + parts),
        out_specs=[apart] * 2,
        out_shape=[pltpu.HBM((samples, wires), BF16)] * 2,
        input_output_aliases={1: 1},
        scratch_shapes=[
            pltpu.VMEM((samples, wires), BF16),
            pltpu.VMEM((samples, wires), BF16),
            pltpu.SemaphoreType.DMA((copies,)),
            pltpu.SemaphoreType.DMA((copies,)),
            pltpu.SemaphoreType.DMA,
        ],
        compiler_params=params,
        cost_estimate=pl.CostEstimate(
            flops=2 * CHUNK * flops, bytes_accessed=10 << 20, transcendentals=0
        ),
    )(
        on_hbm(seed_on_tension),
        on_hbm(early),
        on_vmem(tail),
        *map(on_vmem, (back, fresh_a, decay, after, counts, *covered.ka)),
    )

    top = jnp.max(all_lse, axis=0)
    total = jnp.sum(jnp.exp2(all_lse - top[None]), axis=0)
    softened = ((top * LN2 + jnp.log(total)) / SHARPNESS).reshape(wires)
    return (tension, gradient, softened)


def solution(mesh):
    placed = (P("tm", "parts"), P("tm", "parts"), P(None, ("parts", "tm")), P(), P(), P("parts"))
    return jax.shard_map(
        body,
        mesh=mesh,
        in_specs=placed,
        out_specs=(P("tm", "parts"), P("tm", "parts"), P("parts")),
        check_vma=False,
    )
```

```python
import functools
import math

import jax
import jax.numpy as jnp
from jax import lax
from jax.experimental import pallas as pl
from jax.experimental.pallas import tpu as pltpu
from jax.sharding import PartitionSpec as P

CHUNK = 128
LEVELS = 7
SHARPNESS = 4.0
LOG2E = math.log2(math.e)
LN2 = math.log(2.0)
F32 = jnp.float32
BF16 = jnp.bfloat16


def as_column(row):
    m = row.shape[1]
    r = lax.broadcasted_iota(jnp.int32, (m, m), 0)
    c = lax.broadcasted_iota(jnp.int32, (m, m), 1)
    return jnp.sum(jnp.where(r == c, jnp.broadcast_to(row, (m, m)), 0.0), axis=1, keepdims=True)


def rates_and_gains(rates_ref, fit_ref):
    rates = as_column(rates_ref[...])
    gains = as_column(fit_ref[...]) * jnp.sqrt(rates)
    return rates * LOG2E, gains


def level_sums():
    v = lax.broadcasted_iota(jnp.int32, (CHUNK, CHUNK), 0)
    u = lax.broadcasted_iota(jnp.int32, (CHUNK, CHUNK), 1)
    apart = v ^ u
    tables = []
    for level in range(LEVELS):
        half = 1 << level
        near = apart < half
        inside = jnp.where((u & half) != 0, jnp.where(v <= u, -1.0, 0.0), jnp.where(v > u, -1.0, 0.0))
        tables.append(jnp.where(near, inside, 0.0).astype(BF16))
    return jnp.concatenate(tables, axis=1)


def wide(a, times):
    return jnp.concatenate([a] * times, axis=1)


def stacked(heat_ref, speed, first, count):
    return jnp.concatenate(
        [
            heat_ref[:, c * CHUNK : (c + 1) * CHUNK] * speed
            for c in range(first, first + count)
        ],
        axis=0,
    )


def group_of(chunks, most):
    return max(g for g in range(1, most + 1) if chunks % g == 0)


def pieces_of(chunks):
    if chunks % 8:
        return [1] * chunks
    unit = chunks // 8
    return [3 * unit, 2 * unit, 2 * unit, unit]


def prefixes(heat):
    high = heat.astype(BF16)
    rest = heat - high.astype(F32)
    middle = rest.astype(BF16)
    low = (rest - middle.astype(F32)).astype(BF16)
    v = lax.broadcasted_iota(jnp.int32, (CHUNK, CHUNK), 0)
    u = lax.broadcasted_iota(jnp.int32, (CHUNK, CHUNK), 1)
    ones = jnp.concatenate(
        [jnp.where(v <= u, 1.0, 0.0).astype(BF16), jnp.where(v > u, 1.0, 0.0).astype(BF16)],
        axis=1,
    )
    both = jnp.dot(
        jnp.concatenate([high, middle, low], axis=1),
        jnp.concatenate([ones] * 3, axis=0),
        preferred_element_type=F32,
    )
    return both[:, :CHUNK], both[:, CHUNK:], jnp.concatenate([high, middle], axis=1)


def totals_kernel(
    heat_hbm, rates_hbm, fits_hbm, cur_hbm, cot_hbm,
    cur_ref, fresh_f_ref, fresh_a_ref, decay_ref, msg_ref,
    split_ref, start_ref, back_ref, gains_ref, sums_ref,
    cot_ref, heat_ref, rates_ref, fits_ref, small_sem, cur_sem, cot_sem,
):
    modes = heat_ref.shape[0]
    samples, wires = cur_ref.shape
    reps = wires // CHUNK
    chunks = samples // CHUNK
    group = group_of(chunks, 3)

    small = [
        pltpu.make_async_copy(heat_hbm, heat_ref, small_sem.at[0]),
        pltpu.make_async_copy(rates_hbm, rates_ref, small_sem.at[1]),
        pltpu.make_async_copy(fits_hbm, fits_ref, small_sem.at[2]),
    ]
    for copy in small:
        copy.start()
    load_cur = pltpu.make_async_copy(cur_hbm, cur_ref, cur_sem)
    load_cot = pltpu.make_async_copy(cot_hbm, cot_ref, cot_sem)
    load_cur.start()
    load_cot.start()
    sums_ref[...] = level_sums()
    for copy in small:
        copy.wait()

    speed, gains = rates_and_gains(rates_ref, fits_ref)
    gain_stack = jnp.concatenate([gains] * group, axis=0)
    gains_ref[...] = jnp.broadcast_to(
        jnp.concatenate([gains] * (CHUNK // modes), axis=0), gains_ref.shape
    )
    for first in range(0, chunks, group):
        rows = slice(first * modes, (first + group) * modes)
        pre, suf, split = prefixes(stacked(heat_ref, speed, first, group))
        split_ref[rows, :] = split
        start_ref[rows, :] = (gain_stack * jnp.exp2(-pre)).astype(BF16)
        back_ref[rows, :] = jnp.exp2(-suf).astype(BF16)
        decay_ref[rows, :] = jnp.exp2(-(pre + suf))

    tf = jnp.zeros((modes, wires), F32)
    ta = jnp.zeros((modes, wires), F32)
    dc = jnp.ones((modes, CHUNK), F32)
    load_cur.wait()
    for c in range(chunks):
        span = slice(c * CHUNK, (c + 1) * CHUNK)
        rows = slice(c * modes, (c + 1) * modes)
        fresh_f = jnp.dot(back_ref[rows, :], cur_ref[span, :], preferred_element_type=F32)
        fresh_f_ref[rows, :] = fresh_f
        tf = wide(decay_ref[rows, :], reps) * tf + fresh_f
    load_cot.wait()
    for c in range(chunks):
        span = slice(c * CHUNK, (c + 1) * CHUNK)
        rows = slice(c * modes, (c + 1) * modes)
        fresh_a = jnp.dot(start_ref[rows, :], cot_ref[span, :], preferred_element_type=F32)
        fresh_a_ref[rows, :] = fresh_a.astype(BF16)
        ta = ta + wide(dc, reps) * fresh_a
        dc = dc * decay_ref[rows, :]
    for k in range(reps):
        lanes = slice(k * CHUNK, (k + 1) * CHUNK)
        msg_ref[k] = tf[:, lanes]
        msg_ref[reps + k] = ta[:, lanes]
    msg_ref[2 * reps] = dc


def kernels_kernel(modes, first, split_ref, gains_ref, sums_ref, kf_ref, ka_ref):
    group = CHUNK // modes
    t = lax.broadcasted_iota(jnp.int32, (CHUNK, CHUNK), 0)
    s = lax.broadcasted_iota(jnp.int32, (CHUNK, CHUNK), 1)
    apart = jnp.where(t >= s, t ^ s, -1)
    gains = gains_ref[...]
    gain_sum = jnp.sum(gains[:modes], axis=0, keepdims=True)
    base = jnp.where(apart == 0, jnp.broadcast_to(gain_sum, (CHUNK, CHUNK)), 0.0)
    for g in range(kf_ref.shape[0] // (CHUNK * group)):
        rows = slice((first + g) * CHUNK, (first + g + 1) * CHUNK)
        sums = jnp.dot(
            split_ref[rows, :],
            jnp.concatenate([sums_ref[...]] * 2, axis=0),
            preferred_element_type=F32,
        )
        kernels = [base] * group
        for level in range(LEVELS):
            table = jnp.exp2(sums[:, level * CHUNK : (level + 1) * CHUNK])
            left = (gains * table).astype(BF16).T
            right = table.astype(BF16)
            columns = []
            for c in range(group):
                parts = []
                if c > 0:
                    parts.append(jnp.zeros((c * modes, CHUNK), BF16))
                parts.append(right[c * modes : (c + 1) * modes])
                if c + 1 < group:
                    parts.append(jnp.zeros(((group - 1 - c) * modes, CHUNK), BF16))
                columns.append(jnp.concatenate(parts, axis=0))
            both = jnp.dot(left, jnp.concatenate(columns, axis=1), preferred_element_type=F32)
            keep = apart >= (1 << level)
            kernels = [
                jnp.where(keep, both[:, c * CHUNK : (c + 1) * CHUNK], kernels[c])
                for c in range(group)
            ]
        for c in range(group):
            span = slice((g * group + c) * CHUNK, (g * group + c + 1) * CHUNK)
            kernel = kernels[c].astype(BF16)
            kf_ref[span, :] = kernel
            ka_ref[span, :] = kernel.T


def carry(table, state):
    return lax.dot_general(
        table, state, (((0,), (0,)), ((), ())), preferred_element_type=F32
    )


def part_of(refs, c):
    for ref in refs:
        chunks = ref.shape[0] // CHUNK
        if c < chunks:
            return ref[c * CHUNK : (c + 1) * CHUNK, :]
        c -= chunks


def stress_pieces(chunks):
    if chunks % 8:
        return [1] * chunks
    unit = chunks // 8
    return [2 * unit, 2 * unit, unit, unit, 2 * unit]


def stress_kernel(
    cur_ref, start_ref, fresh_ref, decay_ref, in_ref, counts_ref, *refs
):
    kf_refs = refs[:-5]
    out_hbm, tail_ref, lse_ref, out_ref, sem = refs[-5:]
    samples, wires = cur_ref.shape
    reps = wires // CHUNK
    modes = in_ref.shape[1]
    scale = counts_ref[...].astype(F32) * 0.25
    scale2 = scale * (SHARPNESS * LOG2E)
    state = jnp.concatenate([in_ref[k] for k in range(reps)], axis=1)
    high = jnp.full((8, wires), -1e30, F32)
    amount = jnp.zeros((8, wires), F32)
    stores = []
    first = 0
    pieces = stress_pieces(samples // CHUNK)
    for k, piece in enumerate(pieces):
        last = k == len(pieces) - 1
        for c in range(first, first + piece):
            span = slice(c * CHUNK, (c + 1) * CHUNK)
            rows = slice(c * modes, (c + 1) * modes)
            acc = jnp.dot(part_of(kf_refs, c), cur_ref[span, :], preferred_element_type=F32)
            acc = acc + carry(start_ref[rows, :], state.astype(BF16))
            stress = (acc * scale).astype(BF16)
            if last:
                tail_ref[(c - first) * CHUNK : (c - first + 1) * CHUNK, :] = stress
            else:
                out_ref[span, :] = stress
            z = (acc * scale2).reshape(CHUNK // 8, 8, wires)
            new = jnp.maximum(high, jnp.max(z, axis=0))
            amount = amount * jnp.exp2(high - new) + jnp.sum(jnp.exp2(z - new[None]), axis=0)
            high = new
            state = wide(decay_ref[rows, :], reps) * state + fresh_ref[rows, :]
        if not last:
            done = pl.ds(first * CHUNK, piece * CHUNK)
            copy = pltpu.make_async_copy(out_ref.at[done], out_hbm.at[done], sem.at[k])
            copy.start()
            stores.append(copy)
        first += piece
    top = jnp.max(high, axis=0, keepdims=True)
    total = jnp.sum(amount * jnp.exp2(high - top), axis=0, keepdims=True)
    value = top + jnp.log(total) * LOG2E
    lse_ref[...] = jnp.broadcast_to(value[None], lse_ref.shape)
    for copy in stores:
        copy.wait()


def adjoint_kernel(
    cot_hbm, early_hbm, tail_ref, back_ref, fresh_ref, decay_ref, in_ref, counts_ref, *refs
):
    ka_refs = refs[:-7]
    out_hbm, stress_hbm, cot_ref, out_ref, load_sem, sem, tail_sem = refs[-7:]
    samples, wires = cot_ref.shape
    reps = wires // CHUNK
    chunks = samples // CHUNK
    modes = in_ref.shape[1]
    scale = counts_ref[...].astype(F32) * 0.25
    state = jnp.concatenate([in_ref[k] for k in range(reps)], axis=1)
    loads = []
    end = chunks
    for k, piece in enumerate(pieces_of(chunks)):
        rows = pl.ds((end - piece) * CHUNK, piece * CHUNK)
        copy = pltpu.make_async_copy(cot_hbm.at[rows], cot_ref.at[rows], load_sem.at[k])
        copy.start()
        loads.append(copy)
        end -= piece
    tail = tail_ref.shape[0]
    copy = pltpu.make_async_copy(tail_ref, stress_hbm.at[pl.ds(samples - tail, tail)], tail_sem)
    copy.start()
    stores = [copy]
    end = chunks
    for k, piece in enumerate(pieces_of(chunks)):
        loads[k].wait()
        for c in reversed(range(end - piece, end)):
            span = slice(c * CHUNK, (c + 1) * CHUNK)
            rows = slice(c * modes, (c + 1) * modes)
            acc = jnp.dot(part_of(ka_refs, c), cot_ref[span, :], preferred_element_type=F32)
            acc = acc + carry(back_ref[rows, :], state.astype(BF16))
            out_ref[span, :] = (acc * scale).astype(BF16)
            state = wide(decay_ref[rows, :], reps) * state + fresh_ref[rows, :].astype(F32)
        done = pl.ds((end - piece) * CHUNK, piece * CHUNK)
        copy = pltpu.make_async_copy(out_ref.at[done], out_hbm.at[done], sem.at[k])
        copy.start()
        stores.append(copy)
        end -= piece
    for copy in stores:
        copy.wait()


def on_vmem(a):
    return pltpu.with_memory_space_constraint(a, pltpu.VMEM)


def on_hbm(a):
    return pltpu.with_memory_space_constraint(a, pltpu.HBM)


def hops_of(n):
    return [1 << k for k in range(n.bit_length() - 1)]


def scan_devices(msg, uppers, reps, run_part, parts):
    n = lax.axis_size("tm")
    half = reps // 2
    hops = hops_of(n)
    late = uppers[0]
    pairs = [(i, i ^ 1) for i in range(n)]

    low_f, high_f = msg[:half], msg[half:reps]
    low_a, high_a = msg[reps : reps + half], msg[reps + half : 2 * reps]
    mine_d = msg[2 * reps :]
    sent = jnp.concatenate(
        [jnp.where(late, low_f, high_f), jnp.where(late, low_a, high_a), mine_d], axis=0
    )
    mine_f, mine_a = jnp.where(late, high_f, low_f), jnp.where(late, high_a, low_a)
    got = lax.ppermute(sent, "tm", pairs)
    got_f, got_a, got_d = got[:half], got[half : 2 * half], got[2 * half :]
    first_f, last_a = jnp.where(late, got_f, mine_f), jnp.where(late, mine_a, got_a)
    first_d, last_d = jnp.where(late, got_d, mine_d), jnp.where(late, mine_d, got_d)
    msg = jnp.concatenate(
        [
            last_d * first_f + jnp.where(late, mine_f, got_f),
            jnp.where(late, got_a, mine_a) + first_d * last_a,
            mine_d * got_d,
        ],
        axis=0,
    )
    before = jnp.zeros_like(mine_f)
    after = jnp.zeros_like(mine_f)
    d_before = jnp.ones_like(mine_d)
    d_after = jnp.ones_like(mine_d)
    msg, first_f, last_a, first_d, last_d = lax.optimization_barrier(
        (msg, first_f, last_a, first_d, last_d)
    )
    for index, hop in list(enumerate(hops))[1:-2]:
        upper = uppers[index]
        mine_f, mine_a, mine_d = msg[:half], msg[half : 2 * half], msg[2 * half :]
        part = index - len(hops) + 2 + parts - 1
        msg = run_part.gate(part, msg)
        got = lax.ppermute(msg, "tm", [(i, i ^ hop) for i in range(n)])
        got = run_part(part, got)
        got_f, got_a, got_d = got[:half], got[half : 2 * half], got[2 * half :]
        next_f = jnp.where(upper, mine_d * got_f + mine_f, got_d * mine_f + got_f)
        next_a = jnp.where(upper, got_d * mine_a + got_a, mine_d * got_a + mine_a)
        msg = jnp.concatenate([next_f, next_a, mine_d * got_d], axis=0)
        before = jnp.where(upper, d_before * got_f + before, before)
        after = jnp.where(upper, after, d_after * got_a + after)
        d_before = jnp.where(upper, d_before * got_d, d_before)
        d_after = jnp.where(upper, d_after, d_after * got_d)
        msg, before, after, d_before, d_after = lax.optimization_barrier(
            (msg, before, after, d_before, d_after)
        )
    near, far = uppers[-2], uppers[-1]
    mine_f, mine_a, mine_d = msg[:half], msg[half : 2 * half], msg[2 * half :]
    to_near = jnp.concatenate([jnp.where(near, mine_a, mine_f), mine_d], axis=0)
    to_far = jnp.concatenate([jnp.where(far, mine_a, mine_f), mine_d], axis=0)
    to_near, to_far = lax.optimization_barrier((to_near, to_far))
    to_near = run_part.gate(parts - 1, to_near)
    quarter = hops[-2]
    got = [
        lax.ppermute(sent, "tm", [(i, i ^ hop) for i in range(n)])
        for sent, hop in ((to_far, 2 * quarter), (to_near, quarter), (to_far, 3 * quarter))
    ]
    got = run_part(parts - 1, tuple(got))
    (x2, d2), (x1, d1), (x3, d3) = [(g[:half], g[half:]) for g in got]
    others_f = jnp.where(
        far,
        jnp.where(near, (x3 * d2 + x2) * d1 + x1, d3 * x2 + x3),
        jnp.where(near, x1, 0.0),
    )
    others_a = jnp.where(
        far,
        jnp.where(near, 0.0, x1),
        jnp.where(near, x3 + d3 * x2, x1 + d1 * (x2 + d2 * x3)),
    )
    before = d_before * others_f + before
    after = d_after * others_a + after
    second_f = first_d * before + first_f
    first_a = last_d * after + last_a
    mine_f, mine_a = jnp.where(late, second_f, before), jnp.where(late, after, first_a)
    sent = jnp.concatenate(
        [jnp.where(late, before, second_f), jnp.where(late, first_a, after)], axis=0
    )
    got = lax.ppermute(sent, "tm", pairs)
    got_f, got_a = got[:half], got[half:]
    before = jnp.concatenate(
        [jnp.where(late, got_f, mine_f), jnp.where(late, mine_f, got_f)], axis=0
    )
    after = jnp.concatenate(
        [jnp.where(late, got_a, mine_a), jnp.where(late, mine_a, got_a)], axis=0
    )
    return before, after


class KernelParts:
    def __init__(self, split, gains, sums, modes, counts, params):
        self.split, self.gains, self.sums = split, gains, sums
        self.modes, self.counts, self.params = modes, counts, params
        self.kf, self.ka = [], []

    def gate(self, part, sent):
        if part >= 0:
            sent, self.gains = lax.optimization_barrier((sent, self.gains))
        return sent

    def __call__(self, part, got):
        if part < 0:
            return got
        length = self.counts[part] * CHUNK * (CHUNK // self.modes)
        whole = pl.BlockSpec(memory_space=pltpu.VMEM)
        kf, ka = pl.pallas_call(
            functools.partial(kernels_kernel, self.modes, sum(self.counts[:part])),
            name="kernels",
            in_specs=[whole] * 3,
            out_specs=[whole] * 2,
            out_shape=[pltpu.VMEM((length, CHUNK), BF16)] * 2,
            compiler_params=self.params,
            cost_estimate=pl.CostEstimate(
                flops=20 * length * CHUNK * CHUNK, bytes_accessed=8 << 20, transcendentals=0
            ),
        )(on_vmem(self.split), on_vmem(self.gains), on_vmem(self.sums))
        got, kf, ka = lax.optimization_barrier((got, kf, ka))
        self.kf.append(kf)
        self.ka.append(ka)
        return got


def body(currents, seed_on_tension, mode_diffusivity_factor, decay_rates, fit_weights, counts):
    samples, wires = currents.shape
    modes = decay_rates.shape[0]
    devices = lax.axis_size("tm")
    chunks = samples // CHUNK
    reps = wires // CHUNK
    me = lax.axis_index("tm")
    uppers = tuple((me & hop) != 0 for hop in hops_of(devices))
    rates, uppers = lax.optimization_barrier((decay_rates.reshape(1, modes), uppers))
    fits = fit_weights.reshape(1, modes)
    counts = counts.reshape(1, wires)
    params = pltpu.CompilerParams(vmem_limit_bytes=16 << 20)
    apart = pl.BlockSpec(memory_space=pl.ANY)
    whole = pl.BlockSpec(memory_space=pltpu.VMEM)
    flops = 2 * samples * wires
    copies = len(pieces_of(chunks))

    cur, fresh_f, fresh_a, decay, msg, split, start, back, gains, sums = pl.pallas_call(
        totals_kernel,
        name="totals",
        in_specs=[apart] * 5,
        out_specs=[whole] * 10,
        out_shape=[
            pltpu.VMEM((samples, wires), BF16),
            pltpu.VMEM((chunks * modes, wires), F32),
            pltpu.VMEM((chunks * modes, wires), BF16),
            pltpu.VMEM((chunks * modes, CHUNK), F32),
            pltpu.VMEM((2 * reps + 1, modes, CHUNK), F32),
            pltpu.VMEM((chunks * modes, 2 * CHUNK), BF16),
            pltpu.VMEM((chunks * modes, CHUNK), BF16),
            pltpu.VMEM((chunks * modes, CHUNK), BF16),
            pltpu.VMEM((CHUNK, CHUNK), F32),
            pltpu.VMEM((CHUNK, LEVELS * CHUNK), BF16),
        ],
        scratch_shapes=[
            pltpu.VMEM((samples, wires), BF16),
            pltpu.VMEM((modes, samples), F32),
            pltpu.VMEM((1, modes), F32),
            pltpu.VMEM((1, modes), F32),
            pltpu.SemaphoreType.DMA((3,)),
            pltpu.SemaphoreType.DMA,
            pltpu.SemaphoreType.DMA,
        ],
        compiler_params=params,
        cost_estimate=pl.CostEstimate(
            flops=2 * modes * flops, bytes_accessed=14 << 20, transcendentals=0
        ),
    )(
        on_hbm(mode_diffusivity_factor),
        on_hbm(rates),
        on_hbm(fits),
        on_hbm(currents),
        on_hbm(seed_on_tension),
    )

    groups = chunks * modes // CHUNK
    parts = 2
    shares = [groups - groups // 3, groups // 3]
    covered = KernelParts(split, gains, sums, modes, shares, params)
    before, after = scan_devices(msg, uppers, reps, covered, parts)

    pieces = stress_pieces(chunks)
    early, tail, lse = pl.pallas_call(
        stress_kernel,
        name="stress",
        in_specs=[whole] * (6 + parts),
        out_specs=[apart, whole, whole],
        out_shape=[
            pltpu.HBM((samples, wires), BF16),
            pltpu.VMEM((pieces[-1] * CHUNK, wires), BF16),
            pltpu.HBM((devices, 1, wires), F32),
        ],
        scratch_shapes=[pltpu.VMEM((samples, wires), BF16), pltpu.SemaphoreType.DMA((len(pieces),))],
        compiler_params=params,
        cost_estimate=pl.CostEstimate(
            flops=2 * CHUNK * flops, bytes_accessed=10 << 20, transcendentals=0
        ),
    )(*map(on_vmem, (cur, start, fresh_f, decay, before, counts, *covered.kf)))

    all_lse = lax.all_to_all(lse, "tm", 0, 0, tiled=True)

    gradient, tension = pl.pallas_call(
        adjoint_kernel,
        name="adjoint",
        in_specs=[apart] * 2 + [whole] * (6 + parts),
        out_specs=[apart] * 2,
        out_shape=[pltpu.HBM((samples, wires), BF16)] * 2,
        input_output_aliases={1: 1},
        scratch_shapes=[
            pltpu.VMEM((samples, wires), BF16),
            pltpu.VMEM((samples, wires), BF16),
            pltpu.SemaphoreType.DMA((copies,)),
            pltpu.SemaphoreType.DMA((copies,)),
            pltpu.SemaphoreType.DMA,
        ],
        compiler_params=params,
        cost_estimate=pl.CostEstimate(
            flops=2 * CHUNK * flops, bytes_accessed=10 << 20, transcendentals=0
        ),
    )(
        on_hbm(seed_on_tension),
        on_hbm(early),
        on_vmem(tail),
        *map(on_vmem, (back, fresh_a, decay, after, counts, *covered.ka)),
    )

    top = jnp.max(all_lse, axis=0)
    total = jnp.sum(jnp.exp2(all_lse - top[None]), axis=0)
    softened = ((top * LN2 + jnp.log(total)) / SHARPNESS).reshape(wires)
    return (tension, gradient, softened)


def solution(mesh):
    placed = (P("tm", "parts"), P("tm", "parts"), P(None, ("parts", "tm")), P(), P(), P("parts"))
    return jax.shard_map(
        body,
        mesh=mesh,
        in_specs=placed,
        out_specs=(P("tm", "parts"), P("tm", "parts"), P("parts")),
        check_vma=False,
    )
```

```python
import functools
import math

import jax
import jax.numpy as jnp
from jax import lax
from jax.experimental import pallas as pl
from jax.experimental.pallas import tpu as pltpu
from jax.sharding import PartitionSpec as P

CHUNK = 128
LEVELS = 7
SHARPNESS = 4.0
LOG2E = math.log2(math.e)
LN2 = math.log(2.0)
F32 = jnp.float32
BF16 = jnp.bfloat16


def as_column(row):
    m = row.shape[1]
    r = lax.broadcasted_iota(jnp.int32, (m, m), 0)
    c = lax.broadcasted_iota(jnp.int32, (m, m), 1)
    return jnp.sum(jnp.where(r == c, jnp.broadcast_to(row, (m, m)), 0.0), axis=1, keepdims=True)


def rates_and_gains(rates_ref, fit_ref):
    rates = as_column(rates_ref[...])
    gains = as_column(fit_ref[...]) * jnp.sqrt(rates)
    return rates * LOG2E, gains


def level_sums():
    v = lax.broadcasted_iota(jnp.int32, (CHUNK, CHUNK), 0)
    u = lax.broadcasted_iota(jnp.int32, (CHUNK, CHUNK), 1)
    apart = v ^ u
    tables = []
    for level in range(LEVELS):
        half = 1 << level
        near = apart < half
        inside = jnp.where((u & half) != 0, jnp.where(v <= u, -1.0, 0.0), jnp.where(v > u, -1.0, 0.0))
        tables.append(jnp.where(near, inside, 0.0).astype(BF16))
    return jnp.concatenate(tables, axis=1)


def wide(a, times):
    return jnp.concatenate([a] * times, axis=1)


def stacked(heat_ref, speed, first, count):
    return jnp.concatenate(
        [
            heat_ref[:, c * CHUNK : (c + 1) * CHUNK] * speed
            for c in range(first, first + count)
        ],
        axis=0,
    )


def group_of(chunks, most):
    return max(g for g in range(1, most + 1) if chunks % g == 0)


def pieces_of(chunks):
    if chunks % 8:
        return [1] * chunks
    unit = chunks // 8
    return [3 * unit, 2 * unit, 2 * unit, unit]


def prefixes(heat):
    high = heat.astype(BF16)
    rest = heat - high.astype(F32)
    middle = rest.astype(BF16)
    low = (rest - middle.astype(F32)).astype(BF16)
    v = lax.broadcasted_iota(jnp.int32, (CHUNK, CHUNK), 0)
    u = lax.broadcasted_iota(jnp.int32, (CHUNK, CHUNK), 1)
    ones = jnp.concatenate(
        [jnp.where(v <= u, 1.0, 0.0).astype(BF16), jnp.where(v > u, 1.0, 0.0).astype(BF16)],
        axis=1,
    )
    both = jnp.dot(
        jnp.concatenate([high, middle, low], axis=1),
        jnp.concatenate([ones] * 3, axis=0),
        preferred_element_type=F32,
    )
    return both[:, :CHUNK], both[:, CHUNK:], jnp.concatenate([high, middle], axis=1)


def totals_kernel(
    heat_hbm, rates_hbm, fits_hbm, cur_hbm, cot_hbm,
    cur_ref, fresh_f_ref, fresh_a_ref, decay_ref, msg_ref,
    split_ref, start_ref, back_ref, gains_ref, sums_ref,
    cot_ref, heat_ref, rates_ref, fits_ref, small_sem, cur_sem, cot_sem,
):
    modes = heat_ref.shape[0]
    samples, wires = cur_ref.shape
    reps = wires // CHUNK
    chunks = samples // CHUNK
    group = group_of(chunks, 3)

    small = [
        pltpu.make_async_copy(heat_hbm, heat_ref, small_sem.at[0]),
        pltpu.make_async_copy(rates_hbm, rates_ref, small_sem.at[1]),
        pltpu.make_async_copy(fits_hbm, fits_ref, small_sem.at[2]),
    ]
    for copy in small:
        copy.start()
    load_cur = pltpu.make_async_copy(cur_hbm, cur_ref, cur_sem)
    load_cot = pltpu.make_async_copy(cot_hbm, cot_ref, cot_sem)
    load_cur.start()
    load_cot.start()
    sums_ref[...] = level_sums()
    for copy in small:
        copy.wait()

    speed, gains = rates_and_gains(rates_ref, fits_ref)
    gain_stack = jnp.concatenate([gains] * group, axis=0)
    gains_ref[...] = jnp.broadcast_to(
        jnp.concatenate([gains] * (CHUNK // modes), axis=0), gains_ref.shape
    )
    for first in range(0, chunks, group):
        rows = slice(first * modes, (first + group) * modes)
        pre, suf, split = prefixes(stacked(heat_ref, speed, first, group))
        split_ref[rows, :] = split
        start_ref[rows, :] = (gain_stack * jnp.exp2(-pre)).astype(BF16)
        back_ref[rows, :] = jnp.exp2(-suf).astype(BF16)
        decay_ref[rows, :] = jnp.exp2(-(pre + suf))

    tf = jnp.zeros((modes, wires), F32)
    ta = jnp.zeros((modes, wires), F32)
    dc = jnp.ones((modes, CHUNK), F32)
    load_cur.wait()
    for c in range(chunks):
        span = slice(c * CHUNK, (c + 1) * CHUNK)
        rows = slice(c * modes, (c + 1) * modes)
        fresh_f = jnp.dot(back_ref[rows, :], cur_ref[span, :], preferred_element_type=F32)
        fresh_f_ref[rows, :] = fresh_f
        tf = wide(decay_ref[rows, :], reps) * tf + fresh_f
    load_cot.wait()
    for c in range(chunks):
        span = slice(c * CHUNK, (c + 1) * CHUNK)
        rows = slice(c * modes, (c + 1) * modes)
        fresh_a = jnp.dot(start_ref[rows, :], cot_ref[span, :], preferred_element_type=F32)
        fresh_a_ref[rows, :] = fresh_a.astype(BF16)
        ta = ta + wide(dc, reps) * fresh_a
        dc = dc * decay_ref[rows, :]
    for k in range(reps):
        lanes = slice(k * CHUNK, (k + 1) * CHUNK)
        msg_ref[k] = tf[:, lanes]
        msg_ref[reps + k] = ta[:, lanes]
    msg_ref[2 * reps] = dc


def kernels_kernel(modes, first, split_ref, gains_ref, sums_ref, kf_ref, ka_ref):
    group = CHUNK // modes
    t = lax.broadcasted_iota(jnp.int32, (CHUNK, CHUNK), 0)
    s = lax.broadcasted_iota(jnp.int32, (CHUNK, CHUNK), 1)
    apart = jnp.where(t >= s, t ^ s, -1)
    gains = gains_ref[...]
    gain_sum = jnp.sum(gains[:modes], axis=0, keepdims=True)
    base = jnp.where(apart == 0, jnp.broadcast_to(gain_sum, (CHUNK, CHUNK)), 0.0)
    for g in range(kf_ref.shape[0] // (CHUNK * group)):
        rows = slice((first + g) * CHUNK, (first + g + 1) * CHUNK)
        sums = jnp.dot(
            split_ref[rows, :],
            jnp.concatenate([sums_ref[...]] * 2, axis=0),
            preferred_element_type=F32,
        )
        kernels = [base] * group
        for level in range(LEVELS):
            table = jnp.exp2(sums[:, level * CHUNK : (level + 1) * CHUNK])
            left = (gains * table).astype(BF16).T
            right = table.astype(BF16)
            columns = []
            for c in range(group):
                parts = []
                if c > 0:
                    parts.append(jnp.zeros((c * modes, CHUNK), BF16))
                parts.append(right[c * modes : (c + 1) * modes])
                if c + 1 < group:
                    parts.append(jnp.zeros(((group - 1 - c) * modes, CHUNK), BF16))
                columns.append(jnp.concatenate(parts, axis=0))
            both = jnp.dot(left, jnp.concatenate(columns, axis=1), preferred_element_type=F32)
            keep = apart >= (1 << level)
            kernels = [
                jnp.where(keep, both[:, c * CHUNK : (c + 1) * CHUNK], kernels[c])
                for c in range(group)
            ]
        for c in range(group):
            span = slice((g * group + c) * CHUNK, (g * group + c + 1) * CHUNK)
            kernel = kernels[c].astype(BF16)
            kf_ref[span, :] = kernel
            ka_ref[span, :] = kernel.T


def carry(table, state):
    return lax.dot_general(
        table, state, (((0,), (0,)), ((), ())), preferred_element_type=F32
    )


def part_of(refs, c):
    for ref in refs:
        chunks = ref.shape[0] // CHUNK
        if c < chunks:
            return ref[c * CHUNK : (c + 1) * CHUNK, :]
        c -= chunks


def stress_pieces(chunks):
    if chunks % 8:
        return [1] * chunks
    unit = chunks // 8
    return [2 * unit, unit, unit, unit, 3 * unit]


def stress_kernel(
    cur_ref, start_ref, fresh_ref, decay_ref, in_ref, counts_ref, *refs
):
    kf_refs = refs[:-5]
    out_hbm, tail_ref, lse_ref, out_ref, sem = refs[-5:]
    samples, wires = cur_ref.shape
    reps = wires // CHUNK
    modes = in_ref.shape[1]
    scale = counts_ref[...].astype(F32) * 0.25
    scale2 = scale * (SHARPNESS * LOG2E)
    state = jnp.concatenate([in_ref[k] for k in range(reps)], axis=1)
    high = jnp.full((8, wires), -1e30, F32)
    amount = jnp.zeros((8, wires), F32)
    stores = []
    first = 0
    pieces = stress_pieces(samples // CHUNK)
    for k, piece in enumerate(pieces):
        last = k == len(pieces) - 1
        for c in range(first, first + piece):
            span = slice(c * CHUNK, (c + 1) * CHUNK)
            rows = slice(c * modes, (c + 1) * modes)
            acc = jnp.dot(part_of(kf_refs, c), cur_ref[span, :], preferred_element_type=F32)
            acc = acc + carry(start_ref[rows, :], state.astype(BF16))
            stress = (acc * scale).astype(BF16)
            if last:
                tail_ref[(c - first) * CHUNK : (c - first + 1) * CHUNK, :] = stress
            else:
                out_ref[span, :] = stress
            z = (acc * scale2).reshape(CHUNK // 8, 8, wires)
            new = jnp.maximum(high, jnp.max(z, axis=0))
            amount = amount * jnp.exp2(high - new) + jnp.sum(jnp.exp2(z - new[None]), axis=0)
            high = new
            state = wide(decay_ref[rows, :], reps) * state + fresh_ref[rows, :]
        if not last:
            done = pl.ds(first * CHUNK, piece * CHUNK)
            copy = pltpu.make_async_copy(out_ref.at[done], out_hbm.at[done], sem.at[k])
            copy.start()
            stores.append(copy)
        first += piece
    top = jnp.max(high, axis=0, keepdims=True)
    total = jnp.sum(amount * jnp.exp2(high - top), axis=0, keepdims=True)
    value = top + jnp.log(total) * LOG2E
    lse_ref[...] = jnp.broadcast_to(value[None], lse_ref.shape)
    for copy in stores:
        copy.wait()


def adjoint_kernel(
    cot_hbm, early_hbm, tail_ref, back_ref, fresh_ref, decay_ref, in_ref, counts_ref, *refs
):
    ka_refs = refs[:-7]
    out_hbm, stress_hbm, cot_ref, out_ref, load_sem, sem, tail_sem = refs[-7:]
    samples, wires = cot_ref.shape
    reps = wires // CHUNK
    chunks = samples // CHUNK
    modes = in_ref.shape[1]
    scale = counts_ref[...].astype(F32) * 0.25
    state = jnp.concatenate([in_ref[k] for k in range(reps)], axis=1)
    loads = []
    end = chunks
    for k, piece in enumerate(pieces_of(chunks)):
        rows = pl.ds((end - piece) * CHUNK, piece * CHUNK)
        copy = pltpu.make_async_copy(cot_hbm.at[rows], cot_ref.at[rows], load_sem.at[k])
        copy.start()
        loads.append(copy)
        end -= piece
    tail = tail_ref.shape[0]
    copy = pltpu.make_async_copy(tail_ref, stress_hbm.at[pl.ds(samples - tail, tail)], tail_sem)
    copy.start()
    stores = [copy]
    end = chunks
    for k, piece in enumerate(pieces_of(chunks)):
        loads[k].wait()
        for c in reversed(range(end - piece, end)):
            span = slice(c * CHUNK, (c + 1) * CHUNK)
            rows = slice(c * modes, (c + 1) * modes)
            acc = jnp.dot(part_of(ka_refs, c), cot_ref[span, :], preferred_element_type=F32)
            acc = acc + carry(back_ref[rows, :], state.astype(BF16))
            out_ref[span, :] = (acc * scale).astype(BF16)
            state = wide(decay_ref[rows, :], reps) * state + fresh_ref[rows, :].astype(F32)
        done = pl.ds((end - piece) * CHUNK, piece * CHUNK)
        copy = pltpu.make_async_copy(out_ref.at[done], out_hbm.at[done], sem.at[k])
        copy.start()
        stores.append(copy)
        end -= piece
    for copy in stores:
        copy.wait()


def on_vmem(a):
    return pltpu.with_memory_space_constraint(a, pltpu.VMEM)


def on_hbm(a):
    return pltpu.with_memory_space_constraint(a, pltpu.HBM)


def hops_of(n):
    return [1 << k for k in range(n.bit_length() - 1)]


def scan_devices(msg, uppers, reps, run_part, parts):
    n = lax.axis_size("tm")
    half = reps // 2
    hops = hops_of(n)
    late = uppers[0]
    pairs = [(i, i ^ 1) for i in range(n)]

    low_f, high_f = msg[:half], msg[half:reps]
    low_a, high_a = msg[reps : reps + half], msg[reps + half : 2 * reps]
    mine_d = msg[2 * reps :]
    sent = jnp.concatenate(
        [jnp.where(late, low_f, high_f), jnp.where(late, low_a, high_a), mine_d], axis=0
    )
    mine_f, mine_a = jnp.where(late, high_f, low_f), jnp.where(late, high_a, low_a)
    got = lax.ppermute(sent, "tm", pairs)
    got_f, got_a, got_d = got[:half], got[half : 2 * half], got[2 * half :]
    first_f, last_a = jnp.where(late, got_f, mine_f), jnp.where(late, mine_a, got_a)
    first_d, last_d = jnp.where(late, got_d, mine_d), jnp.where(late, mine_d, got_d)
    msg = jnp.concatenate(
        [
            last_d * first_f + jnp.where(late, mine_f, got_f),
            jnp.where(late, got_a, mine_a) + first_d * last_a,
            mine_d * got_d,
        ],
        axis=0,
    )
    before = jnp.zeros_like(mine_f)
    after = jnp.zeros_like(mine_f)
    d_before = jnp.ones_like(mine_d)
    d_after = jnp.ones_like(mine_d)
    msg, first_f, last_a, first_d, last_d = lax.optimization_barrier(
        (msg, first_f, last_a, first_d, last_d)
    )
    for index, hop in list(enumerate(hops))[1:-2]:
        upper = uppers[index]
        mine_f, mine_a, mine_d = msg[:half], msg[half : 2 * half], msg[2 * half :]
        part = index - len(hops) + 2 + parts - 1
        msg = run_part.gate(part, msg)
        got = lax.ppermute(msg, "tm", [(i, i ^ hop) for i in range(n)])
        got = run_part(part, got)
        got_f, got_a, got_d = got[:half], got[half : 2 * half], got[2 * half :]
        next_f = jnp.where(upper, mine_d * got_f + mine_f, got_d * mine_f + got_f)
        next_a = jnp.where(upper, got_d * mine_a + got_a, mine_d * got_a + mine_a)
        msg = jnp.concatenate([next_f, next_a, mine_d * got_d], axis=0)
        before = jnp.where(upper, d_before * got_f + before, before)
        after = jnp.where(upper, after, d_after * got_a + after)
        d_before = jnp.where(upper, d_before * got_d, d_before)
        d_after = jnp.where(upper, d_after, d_after * got_d)
        msg, before, after, d_before, d_after = lax.optimization_barrier(
            (msg, before, after, d_before, d_after)
        )
    near, far = uppers[-2], uppers[-1]
    mine_f, mine_a, mine_d = msg[:half], msg[half : 2 * half], msg[2 * half :]
    to_near = jnp.concatenate([jnp.where(near, mine_a, mine_f), mine_d], axis=0)
    to_far = jnp.concatenate([jnp.where(far, mine_a, mine_f), mine_d], axis=0)
    to_near, to_far = lax.optimization_barrier((to_near, to_far))
    to_near = run_part.gate(parts - 1, to_near)
    quarter = hops[-2]
    got = [
        lax.ppermute(sent, "tm", [(i, i ^ hop) for i in range(n)])
        for sent, hop in ((to_far, 2 * quarter), (to_near, quarter), (to_far, 3 * quarter))
    ]
    got = run_part(parts - 1, tuple(got))
    (x2, d2), (x1, d1), (x3, d3) = [(g[:half], g[half:]) for g in got]
    others_f = jnp.where(
        far,
        jnp.where(near, (x3 * d2 + x2) * d1 + x1, d3 * x2 + x3),
        jnp.where(near, x1, 0.0),
    )
    others_a = jnp.where(
        far,
        jnp.where(near, 0.0, x1),
        jnp.where(near, x3 + d3 * x2, x1 + d1 * (x2 + d2 * x3)),
    )
    before = d_before * others_f + before
    after = d_after * others_a + after
    second_f = first_d * before + first_f
    first_a = last_d * after + last_a
    mine_f, mine_a = jnp.where(late, second_f, before), jnp.where(late, after, first_a)
    sent = jnp.concatenate(
        [jnp.where(late, before, second_f), jnp.where(late, first_a, after)], axis=0
    )
    got = lax.ppermute(sent, "tm", pairs)
    got_f, got_a = got[:half], got[half:]
    before = jnp.concatenate(
        [jnp.where(late, got_f, mine_f), jnp.where(late, mine_f, got_f)], axis=0
    )
    after = jnp.concatenate(
        [jnp.where(late, got_a, mine_a), jnp.where(late, mine_a, got_a)], axis=0
    )
    return before, after


class KernelParts:
    def __init__(self, split, gains, sums, modes, counts, params):
        self.split, self.gains, self.sums = split, gains, sums
        self.modes, self.counts, self.params = modes, counts, params
        self.kf, self.ka = [], []

    def gate(self, part, sent):
        if part >= 0:
            sent, self.gains = lax.optimization_barrier((sent, self.gains))
        return sent

    def __call__(self, part, got):
        if part < 0:
            return got
        length = self.counts[part] * CHUNK * (CHUNK // self.modes)
        whole = pl.BlockSpec(memory_space=pltpu.VMEM)
        kf, ka = pl.pallas_call(
            functools.partial(kernels_kernel, self.modes, sum(self.counts[:part])),
            name="kernels",
            in_specs=[whole] * 3,
            out_specs=[whole] * 2,
            out_shape=[pltpu.VMEM((length, CHUNK), BF16)] * 2,
            compiler_params=self.params,
            cost_estimate=pl.CostEstimate(
                flops=20 * length * CHUNK * CHUNK, bytes_accessed=8 << 20, transcendentals=0
            ),
        )(on_vmem(self.split), on_vmem(self.gains), on_vmem(self.sums))
        got, kf, ka = lax.optimization_barrier((got, kf, ka))
        self.kf.append(kf)
        self.ka.append(ka)
        return got


def body(currents, seed_on_tension, mode_diffusivity_factor, decay_rates, fit_weights, counts):
    samples, wires = currents.shape
    modes = decay_rates.shape[0]
    devices = lax.axis_size("tm")
    chunks = samples // CHUNK
    reps = wires // CHUNK
    me = lax.axis_index("tm")
    uppers = tuple((me & hop) != 0 for hop in hops_of(devices))
    rates, uppers = lax.optimization_barrier((decay_rates.reshape(1, modes), uppers))
    fits = fit_weights.reshape(1, modes)
    counts = counts.reshape(1, wires)
    params = pltpu.CompilerParams(vmem_limit_bytes=16 << 20)
    apart = pl.BlockSpec(memory_space=pl.ANY)
    whole = pl.BlockSpec(memory_space=pltpu.VMEM)
    flops = 2 * samples * wires
    copies = len(pieces_of(chunks))

    cur, fresh_f, fresh_a, decay, msg, split, start, back, gains, sums = pl.pallas_call(
        totals_kernel,
        name="totals",
        in_specs=[apart] * 5,
        out_specs=[whole] * 10,
        out_shape=[
            pltpu.VMEM((samples, wires), BF16),
            pltpu.VMEM((chunks * modes, wires), F32),
            pltpu.VMEM((chunks * modes, wires), BF16),
            pltpu.VMEM((chunks * modes, CHUNK), F32),
            pltpu.VMEM((2 * reps + 1, modes, CHUNK), F32),
            pltpu.VMEM((chunks * modes, 2 * CHUNK), BF16),
            pltpu.VMEM((chunks * modes, CHUNK), BF16),
            pltpu.VMEM((chunks * modes, CHUNK), BF16),
            pltpu.VMEM((CHUNK, CHUNK), F32),
            pltpu.VMEM((CHUNK, LEVELS * CHUNK), BF16),
        ],
        scratch_shapes=[
            pltpu.VMEM((samples, wires), BF16),
            pltpu.VMEM((modes, samples), F32),
            pltpu.VMEM((1, modes), F32),
            pltpu.VMEM((1, modes), F32),
            pltpu.SemaphoreType.DMA((3,)),
            pltpu.SemaphoreType.DMA,
            pltpu.SemaphoreType.DMA,
        ],
        compiler_params=params,
        cost_estimate=pl.CostEstimate(
            flops=2 * modes * flops, bytes_accessed=14 << 20, transcendentals=0
        ),
    )(
        on_hbm(mode_diffusivity_factor),
        on_hbm(rates),
        on_hbm(fits),
        on_hbm(currents),
        on_hbm(seed_on_tension),
    )

    groups = chunks * modes // CHUNK
    parts = 1
    shares = [groups]
    covered = KernelParts(split, gains, sums, modes, shares, params)
    before, after = scan_devices(msg, uppers, reps, covered, parts)

    pieces = stress_pieces(chunks)
    early, tail, lse = pl.pallas_call(
        stress_kernel,
        name="stress",
        in_specs=[whole] * (6 + parts),
        out_specs=[apart, whole, whole],
        out_shape=[
            pltpu.HBM((samples, wires), BF16),
            pltpu.VMEM((pieces[-1] * CHUNK, wires), BF16),
            pltpu.HBM((devices, 1, wires), F32),
        ],
        scratch_shapes=[pltpu.VMEM((samples, wires), BF16), pltpu.SemaphoreType.DMA((len(pieces),))],
        compiler_params=params,
        cost_estimate=pl.CostEstimate(
            flops=2 * CHUNK * flops, bytes_accessed=10 << 20, transcendentals=0
        ),
    )(*map(on_vmem, (cur, start, fresh_f, decay, before, counts, *covered.kf)))

    all_lse = lax.all_to_all(lse, "tm", 0, 0, tiled=True)

    gradient, tension = pl.pallas_call(
        adjoint_kernel,
        name="adjoint",
        in_specs=[apart] * 2 + [whole] * (6 + parts),
        out_specs=[apart] * 2,
        out_shape=[pltpu.HBM((samples, wires), BF16)] * 2,
        input_output_aliases={1: 1},
        scratch_shapes=[
            pltpu.VMEM((samples, wires), BF16),
            pltpu.VMEM((samples, wires), BF16),
            pltpu.SemaphoreType.DMA((copies,)),
            pltpu.SemaphoreType.DMA((copies,)),
            pltpu.SemaphoreType.DMA,
        ],
        compiler_params=params,
        cost_estimate=pl.CostEstimate(
            flops=2 * CHUNK * flops, bytes_accessed=10 << 20, transcendentals=0
        ),
    )(
        on_hbm(seed_on_tension),
        on_hbm(early),
        on_vmem(tail),
        *map(on_vmem, (back, fresh_a, decay, after, counts, *covered.ka)),
    )

    top = jnp.max(all_lse, axis=0)
    total = jnp.sum(jnp.exp2(all_lse - top[None]), axis=0)
    softened = ((top * LN2 + jnp.log(total)) / SHARPNESS).reshape(wires)
    return (tension, gradient, softened)


def solution(mesh):
    placed = (P("tm", "parts"), P("tm", "parts"), P(None, ("parts", "tm")), P(), P(), P("parts"))
    return jax.shard_map(
        body,
        mesh=mesh,
        in_specs=placed,
        out_specs=(P("tm", "parts"), P("tm", "parts"), P("parts")),
        check_vma=False,
    )
```

```python
import functools
import math

import jax
import jax.numpy as jnp
from jax import lax
from jax.experimental import pallas as pl
from jax.experimental.pallas import tpu as pltpu
from jax.sharding import PartitionSpec as P

CHUNK = 128
LEVELS = 7
SHARPNESS = 4.0
LOG2E = math.log2(math.e)
LN2 = math.log(2.0)
F32 = jnp.float32
BF16 = jnp.bfloat16


def as_column(row):
    m = row.shape[1]
    r = lax.broadcasted_iota(jnp.int32, (m, m), 0)
    c = lax.broadcasted_iota(jnp.int32, (m, m), 1)
    return jnp.sum(jnp.where(r == c, jnp.broadcast_to(row, (m, m)), 0.0), axis=1, keepdims=True)


def rates_and_gains(rates_ref, fit_ref):
    rates = as_column(rates_ref[...])
    gains = as_column(fit_ref[...]) * jnp.sqrt(rates)
    return rates * LOG2E, gains


def level_sums():
    v = lax.broadcasted_iota(jnp.int32, (CHUNK, CHUNK), 0)
    u = lax.broadcasted_iota(jnp.int32, (CHUNK, CHUNK), 1)
    apart = v ^ u
    tables = []
    for level in range(LEVELS):
        half = 1 << level
        near = apart < half
        inside = jnp.where((u & half) != 0, jnp.where(v <= u, -1.0, 0.0), jnp.where(v > u, -1.0, 0.0))
        tables.append(jnp.where(near, inside, 0.0).astype(BF16))
    return jnp.concatenate(tables, axis=1)


def wide(a, times):
    return jnp.concatenate([a] * times, axis=1)


def stacked(heat_ref, speed, first, count):
    return jnp.concatenate(
        [
            heat_ref[:, c * CHUNK : (c + 1) * CHUNK] * speed
            for c in range(first, first + count)
        ],
        axis=0,
    )


def group_of(chunks, most):
    return max(g for g in range(1, most + 1) if chunks % g == 0)


def pieces_of(chunks):
    if chunks % 8:
        return [1] * chunks
    unit = chunks // 8
    return [3 * unit, 2 * unit, 2 * unit, unit]


def prefixes(heat):
    high = heat.astype(BF16)
    rest = heat - high.astype(F32)
    middle = rest.astype(BF16)
    low = (rest - middle.astype(F32)).astype(BF16)
    v = lax.broadcasted_iota(jnp.int32, (CHUNK, CHUNK), 0)
    u = lax.broadcasted_iota(jnp.int32, (CHUNK, CHUNK), 1)
    ones = jnp.concatenate(
        [jnp.where(v <= u, 1.0, 0.0).astype(BF16), jnp.where(v > u, 1.0, 0.0).astype(BF16)],
        axis=1,
    )
    both = jnp.dot(
        jnp.concatenate([high, middle, low], axis=1),
        jnp.concatenate([ones] * 3, axis=0),
        preferred_element_type=F32,
    )
    return both[:, :CHUNK], both[:, CHUNK:], jnp.concatenate([high, middle], axis=1)


def totals_kernel(
    heat_hbm, rates_hbm, fits_hbm, cur_hbm, cot_hbm,
    cur_ref, fresh_f_ref, fresh_a_ref, decay_ref, msg_ref,
    split_ref, start_ref, back_ref, gains_ref, sums_ref,
    cot_ref, heat_ref, rates_ref, fits_ref, small_sem, cur_sem, cot_sem,
):
    modes = heat_ref.shape[0]
    samples, wires = cur_ref.shape
    reps = wires // CHUNK
    chunks = samples // CHUNK
    group = group_of(chunks, 4)

    small = [
        pltpu.make_async_copy(heat_hbm, heat_ref, small_sem.at[0]),
        pltpu.make_async_copy(rates_hbm, rates_ref, small_sem.at[1]),
        pltpu.make_async_copy(fits_hbm, fits_ref, small_sem.at[2]),
    ]
    for copy in small:
        copy.start()
    load_cur = pltpu.make_async_copy(cur_hbm, cur_ref, cur_sem)
    load_cot = pltpu.make_async_copy(cot_hbm, cot_ref, cot_sem)
    load_cur.start()
    load_cot.start()
    sums_ref[...] = level_sums()
    for copy in small:
        copy.wait()

    speed, gains = rates_and_gains(rates_ref, fits_ref)
    gain_stack = jnp.concatenate([gains] * group, axis=0)
    gains_ref[...] = jnp.broadcast_to(
        jnp.concatenate([gains] * (CHUNK // modes), axis=0), gains_ref.shape
    )
    for first in range(0, chunks, group):
        rows = slice(first * modes, (first + group) * modes)
        pre, suf, split = prefixes(stacked(heat_ref, speed, first, group))
        split_ref[rows, :] = split
        start_ref[rows, :] = (gain_stack * jnp.exp2(-pre)).astype(BF16)
        back_ref[rows, :] = jnp.exp2(-suf).astype(BF16)
        decay_ref[rows, :] = jnp.exp2(-(pre + suf))

    tf = jnp.zeros((modes, wires), F32)
    ta = jnp.zeros((modes, wires), F32)
    dc = jnp.ones((modes, CHUNK), F32)
    load_cur.wait()
    for c in range(chunks):
        span = slice(c * CHUNK, (c + 1) * CHUNK)
        rows = slice(c * modes, (c + 1) * modes)
        fresh_f = jnp.dot(back_ref[rows, :], cur_ref[span, :], preferred_element_type=F32)
        fresh_f_ref[rows, :] = fresh_f
        tf = wide(decay_ref[rows, :], reps) * tf + fresh_f
    load_cot.wait()
    for c in range(chunks):
        span = slice(c * CHUNK, (c + 1) * CHUNK)
        rows = slice(c * modes, (c + 1) * modes)
        fresh_a = jnp.dot(start_ref[rows, :], cot_ref[span, :], preferred_element_type=F32)
        fresh_a_ref[rows, :] = fresh_a.astype(BF16)
        ta = ta + wide(dc, reps) * fresh_a
        dc = dc * decay_ref[rows, :]
    for k in range(reps):
        lanes = slice(k * CHUNK, (k + 1) * CHUNK)
        msg_ref[k] = tf[:, lanes]
        msg_ref[reps + k] = ta[:, lanes]
    msg_ref[2 * reps] = dc


def kernels_kernel(modes, first, split_ref, gains_ref, sums_ref, kf_ref, ka_ref):
    group = CHUNK // modes
    t = lax.broadcasted_iota(jnp.int32, (CHUNK, CHUNK), 0)
    s = lax.broadcasted_iota(jnp.int32, (CHUNK, CHUNK), 1)
    apart = jnp.where(t >= s, t ^ s, -1)
    gains = gains_ref[...]
    gain_sum = jnp.sum(gains[:modes], axis=0, keepdims=True)
    base = jnp.where(apart == 0, jnp.broadcast_to(gain_sum, (CHUNK, CHUNK)), 0.0)
    for g in range(kf_ref.shape[0] // (CHUNK * group)):
        rows = slice((first + g) * CHUNK, (first + g + 1) * CHUNK)
        sums = jnp.dot(
            split_ref[rows, :],
            jnp.concatenate([sums_ref[...]] * 2, axis=0),
            preferred_element_type=F32,
        )
        kernels = [base] * group
        for level in range(LEVELS):
            table = jnp.exp2(sums[:, level * CHUNK : (level + 1) * CHUNK])
            left = (gains * table).astype(BF16).T
            right = table.astype(BF16)
            columns = []
            for c in range(group):
                parts = []
                if c > 0:
                    parts.append(jnp.zeros((c * modes, CHUNK), BF16))
                parts.append(right[c * modes : (c + 1) * modes])
                if c + 1 < group:
                    parts.append(jnp.zeros(((group - 1 - c) * modes, CHUNK), BF16))
                columns.append(jnp.concatenate(parts, axis=0))
            both = jnp.dot(left, jnp.concatenate(columns, axis=1), preferred_element_type=F32)
            keep = apart >= (1 << level)
            kernels = [
                jnp.where(keep, both[:, c * CHUNK : (c + 1) * CHUNK], kernels[c])
                for c in range(group)
            ]
        for c in range(group):
            span = slice((g * group + c) * CHUNK, (g * group + c + 1) * CHUNK)
            kernel = kernels[c].astype(BF16)
            kf_ref[span, :] = kernel
            ka_ref[span, :] = kernel.T


def carry(table, state):
    return lax.dot_general(
        table, state, (((0,), (0,)), ((), ())), preferred_element_type=F32
    )


def part_of(refs, c):
    for ref in refs:
        chunks = ref.shape[0] // CHUNK
        if c < chunks:
            return ref[c * CHUNK : (c + 1) * CHUNK, :]
        c -= chunks


def stress_pieces(chunks):
    if chunks % 8:
        return [1] * chunks
    unit = chunks // 8
    return [2 * unit, unit, unit, unit, 3 * unit]


def stress_kernel(
    cur_ref, start_ref, fresh_ref, decay_ref, in_ref, counts_ref, *refs
):
    kf_refs = refs[:-5]
    out_hbm, tail_ref, lse_ref, out_ref, sem = refs[-5:]
    samples, wires = cur_ref.shape
    reps = wires // CHUNK
    modes = in_ref.shape[1]
    scale = counts_ref[...].astype(F32) * 0.25
    scale2 = scale * (SHARPNESS * LOG2E)
    state = jnp.concatenate([in_ref[k] for k in range(reps)], axis=1)
    high = jnp.full((8, wires), -1e30, F32)
    amount = jnp.zeros((8, wires), F32)
    stores = []
    first = 0
    pieces = stress_pieces(samples // CHUNK)
    for k, piece in enumerate(pieces):
        last = k == len(pieces) - 1
        for c in range(first, first + piece):
            span = slice(c * CHUNK, (c + 1) * CHUNK)
            rows = slice(c * modes, (c + 1) * modes)
            acc = jnp.dot(part_of(kf_refs, c), cur_ref[span, :], preferred_element_type=F32)
            acc = acc + carry(start_ref[rows, :], state.astype(BF16))
            stress = (acc * scale).astype(BF16)
            if last:
                tail_ref[(c - first) * CHUNK : (c - first + 1) * CHUNK, :] = stress
            else:
                out_ref[span, :] = stress
            z = (acc * scale2).reshape(CHUNK // 8, 8, wires)
            new = jnp.maximum(high, jnp.max(z, axis=0))
            amount = amount * jnp.exp2(high - new) + jnp.sum(jnp.exp2(z - new[None]), axis=0)
            high = new
            state = wide(decay_ref[rows, :], reps) * state + fresh_ref[rows, :]
        if not last:
            done = pl.ds(first * CHUNK, piece * CHUNK)
            copy = pltpu.make_async_copy(out_ref.at[done], out_hbm.at[done], sem.at[k])
            copy.start()
            stores.append(copy)
        first += piece
    top = jnp.max(high, axis=0, keepdims=True)
    total = jnp.sum(amount * jnp.exp2(high - top), axis=0, keepdims=True)
    value = top + jnp.log(total) * LOG2E
    lse_ref[...] = jnp.broadcast_to(value[None], lse_ref.shape)
    for copy in stores:
        copy.wait()


def adjoint_kernel(
    cot_hbm, early_hbm, tail_ref, back_ref, fresh_ref, decay_ref, in_ref, counts_ref, *refs
):
    ka_refs = refs[:-7]
    out_hbm, stress_hbm, cot_ref, out_ref, load_sem, sem, tail_sem = refs[-7:]
    samples, wires = cot_ref.shape
    reps = wires // CHUNK
    chunks = samples // CHUNK
    modes = in_ref.shape[1]
    scale = counts_ref[...].astype(F32) * 0.25
    state = jnp.concatenate([in_ref[k] for k in range(reps)], axis=1)
    load = pltpu.make_async_copy(cot_hbm, cot_ref, load_sem)
    load.start()
    tail = tail_ref.shape[0]
    copy = pltpu.make_async_copy(tail_ref, stress_hbm.at[pl.ds(samples - tail, tail)], tail_sem)
    copy.start()
    stores = [copy]
    load.wait()
    end = chunks
    for k, piece in enumerate(pieces_of(chunks)):
        for c in reversed(range(end - piece, end)):
            span = slice(c * CHUNK, (c + 1) * CHUNK)
            rows = slice(c * modes, (c + 1) * modes)
            acc = jnp.dot(part_of(ka_refs, c), cot_ref[span, :], preferred_element_type=F32)
            acc = acc + carry(back_ref[rows, :], state.astype(BF16))
            out_ref[span, :] = (acc * scale).astype(BF16)
            state = wide(decay_ref[rows, :], reps) * state + fresh_ref[rows, :].astype(F32)
        done = pl.ds((end - piece) * CHUNK, piece * CHUNK)
        copy = pltpu.make_async_copy(out_ref.at[done], out_hbm.at[done], sem.at[k])
        copy.start()
        stores.append(copy)
        end -= piece
    for copy in stores:
        copy.wait()


def on_vmem(a):
    return pltpu.with_memory_space_constraint(a, pltpu.VMEM)


def on_hbm(a):
    return pltpu.with_memory_space_constraint(a, pltpu.HBM)


def hops_of(n):
    return [1 << k for k in range(n.bit_length() - 1)]


def scan_devices(msg, uppers, reps, run_part, parts):
    n = lax.axis_size("tm")
    half = reps // 2
    hops = hops_of(n)
    late = uppers[0]
    pairs = [(i, i ^ 1) for i in range(n)]

    low_f, high_f = msg[:half], msg[half:reps]
    low_a, high_a = msg[reps : reps + half], msg[reps + half : 2 * reps]
    mine_d = msg[2 * reps :]
    sent = jnp.concatenate(
        [jnp.where(late, low_f, high_f), jnp.where(late, low_a, high_a), mine_d], axis=0
    )
    mine_f, mine_a = jnp.where(late, high_f, low_f), jnp.where(late, high_a, low_a)
    got = lax.ppermute(sent, "tm", pairs)
    got_f, got_a, got_d = got[:half], got[half : 2 * half], got[2 * half :]
    first_f, last_a = jnp.where(late, got_f, mine_f), jnp.where(late, mine_a, got_a)
    first_d, last_d = jnp.where(late, got_d, mine_d), jnp.where(late, mine_d, got_d)
    msg = jnp.concatenate(
        [
            last_d * first_f + jnp.where(late, mine_f, got_f),
            jnp.where(late, got_a, mine_a) + first_d * last_a,
            mine_d * got_d,
        ],
        axis=0,
    )
    before = jnp.zeros_like(mine_f)
    after = jnp.zeros_like(mine_f)
    d_before = jnp.ones_like(mine_d)
    d_after = jnp.ones_like(mine_d)
    msg, first_f, last_a, first_d, last_d = lax.optimization_barrier(
        (msg, first_f, last_a, first_d, last_d)
    )
    for index, hop in list(enumerate(hops))[1:-2]:
        upper = uppers[index]
        mine_f, mine_a, mine_d = msg[:half], msg[half : 2 * half], msg[2 * half :]
        part = index - len(hops) + 2 + parts - 1
        msg = run_part.gate(part, msg)
        got = lax.ppermute(msg, "tm", [(i, i ^ hop) for i in range(n)])
        got = run_part(part, got)
        got_f, got_a, got_d = got[:half], got[half : 2 * half], got[2 * half :]
        next_f = jnp.where(upper, mine_d * got_f + mine_f, got_d * mine_f + got_f)
        next_a = jnp.where(upper, got_d * mine_a + got_a, mine_d * got_a + mine_a)
        msg = jnp.concatenate([next_f, next_a, mine_d * got_d], axis=0)
        before = jnp.where(upper, d_before * got_f + before, before)
        after = jnp.where(upper, after, d_after * got_a + after)
        d_before = jnp.where(upper, d_before * got_d, d_before)
        d_after = jnp.where(upper, d_after, d_after * got_d)
        msg, before, after, d_before, d_after = lax.optimization_barrier(
            (msg, before, after, d_before, d_after)
        )
    near, far = uppers[-2], uppers[-1]
    mine_f, mine_a, mine_d = msg[:half], msg[half : 2 * half], msg[2 * half :]
    to_near = jnp.concatenate([jnp.where(near, mine_a, mine_f), mine_d], axis=0)
    to_far = jnp.concatenate([jnp.where(far, mine_a, mine_f), mine_d], axis=0)
    to_near, to_far = lax.optimization_barrier((to_near, to_far))
    to_near = run_part.gate(parts - 1, to_near)
    quarter = hops[-2]
    got = [
        lax.ppermute(sent, "tm", [(i, i ^ hop) for i in range(n)])
        for sent, hop in ((to_far, 2 * quarter), (to_near, quarter), (to_far, 3 * quarter))
    ]
    got = run_part(parts - 1, tuple(got))
    (x2, d2), (x1, d1), (x3, d3) = [(g[:half], g[half:]) for g in got]
    others_f = jnp.where(
        far,
        jnp.where(near, (x3 * d2 + x2) * d1 + x1, d3 * x2 + x3),
        jnp.where(near, x1, 0.0),
    )
    others_a = jnp.where(
        far,
        jnp.where(near, 0.0, x1),
        jnp.where(near, x3 + d3 * x2, x1 + d1 * (x2 + d2 * x3)),
    )
    before = d_before * others_f + before
    after = d_after * others_a + after
    second_f = first_d * before + first_f
    first_a = last_d * after + last_a
    mine_f, mine_a = jnp.where(late, second_f, before), jnp.where(late, after, first_a)
    sent = jnp.concatenate(
        [jnp.where(late, before, second_f), jnp.where(late, first_a, after)], axis=0
    )
    got = lax.ppermute(sent, "tm", pairs)
    got_f, got_a = got[:half], got[half:]
    before = jnp.concatenate(
        [jnp.where(late, got_f, mine_f), jnp.where(late, mine_f, got_f)], axis=0
    )
    after = jnp.concatenate(
        [jnp.where(late, got_a, mine_a), jnp.where(late, mine_a, got_a)], axis=0
    )
    return before, after


class KernelParts:
    def __init__(self, split, gains, sums, modes, counts, params):
        self.split, self.gains, self.sums = split, gains, sums
        self.modes, self.counts, self.params = modes, counts, params
        self.kf, self.ka = [], []

    def gate(self, part, sent):
        if part >= 0:
            sent, self.gains = lax.optimization_barrier((sent, self.gains))
        return sent

    def __call__(self, part, got):
        if part < 0:
            return got
        length = self.counts[part] * CHUNK * (CHUNK // self.modes)
        whole = pl.BlockSpec(memory_space=pltpu.VMEM)
        kf, ka = pl.pallas_call(
            functools.partial(kernels_kernel, self.modes, sum(self.counts[:part])),
            name="kernels",
            in_specs=[whole] * 3,
            out_specs=[whole] * 2,
            out_shape=[pltpu.VMEM((length, CHUNK), BF16)] * 2,
            compiler_params=self.params,
            cost_estimate=pl.CostEstimate(
                flops=20 * length * CHUNK * CHUNK, bytes_accessed=8 << 20, transcendentals=0
            ),
        )(on_vmem(self.split), on_vmem(self.gains), on_vmem(self.sums))
        got, kf, ka = lax.optimization_barrier((got, kf, ka))
        self.kf.append(kf)
        self.ka.append(ka)
        return got


def body(currents, seed_on_tension, mode_diffusivity_factor, decay_rates, fit_weights, counts):
    samples, wires = currents.shape
    modes = decay_rates.shape[0]
    devices = lax.axis_size("tm")
    chunks = samples // CHUNK
    reps = wires // CHUNK
    me = lax.axis_index("tm")
    uppers = tuple((me & hop) != 0 for hop in hops_of(devices))
    rates, uppers = lax.optimization_barrier((decay_rates.reshape(1, modes), uppers))
    fits = fit_weights.reshape(1, modes)
    counts = counts.reshape(1, wires)
    params = pltpu.CompilerParams(vmem_limit_bytes=16 << 20)
    apart = pl.BlockSpec(memory_space=pl.ANY)
    whole = pl.BlockSpec(memory_space=pltpu.VMEM)
    flops = 2 * samples * wires
    copies = len(pieces_of(chunks))

    cur, fresh_f, fresh_a, decay, msg, split, start, back, gains, sums = pl.pallas_call(
        totals_kernel,
        name="totals",
        in_specs=[apart] * 5,
        out_specs=[whole] * 10,
        out_shape=[
            pltpu.VMEM((samples, wires), BF16),
            pltpu.VMEM((chunks * modes, wires), F32),
            pltpu.VMEM((chunks * modes, wires), BF16),
            pltpu.VMEM((chunks * modes, CHUNK), F32),
            pltpu.VMEM((2 * reps + 1, modes, CHUNK), F32),
            pltpu.VMEM((chunks * modes, 2 * CHUNK), BF16),
            pltpu.VMEM((chunks * modes, CHUNK), BF16),
            pltpu.VMEM((chunks * modes, CHUNK), BF16),
            pltpu.VMEM((CHUNK, CHUNK), F32),
            pltpu.VMEM((CHUNK, LEVELS * CHUNK), BF16),
        ],
        scratch_shapes=[
            pltpu.VMEM((samples, wires), BF16),
            pltpu.VMEM((modes, samples), F32),
            pltpu.VMEM((1, modes), F32),
            pltpu.VMEM((1, modes), F32),
            pltpu.SemaphoreType.DMA((3,)),
            pltpu.SemaphoreType.DMA,
            pltpu.SemaphoreType.DMA,
        ],
        compiler_params=params,
        cost_estimate=pl.CostEstimate(
            flops=2 * modes * flops, bytes_accessed=14 << 20, transcendentals=0
        ),
    )(
        on_hbm(mode_diffusivity_factor),
        on_hbm(rates),
        on_hbm(fits),
        on_hbm(currents),
        on_hbm(seed_on_tension),
    )

    groups = chunks * modes // CHUNK
    parts = 1
    shares = [groups]
    covered = KernelParts(split, gains, sums, modes, shares, params)
    before, after = scan_devices(msg, uppers, reps, covered, parts)

    pieces = stress_pieces(chunks)
    early, tail, lse = pl.pallas_call(
        stress_kernel,
        name="stress",
        in_specs=[whole] * (6 + parts),
        out_specs=[apart, whole, whole],
        out_shape=[
            pltpu.HBM((samples, wires), BF16),
            pltpu.VMEM((pieces[-1] * CHUNK, wires), BF16),
            pltpu.HBM((devices, 1, wires), F32),
        ],
        scratch_shapes=[pltpu.VMEM((samples, wires), BF16), pltpu.SemaphoreType.DMA((len(pieces),))],
        compiler_params=params,
        cost_estimate=pl.CostEstimate(
            flops=2 * CHUNK * flops, bytes_accessed=10 << 20, transcendentals=0
        ),
    )(*map(on_vmem, (cur, start, fresh_f, decay, before, counts, *covered.kf)))

    all_lse = lax.all_to_all(lse, "tm", 0, 0, tiled=True)

    gradient, tension = pl.pallas_call(
        adjoint_kernel,
        name="adjoint",
        in_specs=[apart] * 2 + [whole] * (6 + parts),
        out_specs=[apart] * 2,
        out_shape=[pltpu.HBM((samples, wires), BF16)] * 2,
        input_output_aliases={1: 1},
        scratch_shapes=[
            pltpu.VMEM((samples, wires), BF16),
            pltpu.VMEM((samples, wires), BF16),
            pltpu.SemaphoreType.DMA,
            pltpu.SemaphoreType.DMA((copies,)),
            pltpu.SemaphoreType.DMA,
        ],
        compiler_params=params,
        cost_estimate=pl.CostEstimate(
            flops=2 * CHUNK * flops, bytes_accessed=10 << 20, transcendentals=0
        ),
    )(
        on_hbm(seed_on_tension),
        on_hbm(early),
        on_vmem(tail),
        *map(on_vmem, (back, fresh_a, decay, after, counts, *covered.ka)),
    )

    top = jnp.max(all_lse, axis=0)
    total = jnp.sum(jnp.exp2(all_lse - top[None]), axis=0)
    softened = ((top * LN2 + jnp.log(total)) / SHARPNESS).reshape(wires)
    return (tension, gradient, softened)


def solution(mesh):
    placed = (P("tm", "parts"), P("tm", "parts"), P(None, ("parts", "tm")), P(), P(), P("parts"))
    return jax.shard_map(
        body,
        mesh=mesh,
        in_specs=placed,
        out_specs=(P("tm", "parts"), P("tm", "parts"), P("parts")),
        check_vma=False,
    )
```

```python
import functools
import math

import jax
import jax.numpy as jnp
from jax import lax
from jax.experimental import pallas as pl
from jax.experimental.pallas import tpu as pltpu
from jax.sharding import PartitionSpec as P

CHUNK = 128
LEVELS = 7
SHARPNESS = 4.0
LOG2E = math.log2(math.e)
LN2 = math.log(2.0)
F32 = jnp.float32
BF16 = jnp.bfloat16


def as_column(row):
    m = row.shape[1]
    r = lax.broadcasted_iota(jnp.int32, (m, m), 0)
    c = lax.broadcasted_iota(jnp.int32, (m, m), 1)
    return jnp.sum(jnp.where(r == c, jnp.broadcast_to(row, (m, m)), 0.0), axis=1, keepdims=True)


def rates_and_gains(rates_ref, fit_ref):
    rates = as_column(rates_ref[...])
    gains = as_column(fit_ref[...]) * jnp.sqrt(rates)
    return rates * LOG2E, gains


def level_sums():
    v = lax.broadcasted_iota(jnp.int32, (CHUNK, CHUNK), 0)
    u = lax.broadcasted_iota(jnp.int32, (CHUNK, CHUNK), 1)
    apart = v ^ u
    tables = []
    for level in range(LEVELS):
        half = 1 << level
        near = apart < half
        inside = jnp.where((u & half) != 0, jnp.where(v <= u, -1.0, 0.0), jnp.where(v > u, -1.0, 0.0))
        tables.append(jnp.where(near, inside, 0.0).astype(BF16))
    return jnp.concatenate(tables, axis=1)


def wide(a, times):
    return jnp.concatenate([a] * times, axis=1)


def stacked(heat_ref, speed, first, count):
    return jnp.concatenate(
        [
            heat_ref[:, c * CHUNK : (c + 1) * CHUNK] * speed
            for c in range(first, first + count)
        ],
        axis=0,
    )


def group_of(chunks, most):
    return max(g for g in range(1, most + 1) if chunks % g == 0)


def pieces_of(chunks):
    if chunks % 8:
        return [1] * chunks
    unit = chunks // 8
    return [3 * unit, 2 * unit, 2 * unit, unit]


def prefixes(heat):
    high = heat.astype(BF16)
    rest = heat - high.astype(F32)
    middle = rest.astype(BF16)
    low = (rest - middle.astype(F32)).astype(BF16)
    v = lax.broadcasted_iota(jnp.int32, (CHUNK, CHUNK), 0)
    u = lax.broadcasted_iota(jnp.int32, (CHUNK, CHUNK), 1)
    ones = jnp.concatenate(
        [jnp.where(v <= u, 1.0, 0.0).astype(BF16), jnp.where(v > u, 1.0, 0.0).astype(BF16)],
        axis=1,
    )
    both = jnp.dot(
        jnp.concatenate([high, middle, low], axis=1),
        jnp.concatenate([ones] * 3, axis=0),
        preferred_element_type=F32,
    )
    return both[:, :CHUNK], both[:, CHUNK:], jnp.concatenate([high, middle], axis=1)


def totals_kernel(
    heat_hbm, rates_hbm, fits_hbm, cur_hbm, cot_hbm,
    cur_ref, fresh_f_ref, fresh_a_ref, decay_ref, msg_ref,
    split_ref, start_ref, back_ref, gains_ref, sums_ref,
    cot_ref, heat_ref, rates_ref, fits_ref, small_sem, cur_sem, cot_sem,
):
    modes = heat_ref.shape[0]
    samples, wires = cur_ref.shape
    reps = wires // CHUNK
    chunks = samples // CHUNK
    group = group_of(chunks, 3)

    small = [
        pltpu.make_async_copy(heat_hbm, heat_ref, small_sem.at[0]),
        pltpu.make_async_copy(rates_hbm, rates_ref, small_sem.at[1]),
        pltpu.make_async_copy(fits_hbm, fits_ref, small_sem.at[2]),
    ]
    for copy in small:
        copy.start()
    load_cur = pltpu.make_async_copy(cur_hbm, cur_ref, cur_sem)
    load_cot = pltpu.make_async_copy(cot_hbm, cot_ref, cot_sem)
    load_cur.start()
    load_cot.start()
    sums_ref[...] = level_sums()
    for copy in small:
        copy.wait()

    speed, gains = rates_and_gains(rates_ref, fits_ref)
    gain_stack = jnp.concatenate([gains] * group, axis=0)
    gains_ref[...] = jnp.broadcast_to(
        jnp.concatenate([gains] * (CHUNK // modes), axis=0), gains_ref.shape
    )
    for first in range(0, chunks, group):
        rows = slice(first * modes, (first + group) * modes)
        pre, suf, split = prefixes(stacked(heat_ref, speed, first, group))
        split_ref[rows, :] = split
        start_ref[rows, :] = (gain_stack * jnp.exp2(-pre)).astype(BF16)
        back_ref[rows, :] = jnp.exp2(-suf).astype(BF16)
        decay_ref[rows, :] = jnp.exp2(-(pre + suf))

    tf = jnp.zeros((modes, wires), F32)
    ta = jnp.zeros((modes, wires), F32)
    dc = jnp.ones((modes, CHUNK), F32)
    load_cur.wait()
    for c in range(chunks):
        span = slice(c * CHUNK, (c + 1) * CHUNK)
        rows = slice(c * modes, (c + 1) * modes)
        fresh_f = jnp.dot(back_ref[rows, :], cur_ref[span, :], preferred_element_type=F32)
        fresh_f_ref[rows, :] = fresh_f
        tf = wide(decay_ref[rows, :], reps) * tf + fresh_f
    load_cot.wait()
    for c in range(chunks):
        span = slice(c * CHUNK, (c + 1) * CHUNK)
        rows = slice(c * modes, (c + 1) * modes)
        fresh_a = jnp.dot(start_ref[rows, :], cot_ref[span, :], preferred_element_type=F32)
        fresh_a_ref[rows, :] = fresh_a.astype(BF16)
        ta = ta + wide(dc, reps) * fresh_a
        dc = dc * decay_ref[rows, :]
    for k in range(reps):
        lanes = slice(k * CHUNK, (k + 1) * CHUNK)
        msg_ref[k] = tf[:, lanes]
        msg_ref[reps + k] = ta[:, lanes]
    msg_ref[2 * reps] = dc


def kernels_kernel(modes, first, split_ref, gains_ref, sums_ref, kf_ref, ka_ref):
    group = CHUNK // modes
    t = lax.broadcasted_iota(jnp.int32, (CHUNK, CHUNK), 0)
    s = lax.broadcasted_iota(jnp.int32, (CHUNK, CHUNK), 1)
    apart = jnp.where(t >= s, t ^ s, -1)
    gains = gains_ref[...]
    gain_sum = jnp.sum(gains[:modes], axis=0, keepdims=True)
    base = jnp.where(apart == 0, jnp.broadcast_to(gain_sum, (CHUNK, CHUNK)), 0.0)
    for g in range(kf_ref.shape[0] // (CHUNK * group)):
        rows = slice((first + g) * CHUNK, (first + g + 1) * CHUNK)
        sums = jnp.dot(
            split_ref[rows, :],
            jnp.concatenate([sums_ref[...]] * 2, axis=0),
            preferred_element_type=F32,
        )
        kernels = [base] * group
        for level in range(LEVELS):
            table = jnp.exp2(sums[:, level * CHUNK : (level + 1) * CHUNK])
            left = (gains * table).astype(BF16).T
            right = table.astype(BF16)
            columns = []
            for c in range(group):
                parts = []
                if c > 0:
                    parts.append(jnp.zeros((c * modes, CHUNK), BF16))
                parts.append(right[c * modes : (c + 1) * modes])
                if c + 1 < group:
                    parts.append(jnp.zeros(((group - 1 - c) * modes, CHUNK), BF16))
                columns.append(jnp.concatenate(parts, axis=0))
            both = jnp.dot(left, jnp.concatenate(columns, axis=1), preferred_element_type=F32)
            keep = apart >= (1 << level)
            kernels = [
                jnp.where(keep, both[:, c * CHUNK : (c + 1) * CHUNK], kernels[c])
                for c in range(group)
            ]
        for c in range(group):
            span = slice((g * group + c) * CHUNK, (g * group + c + 1) * CHUNK)
            kernel = kernels[c].astype(BF16)
            kf_ref[span, :] = kernel
            ka_ref[span, :] = kernel.T


def carry(table, state):
    return lax.dot_general(
        table, state, (((0,), (0,)), ((), ())), preferred_element_type=F32
    )


def part_of(refs, c):
    for ref in refs:
        chunks = ref.shape[0] // CHUNK
        if c < chunks:
            return ref[c * CHUNK : (c + 1) * CHUNK, :]
        c -= chunks


def stress_pieces(chunks):
    if chunks % 8:
        return [1] * chunks
    unit = chunks // 8
    return [2 * unit, unit, unit, unit, 3 * unit]


def stress_kernel(
    cur_ref, start_ref, fresh_ref, decay_ref, in_ref, counts_ref, *refs
):
    kf_refs = refs[:-5]
    out_hbm, tail_ref, lse_ref, out_ref, sem = refs[-5:]
    samples, wires = cur_ref.shape
    reps = wires // CHUNK
    modes = in_ref.shape[1]
    scale = counts_ref[...].astype(F32) * 0.25
    scale2 = scale * (SHARPNESS * LOG2E)
    state = jnp.concatenate([in_ref[k] for k in range(reps)], axis=1)
    high = jnp.full((8, wires), -1e30, F32)
    amount = jnp.zeros((8, wires), F32)
    stores = []
    first = 0
    pieces = stress_pieces(samples // CHUNK)
    for k, piece in enumerate(pieces):
        last = k == len(pieces) - 1
        for c in range(first, first + piece):
            span = slice(c * CHUNK, (c + 1) * CHUNK)
            rows = slice(c * modes, (c + 1) * modes)
            acc = jnp.dot(part_of(kf_refs, c), cur_ref[span, :], preferred_element_type=F32)
            acc = acc + carry(start_ref[rows, :], state.astype(BF16))
            stress = (acc * scale).astype(BF16)
            if last:
                tail_ref[(c - first) * CHUNK : (c - first + 1) * CHUNK, :] = stress
            else:
                out_ref[span, :] = stress
            z = (acc * scale2).reshape(CHUNK // 8, 8, wires)
            new = jnp.maximum(high, jnp.max(z, axis=0))
            amount = amount * jnp.exp2(high - new) + jnp.sum(jnp.exp2(z - new[None]), axis=0)
            high = new
            state = wide(decay_ref[rows, :], reps) * state + fresh_ref[rows, :]
        if not last:
            done = pl.ds(first * CHUNK, piece * CHUNK)
            copy = pltpu.make_async_copy(out_ref.at[done], out_hbm.at[done], sem.at[k])
            copy.start()
            stores.append(copy)
        first += piece
    top = jnp.max(high, axis=0, keepdims=True)
    total = jnp.sum(amount * jnp.exp2(high - top), axis=0, keepdims=True)
    value = top + jnp.log(total) * LOG2E
    lse_ref[...] = jnp.broadcast_to(value[None], lse_ref.shape)
    for copy in stores:
        copy.wait()


def adjoint_kernel(
    cot_hbm, early_hbm, tail_ref, back_ref, fresh_ref, decay_ref, in_ref, counts_ref, *refs
):
    ka_refs = refs[:-7]
    out_hbm, stress_hbm, cot_ref, out_ref, load_sem, sem, tail_sem = refs[-7:]
    samples, wires = cot_ref.shape
    reps = wires // CHUNK
    chunks = samples // CHUNK
    modes = in_ref.shape[1]
    scale = counts_ref[...].astype(F32) * 0.25
    state = jnp.concatenate([in_ref[k] for k in range(reps)], axis=1)
    loads = []
    end = chunks
    for k, piece in enumerate(pieces_of(chunks)):
        rows = pl.ds((end - piece) * CHUNK, piece * CHUNK)
        copy = pltpu.make_async_copy(cot_hbm.at[rows], cot_ref.at[rows], load_sem.at[k])
        copy.start()
        loads.append(copy)
        end -= piece
    tail = tail_ref.shape[0]
    copy = pltpu.make_async_copy(tail_ref, stress_hbm.at[pl.ds(samples - tail, tail)], tail_sem)
    copy.start()
    stores = [copy]
    end = chunks
    for k, piece in enumerate(pieces_of(chunks)):
        loads[k].wait()
        for c in reversed(range(end - piece, end)):
            span = slice(c * CHUNK, (c + 1) * CHUNK)
            rows = slice(c * modes, (c + 1) * modes)
            acc = jnp.dot(part_of(ka_refs, c), cot_ref[span, :], preferred_element_type=F32)
            acc = acc + carry(back_ref[rows, :], state.astype(BF16))
            out_ref[span, :] = (acc * scale).astype(BF16)
            state = wide(decay_ref[rows, :], reps) * state + fresh_ref[rows, :].astype(F32)
        done = pl.ds((end - piece) * CHUNK, piece * CHUNK)
        copy = pltpu.make_async_copy(out_ref.at[done], out_hbm.at[done], sem.at[k])
        copy.start()
        stores.append(copy)
        end -= piece
    for copy in stores:
        copy.wait()


def on_vmem(a):
    return pltpu.with_memory_space_constraint(a, pltpu.VMEM)


def on_hbm(a):
    return pltpu.with_memory_space_constraint(a, pltpu.HBM)


def hops_of(n):
    return [1 << k for k in range(n.bit_length() - 1)]


def scan_devices(msg, uppers, reps, run_part, parts):
    n = lax.axis_size("tm")
    half = reps // 2
    hops = hops_of(n)
    late = uppers[0]
    pairs = [(i, i ^ 1) for i in range(n)]

    low_f, high_f = msg[:half], msg[half:reps]
    low_a, high_a = msg[reps : reps + half], msg[reps + half : 2 * reps]
    mine_d = msg[2 * reps :]
    sent = jnp.concatenate(
        [jnp.where(late, low_f, high_f), jnp.where(late, low_a, high_a), mine_d], axis=0
    )
    mine_f, mine_a = jnp.where(late, high_f, low_f), jnp.where(late, high_a, low_a)
    got = lax.ppermute(sent, "tm", pairs)
    got_f, got_a, got_d = got[:half], got[half : 2 * half], got[2 * half :]
    first_f, last_a = jnp.where(late, got_f, mine_f), jnp.where(late, mine_a, got_a)
    first_d, last_d = jnp.where(late, got_d, mine_d), jnp.where(late, mine_d, got_d)
    msg = jnp.concatenate(
        [
            last_d * first_f + jnp.where(late, mine_f, got_f),
            jnp.where(late, got_a, mine_a) + first_d * last_a,
            mine_d * got_d,
        ],
        axis=0,
    )
    before = jnp.zeros_like(mine_f)
    after = jnp.zeros_like(mine_f)
    d_before = jnp.ones_like(mine_d)
    d_after = jnp.ones_like(mine_d)
    msg, first_f, last_a, first_d, last_d = lax.optimization_barrier(
        (msg, first_f, last_a, first_d, last_d)
    )
    for index, hop in list(enumerate(hops))[1:-2]:
        upper = uppers[index]
        mine_f, mine_a, mine_d = msg[:half], msg[half : 2 * half], msg[2 * half :]
        part = index - len(hops) + 2 + parts - 1
        msg = run_part.gate(part, msg)
        got = lax.ppermute(msg, "tm", [(i, i ^ hop) for i in range(n)])
        got = run_part(part, got)
        got_f, got_a, got_d = got[:half], got[half : 2 * half], got[2 * half :]
        next_f = jnp.where(upper, mine_d * got_f + mine_f, got_d * mine_f + got_f)
        next_a = jnp.where(upper, got_d * mine_a + got_a, mine_d * got_a + mine_a)
        msg = jnp.concatenate([next_f, next_a, mine_d * got_d], axis=0)
        before = jnp.where(upper, d_before * got_f + before, before)
        after = jnp.where(upper, after, d_after * got_a + after)
        d_before = jnp.where(upper, d_before * got_d, d_before)
        d_after = jnp.where(upper, d_after, d_after * got_d)
        msg, before, after, d_before, d_after = lax.optimization_barrier(
            (msg, before, after, d_before, d_after)
        )
    near, far = uppers[-2], uppers[-1]
    mine_f, mine_a, mine_d = msg[:half], msg[half : 2 * half], msg[2 * half :]
    to_near = jnp.concatenate([jnp.where(near, mine_a, mine_f), mine_d], axis=0)
    to_far = jnp.concatenate([jnp.where(far, mine_a, mine_f), mine_d], axis=0)
    to_near, to_far = lax.optimization_barrier((to_near, to_far))
    to_near = run_part.gate(parts - 1, to_near)
    quarter = hops[-2]
    got = [
        lax.ppermute(sent, "tm", [(i, i ^ hop) for i in range(n)])
        for sent, hop in ((to_near, quarter), (to_far, 2 * quarter), (to_far, 3 * quarter))
    ]
    got = run_part(parts - 1, tuple(got))
    (x1, d1), (x2, d2), (x3, d3) = [(g[:half], g[half:]) for g in got]
    others_f = jnp.where(
        far,
        jnp.where(near, (x3 * d2 + x2) * d1 + x1, d3 * x2 + x3),
        jnp.where(near, x1, 0.0),
    )
    others_a = jnp.where(
        far,
        jnp.where(near, 0.0, x1),
        jnp.where(near, x3 + d3 * x2, x1 + d1 * (x2 + d2 * x3)),
    )
    before = d_before * others_f + before
    after = d_after * others_a + after
    second_f = first_d * before + first_f
    first_a = last_d * after + last_a
    mine_f, mine_a = jnp.where(late, second_f, before), jnp.where(late, after, first_a)
    sent = jnp.concatenate(
        [jnp.where(late, before, second_f), jnp.where(late, first_a, after)], axis=0
    )
    got = lax.ppermute(sent, "tm", pairs)
    got_f, got_a = got[:half], got[half:]
    before = jnp.concatenate(
        [jnp.where(late, got_f, mine_f), jnp.where(late, mine_f, got_f)], axis=0
    )
    after = jnp.concatenate(
        [jnp.where(late, got_a, mine_a), jnp.where(late, mine_a, got_a)], axis=0
    )
    return before, after


class KernelParts:
    def __init__(self, split, gains, sums, modes, counts, params):
        self.split, self.gains, self.sums = split, gains, sums
        self.modes, self.counts, self.params = modes, counts, params
        self.kf, self.ka = [], []

    def gate(self, part, sent):
        if part >= 0:
            sent, self.gains = lax.optimization_barrier((sent, self.gains))
        return sent

    def __call__(self, part, got):
        if part < 0:
            return got
        length = self.counts[part] * CHUNK * (CHUNK // self.modes)
        whole = pl.BlockSpec(memory_space=pltpu.VMEM)
        kf, ka = pl.pallas_call(
            functools.partial(kernels_kernel, self.modes, sum(self.counts[:part])),
            name="kernels",
            in_specs=[whole] * 3,
            out_specs=[whole] * 2,
            out_shape=[pltpu.VMEM((length, CHUNK), BF16)] * 2,
            compiler_params=self.params,
            cost_estimate=pl.CostEstimate(
                flops=20 * length * CHUNK * CHUNK, bytes_accessed=8 << 20, transcendentals=0
            ),
        )(on_vmem(self.split), on_vmem(self.gains), on_vmem(self.sums))
        got, kf, ka = lax.optimization_barrier((got, kf, ka))
        self.kf.append(kf)
        self.ka.append(ka)
        return got


def body(currents, seed_on_tension, mode_diffusivity_factor, decay_rates, fit_weights, counts):
    samples, wires = currents.shape
    modes = decay_rates.shape[0]
    devices = lax.axis_size("tm")
    chunks = samples // CHUNK
    reps = wires // CHUNK
    me = lax.axis_index("tm")
    uppers = tuple((me & hop) != 0 for hop in hops_of(devices))
    rates, uppers = lax.optimization_barrier((decay_rates.reshape(1, modes), uppers))
    fits = fit_weights.reshape(1, modes)
    counts = counts.reshape(1, wires)
    params = pltpu.CompilerParams(vmem_limit_bytes=16 << 20)
    apart = pl.BlockSpec(memory_space=pl.ANY)
    whole = pl.BlockSpec(memory_space=pltpu.VMEM)
    flops = 2 * samples * wires
    copies = len(pieces_of(chunks))

    cur, fresh_f, fresh_a, decay, msg, split, start, back, gains, sums = pl.pallas_call(
        totals_kernel,
        name="totals",
        in_specs=[apart] * 5,
        out_specs=[whole] * 10,
        out_shape=[
            pltpu.VMEM((samples, wires), BF16),
            pltpu.VMEM((chunks * modes, wires), F32),
            pltpu.VMEM((chunks * modes, wires), BF16),
            pltpu.VMEM((chunks * modes, CHUNK), F32),
            pltpu.VMEM((2 * reps + 1, modes, CHUNK), F32),
            pltpu.VMEM((chunks * modes, 2 * CHUNK), BF16),
            pltpu.VMEM((chunks * modes, CHUNK), BF16),
            pltpu.VMEM((chunks * modes, CHUNK), BF16),
            pltpu.VMEM((CHUNK, CHUNK), F32),
            pltpu.VMEM((CHUNK, LEVELS * CHUNK), BF16),
        ],
        scratch_shapes=[
            pltpu.VMEM((samples, wires), BF16),
            pltpu.VMEM((modes, samples), F32),
            pltpu.VMEM((1, modes), F32),
            pltpu.VMEM((1, modes), F32),
            pltpu.SemaphoreType.DMA((3,)),
            pltpu.SemaphoreType.DMA,
            pltpu.SemaphoreType.DMA,
        ],
        compiler_params=params,
        cost_estimate=pl.CostEstimate(
            flops=2 * modes * flops, bytes_accessed=14 << 20, transcendentals=0
        ),
    )(
        on_hbm(mode_diffusivity_factor),
        on_hbm(rates),
        on_hbm(fits),
        on_hbm(currents),
        on_hbm(seed_on_tension),
    )

    groups = chunks * modes // CHUNK
    parts = 1
    shares = [groups]
    covered = KernelParts(split, gains, sums, modes, shares, params)
    before, after = scan_devices(msg, uppers, reps, covered, parts)

    pieces = stress_pieces(chunks)
    early, tail, lse = pl.pallas_call(
        stress_kernel,
        name="stress",
        in_specs=[whole] * (6 + parts),
        out_specs=[apart, whole, whole],
        out_shape=[
            pltpu.HBM((samples, wires), BF16),
            pltpu.VMEM((pieces[-1] * CHUNK, wires), BF16),
            pltpu.HBM((devices, 1, wires), F32),
        ],
        scratch_shapes=[pltpu.VMEM((samples, wires), BF16), pltpu.SemaphoreType.DMA((len(pieces),))],
        compiler_params=params,
        cost_estimate=pl.CostEstimate(
            flops=2 * CHUNK * flops, bytes_accessed=10 << 20, transcendentals=0
        ),
    )(*map(on_vmem, (cur, start, fresh_f, decay, before, counts, *covered.kf)))

    all_lse = lax.all_to_all(lse, "tm", 0, 0, tiled=True)

    gradient, tension = pl.pallas_call(
        adjoint_kernel,
        name="adjoint",
        in_specs=[apart] * 2 + [whole] * (6 + parts),
        out_specs=[apart] * 2,
        out_shape=[pltpu.HBM((samples, wires), BF16)] * 2,
        input_output_aliases={1: 1},
        scratch_shapes=[
            pltpu.VMEM((samples, wires), BF16),
            pltpu.VMEM((samples, wires), BF16),
            pltpu.SemaphoreType.DMA((copies,)),
            pltpu.SemaphoreType.DMA((copies,)),
            pltpu.SemaphoreType.DMA,
        ],
        compiler_params=params,
        cost_estimate=pl.CostEstimate(
            flops=2 * CHUNK * flops, bytes_accessed=10 << 20, transcendentals=0
        ),
    )(
        on_hbm(seed_on_tension),
        on_hbm(early),
        on_vmem(tail),
        *map(on_vmem, (back, fresh_a, decay, after, counts, *covered.ka)),
    )

    top = jnp.max(all_lse, axis=0)
    total = jnp.sum(jnp.exp2(all_lse - top[None]), axis=0)
    softened = ((top * LN2 + jnp.log(total)) / SHARPNESS).reshape(wires)
    return (tension, gradient, softened)


def solution(mesh):
    placed = (P("tm", "parts"), P("tm", "parts"), P(None, ("parts", "tm")), P(), P(), P("parts"))
    return jax.shard_map(
        body,
        mesh=mesh,
        in_specs=placed,
        out_specs=(P("tm", "parts"), P("tm", "parts"), P("parts")),
        check_vma=False,
    )
```
